32 devices in a mesh: band: 8 (over z, x), lon: 4 (over y, core).
Axes of the slice: x: 2, y: 2, z: 4, core: 2. Of those that a mesh axis runs over, the one named last changes fastest.
Arguments:
- loads: float32 [2, 2, 32, 4096], P(None, None, 'band', 'lon'), may hold values from -6 to 6
- legendre: bfloat16 [1024, 1024, 32], P('band', 'lon'), may hold values from -1 to 1
- love: float32 [2, 2, 1024], P(None, None, 'lon'), may hold values from -4 to 4
- cycle_weight: float32 [32], replicated, may hold values from 0.25 to 1
- order_list: int32 [1024], replicated, may hold values from 0 to 1023, as said below
- cycle_order: int32 [32], replicated, may hold values from 0 to 31, each once
Outputs:
- sea_response: float32 [2, 2, 32, 4096], P(None, None, 'band', 'lon')
The draws below stay inside these ranges and needn't reach their ends.
Inputs may be any that keep to these rules, and one draw needn't show every extreme that they name: `order_list`: entries b * 128 to b * 128 + 127 are the orders held by band index b; every order appears once, and the orders of every band index have the same sum. Row j of the grid holds cycle pair cycle_order[j].
All inputs are finite; a program needn't handle non-finite values.
Results may differ from the reference program's by a relative error of at most 0.0041.
Values may be sent and summed in bfloat16 or wider, within the bound.
No kernel may reach another device: no remote copies, remote signals or barrier semaphores. Data moves between devices by JAX's collectives and lax.ppermute only.
A program may use at most 64 MiB of HBM per device.

```python
import math
import jax
import jax.numpy as jnp
from jax import lax

M = 1024
NLON = 4096
NH = 32
OPD = 128


def draw_order_list(key, part):
    owners = M // OPD
    halves = OPD // 2
    subkeys = jax.random.split(jax.random.fold_in(key, 11), halves)
    shuffles = jax.vmap(lambda subkey: jax.random.permutation(subkey, owners))(subkeys).astype(jnp.int32)
    offsets = jnp.arange(halves, dtype=jnp.int32)[:, None] * (2 * owners)
    first_half = offsets + shuffles
    second_half = offsets + owners + (owners - 1 - shuffles)
    slot_table = jnp.stack([first_half, second_half], axis=2)
    slot_table = jnp.transpose(slot_table, (1, 0, 2)).reshape(owners, OPD)
    owner_keys = jax.random.split(jax.random.fold_in(key, 23), owners)
    slot_table = jax.vmap(lambda subkey, order_row: jax.random.permutation(subkey, order_row))(owner_keys, slot_table)
    return slot_table.reshape(M).astype(jnp.int32)


def shard_levels(stream_key, extent, pieces, smallest, top_value):
    factor_of, own = 1.0, jax.random.fold_in(stream_key, 6)
    for axis_at, shards_of in pieces:
        heights = jnp.exp(jax.random.uniform(jax.random.fold_in(own, axis_at), (shards_of,), jnp.float32, smallest / len(pieces), top_value / len(pieces)))
        factor_of = factor_of * jnp.repeat(heights, extent[axis_at] // shards_of).reshape([-1 if axis == axis_at else 1 for axis in range(len(extent))])
    return factor_of


def gaussian(key, dims, spread, limit, pieces=(), kind=jnp.bfloat16):
    level = shard_levels(key, dims, pieces, -0.22, 0.18) if pieces else 1.0
    array = jax.random.normal(key, dims, jnp.float32) * spread * level
    return jnp.minimum(jnp.maximum(array, -limit), limit).astype(kind)


def setup_inputs(seed: int = 0) -> dict:
    key_list = jax.random.split(jax.random.key(seed), 7)
    loads = gaussian(key_list[0], (2, 2, NH, NLON), 1.0, 6.0, ((2, 8), (3, 4)), jnp.float32)
    legendre = gaussian(key_list[1], (M, M, NH), NH ** -0.5, 1.0, ((0, 8), (1, 4)))
    love = gaussian(key_list[2], (2, 2, M), 1.0, 4.0, ((2, 4),), jnp.float32)
    cycle_weight = jnp.clip(jnp.exp(jax.random.uniform(key_list[3], (NH,), jnp.float32, math.log(0.25), math.log(1.0))), 0.25, 1.0)
    order_list = draw_order_list(jax.random.fold_in(key_list[6], 71), 0)
    cycle_order = jax.random.permutation(key_list[5], NH).astype(jnp.int32)
    return {"loads": loads, "legendre": legendre, "love": love, "cycle_weight": cycle_weight, "order_list": order_list, "cycle_order": cycle_order}


def cycle_basis(order_ids, positions, total):
    phase = positions[:, None] * order_ids[None, :] % total
    angle = phase.astype(jnp.float32) * (2.0 * math.pi / total)
    scale = 1.0 / math.sqrt(total)
    return (jnp.cos(angle) * scale, jnp.sin(angle) * scale)

def reference(loads, legendre, love, cycle_weight, order_list, cycle_order):
    highest = lax.Precision.HIGHEST
    total = loads.shape[3]
    orders = order_list.shape[0]
    positions = jnp.arange(total, dtype=jnp.int32)
    cosine, sine = cycle_basis(order_list, positions, total)
    forward = jnp.stack([cosine, -sine], axis=1)
    spectrum = jnp.einsum('fhjx,xrm->fhjrm', loads, forward, precision=highest)
    weights = jnp.take(cycle_weight, cycle_order)[None, :, None, None]
    northern = spectrum[:, 0]
    southern = spectrum[:, 1]
    symmetric = ((northern + southern) * weights).astype(jnp.bfloat16)
    antisym = ((northern - southern) * weights).astype(jnp.bfloat16)
    folded = jnp.stack([symmetric, antisym], axis=1)
    degrees = jnp.arange(orders, dtype=jnp.int32)

    def per_order(slot):
        order = order_list[slot]
        table_rows = jnp.take(legendre[slot], cycle_order, axis=1).astype(jnp.float32)
        column = jnp.transpose(folded[..., slot], (2, 0, 1, 3)).reshape(-1, 8).astype(jnp.float32)
        analysed = jnp.dot(table_rows, column, precision=highest, preferred_element_type=jnp.float32).reshape(orders, 2, 2, 2)
        even = (degrees - order) % 2 == 0
        valid = degrees >= order
        selected = jnp.where(even[:, None, None], analysed[:, :, 0], analysed[:, :, 1])
        selected = selected * valid[:, None, None].astype(jnp.float32)
        response = jnp.einsum('gfl,lfr->lgr', love, selected, precision=highest).astype(jnp.bfloat16)
        even_part = jnp.where((even & valid)[:, None, None], response, jnp.zeros_like(response))
        odd_part = jnp.where((~even & valid)[:, None, None], response, jnp.zeros_like(response))
        stacked = jnp.stack([even_part, odd_part], axis=2).reshape(orders, 8).astype(jnp.float32)
        synthesis = jnp.dot(table_rows.T, stacked, precision=highest, preferred_element_type=jnp.float32).reshape(-1, 2, 2, 2)
        return jnp.stack([synthesis[:, :, 0] + synthesis[:, :, 1], synthesis[:, :, 0] - synthesis[:, :, 1]], axis=2)
    cycle_values = lax.map(per_order, jnp.arange(orders, dtype=jnp.int32))
    factor = jnp.where(order_list == 0, 1.0, 2.0).astype(jnp.float32)
    inverse = jnp.stack([cosine.T, -sine.T], axis=0)
    scaled = cycle_values * factor[:, None, None, None, None]
    return jnp.einsum('sjghr,rsx->ghjx', scaled, inverse, precision=highest)
```

```python
import functools
import math

import jax
import jax.numpy as jnp
from jax import lax
from jax.experimental import pallas as pl
from jax.experimental.pallas import tpu as pltpu
from jax.sharding import PartitionSpec as P

LANES = 128
ROWS = 8
NT = (((1,), (1,)), ((), ()))


def iota(shape, axis):
    return lax.broadcasted_iota(jnp.int32, shape, axis)


def turn(phase, total):
    shift = (total // 4).bit_length() - 1
    quadrant = (phase + total // 8) >> shift
    x = (phase - (quadrant << shift)).astype(jnp.float32) * (2.0 * math.pi / total)
    z = x * x
    s = ((-1.9515295891e-4 * z + 8.3321608736e-3) * z - 1.6666654611e-1) * z * x + x
    c = ((2.443315711809948e-5 * z - 1.388731625493765e-3) * z + 4.166664568298827e-2) * z * z
    c = c - 0.5 * z + 1.0
    odd = (quadrant & 1) == 1
    cosine = jnp.where(odd, s, c)
    sine = jnp.where(odd, c, s)
    cosine = jnp.where(((quadrant + 1) & 2) == 2, -cosine, cosine)
    sine = jnp.where((quadrant & 2) == 2, -sine, sine)
    return cosine, sine


def split(x):
    high = x.astype(jnp.bfloat16)
    return high, (x - high.astype(jnp.float32)).astype(jnp.bfloat16)


def dot(a, b):
    return jnp.dot(a, b, preferred_element_type=jnp.float32)


def dot_nt(a, b):
    return lax.dot_general(a, b, NT, preferred_element_type=jnp.float32)


def analyse_grid(lon_count, owners, total, orders_ref, weight_ref, cycle_ref, loads_ref, out_ref, points_ref, mid_ref):
    cycles = loads_ref.shape[3]
    blocks = loads_ref.shape[4] // LANES
    per_owner = orders_ref.shape[1]
    quarter = per_owner // lon_count
    pieces = LANES // quarter
    tiles = owners // pieces
    band, lon = lax.axis_index("band"), lax.axis_index("lon")

    mine = pltpu.roll(orders_ref[...], (LANES - quarter * lon) % LANES, 1)
    slot = iota((1, LANES), 1) // quarter
    shifted = [mine if i == 0 else pltpu.roll(mine, quarter * i, 1) for i in range(pieces)]
    rows = []
    for t in range(tiles):
        row = shifted[0][t * pieces : t * pieces + 1]
        for i in range(1, pieces):
            row = jnp.where(slot == i, shifted[i][t * pieces + i : t * pieces + i + 1], row)
        rows.append(row)
    orders = jnp.concatenate(rows, axis=1)
    width = orders.shape[1]

    for q in range(lon_count):
        for a in range(blocks):
            for f in range(2):
                north = loads_ref[q, f, 0, :, a * LANES : (a + 1) * LANES]
                south = loads_ref[q, f, 1, :, a * LANES : (a + 1) * LANES]
                at = ((q * blocks + a) * 2 + f) * 2 * cycles
                points_ref[at : at + 2 * cycles] = jnp.concatenate([north + south, north - south], axis=0)
    high, low = split(points_ref[...])
    cos_b, sin_b = turn((iota((LANES, width), 0) * orders) & (total - 1), total)
    cos_high, cos_low = split(cos_b)
    sin_high, sin_low = split(sin_b)
    basis_high = jnp.concatenate([cos_high, sin_high], axis=1)
    basis_low = jnp.concatenate([cos_low, sin_low], axis=1)
    mid_ref[...] = dot(
        jnp.concatenate([high, low, high], axis=1),
        jnp.concatenate([basis_high, basis_high, basis_low], axis=0),
    )
    count = lon_count * blocks
    cos_a, sin_a = turn((iota((count, width), 0) * LANES * orders) & (total - 1), total)

    step = 2 * cycles
    sums = [[jnp.zeros((step, width), jnp.float32) for _ in range(2)] for _ in range(2)]
    for a in range(count):
        ca, sa = cos_a[a : a + 1], sin_a[a : a + 1]
        for f in range(2):
            at = (a * 2 + f) * step
            tc = mid_ref[at : at + step, :width]
            ts = mid_ref[at : at + step, width:]
            sums[f][0] = sums[f][0] + (ca * tc - sa * ts)
            sums[f][1] = sums[f][1] - (sa * tc + ca * ts)

    sub = iota((step, 1), 0) % cycles
    weight = jnp.zeros((step, 1), jnp.float32)
    for j in range(cycles):
        weight = jnp.where(sub == j, weight_ref[cycle_ref[band * cycles + j]], weight)
    scale = 1.0 / math.sqrt(total)
    sums = [[(sums[f][c] * scale) * weight for c in range(2)] for f in range(2)]
    for owner in range(owners):
        t, i = owner // pieces, owner % pieces
        block = None
        for e in range(4):
            piece = sums[e // 2][e % 2][:, t * LANES : (t + 1) * LANES]
            move = (e - i) * quarter % LANES
            piece = pltpu.roll(piece, move, 1) if move else piece
            block = piece if block is None else jnp.where(slot == e, piece, block)
        block = block.astype(out_ref.dtype)
        for q in range(lon_count):
            out_ref[owner * lon_count + q] = block


def spectral(lon_count, owners, orders_ref, cycle_ref, folded_ref, legendre_ref, love_ref, out_ref, spread_ref, kept_ref):
    per_owner = orders_ref.shape[1]
    quarter = per_owner // lon_count
    degrees = legendre_ref.shape[1]
    cycles = folded_ref.shape[1] // 2
    northern = owners * cycles
    group = degrees // northern
    wide = group * northern
    band, lon = lax.axis_index("band"), lax.axis_index("lon")
    lane = iota((1, LANES), 1)

    def cycle_lanes(repeat):
        place = (lane // (repeat * cycles)) * cycles + lane % cycles
        row = jnp.full((1, LANES), -1, jnp.int32)
        for i in range(northern):
            row = jnp.where(place == i, cycle_ref[i], row)
        return row

    parity_lane = (lane // cycles) % 2
    arrived = cycle_lanes(2)
    found = iota((northern, LANES), 0) == arrived
    pick = []
    for p in range(2):
        one = jnp.where(found & (parity_lane == p), 1.0, 0.0)
        pick += [one] * group
    pick = jnp.concatenate(pick, axis=0).astype(jnp.bfloat16)

    pad = jnp.zeros((LANES - 2 * northern, LANES), jnp.float32)
    for q in range(lon_count):
        pieces = [folded_ref[b * lon_count + q].astype(jnp.float32) for b in range(owners)]
        turned = jnp.transpose(jnp.concatenate(pieces + [pad], axis=0)).astype(jnp.bfloat16)
        spread_ref[q] = dot_nt(turned, pick)

    own = orders_ref[pl.ds(band, 1), :].astype(jnp.float32)
    order_rows = jnp.transpose(jnp.broadcast_to(own, (LANES, per_owner))).astype(jnp.int32)
    degree = lon * degrees + iota((ROWS, degrees), 1)
    diagonal = iota((ROWS, wide), 0) == iota((ROWS, wide), 1) // northern
    love = [[love_ref[g, f : f + 1, :] for f in range(2)] for g in range(2)]

    for q in range(lon_count):
        for pair in range(quarter // (2 * group)):
            halves = []
            for half in range(2):
                first = (pair * 2 + half) * group
                left = []
                for f in range(2):
                    for p in range(2):
                        for c in range(2):
                            at = (f * 2 + c) * quarter + first
                            left.append(
                                jnp.where(diagonal, spread_ref[q, at : at + group, p * wide : (p + 1) * wide], 0.0)
                            )
                left = jnp.concatenate(left, axis=0).astype(jnp.bfloat16)
                start = (q * quarter + first) * northern
                table = legendre_ref[start : start + wide]
                analysed = dot(left, table)
                order = order_rows[q * quarter + first : q * quarter + first + group]
                gap = degree - jnp.concatenate([order] * (degrees // LANES), axis=1)
                valid = gap >= 0
                keep = [valid & ((gap & 1) == p) for p in range(2)]
                mixed = []
                for g in range(2):
                    for p in range(2):
                        for c in range(2):
                            lo = (p * 2 + c) * group
                            hi = ((2 + p) * 2 + c) * group
                            value = love[g][0] * analysed[lo : lo + group] + love[g][1] * analysed[hi : hi + group]
                            mixed.append(jnp.where(keep[p], value, 0.0))
                mixed = jnp.concatenate(mixed, axis=0).astype(jnp.bfloat16)
                halves.append(dot_nt(mixed, table))
            at = q * quarter + pair * 2 * group
            for g in range(2):
                for c in range(2):
                    rows = []
                    for half in range(2):
                        even = halves[half][(g * 4 + c) * group : (g * 4 + c + 1) * group]
                        odd = halves[half][(g * 4 + 2 + c) * group : (g * 4 + 3 + c) * group]
                        rows.append((even, odd))
                    for h in range(2):
                        both = [even + odd if h == 0 else even - odd for even, odd in rows]
                        both = [jnp.where(diagonal, value, 0.0) for value in both]
                        kept_ref[g * 2 + h, c * per_owner + at : c * per_owner + at + 2 * group, :] = jnp.concatenate(
                            both, axis=0
                        ).astype(jnp.bfloat16)

    leaving = cycle_lanes(4).astype(jnp.float32)
    cycle_rows = jnp.transpose(jnp.broadcast_to(leaving, (LANES, LANES))).astype(jnp.int32)
    cycle_rows = jnp.concatenate([cycle_rows] * (wide // LANES), axis=1)
    found = cycle_rows == iota((LANES, wide), 1) % northern
    part = (iota((LANES, wide), 0) // cycles) % 4
    total = None
    for i in range(4):
        pick = jnp.where(found & (part == i), 1.0, 0.0).astype(jnp.bfloat16)
        term = dot_nt(pick, kept_ref[i])
        total = term if total is None else total + term
    total = total.astype(out_ref.dtype)
    for b in range(owners):
        for q in range(lon_count):
            out_ref[b * lon_count + q] = total[b * 4 * cycles : (b + 1) * 4 * cycles]


def synthesise_grid(lon_count, owners, total, orders_ref, values_ref, out_ref, left_ref, right_ref):
    per_owner = orders_ref.shape[1]
    rows = values_ref.shape[1]
    cycles = out_ref.shape[2]
    blocks = out_ref.shape[3] // LANES
    lon = lax.axis_index("lon")
    scale = 1.0 / math.sqrt(total)
    count = owners * per_owner
    for b in range(owners):
        order = orders_ref[b : b + 1, :]
        value = values_ref[b * lon_count].astype(jnp.float32)
        for q in range(1, lon_count):
            value = value + values_ref[b * lon_count + q].astype(jnp.float32)
        factor = jnp.where(order == 0, scale, 2.0 * scale)
        re = value[:, :per_owner] * factor
        im = value[:, per_owner:] * factor
        step = iota((blocks, per_owner), 0) + lon * blocks
        cos_a, sin_a = turn((step * LANES * order) & (total - 1), total)
        cos_b, sin_b = turn((iota((LANES, per_owner), 0) * order) & (total - 1), total)
        at = b * per_owner
        for c, table in ((0, cos_b), (1, sin_b)):
            high, low = split(table)
            right_ref[0, :, c * count + at : c * count + at + per_owner] = high
            right_ref[1, :, c * count + at : c * count + at + per_owner] = low
        for a in range(blocks):
            ca, sa = cos_a[a : a + 1], sin_a[a : a + 1]
            for c, term in ((0, ca * re - sa * im), (1, -(sa * re + ca * im))):
                high, low = split(term)
                left_ref[0, a * rows : (a + 1) * rows, c * count + at : c * count + at + per_owner] = high
                left_ref[1, a * rows : (a + 1) * rows, c * count + at : c * count + at + per_owner] = low
    grid = dot_nt(left_ref[0], right_ref[0])
    grid = grid + dot_nt(left_ref[1], right_ref[0])
    grid = grid + dot_nt(left_ref[0], right_ref[1])
    for a in range(blocks):
        for g in range(2):
            for h in range(2):
                at = a * rows + (g * 2 + h) * cycles
                out_ref[g, h, :, a * LANES : (a + 1) * LANES] = grid[at : at + cycles]


def fits(owners, lon_count, cycles, points, per_owner, degrees):
    northern = owners * cycles
    total = points * lon_count
    return (
        per_owner == LANES
        and 4 * per_owner == lon_count * LANES
        and 2 * cycles == ROWS
        and 4 * northern == LANES
        and ROWS * northern == degrees
        and degrees % LANES == 0
        and owners == ROWS
        and points % LANES == 0
        and total & (total - 1) == 0
        and owners * per_owner * LANES < 1 << 24
    )


def per_device_kernels(loads, legendre, love, cycle_weight, order_list, cycle_order):
    owners = lax.axis_size("band")
    lon_count = lax.axis_size("lon")
    cycles, points = loads.shape[2], loads.shape[3]
    per_owner, degrees, northern = legendre.shape
    total = points * lon_count
    devices = owners * lon_count
    blocks = points // LANES
    everyone = ("band", "lon")
    vmem = pl.BlockSpec(memory_space=pltpu.VMEM)
    smem = pl.BlockSpec(memory_space=pltpu.SMEM)
    table = order_list.reshape(owners, per_owner)

    whole = lax.all_gather(loads, "lon", axis=0)
    count = lon_count * blocks * 4 * cycles
    width = 2 * owners * per_owner // lon_count
    folded = pl.pallas_call(
        functools.partial(analyse_grid, lon_count, owners, total),
        out_shape=jax.ShapeDtypeStruct((devices, 2 * cycles, LANES), jnp.bfloat16),
        in_specs=[vmem, smem, smem, vmem],
        out_specs=vmem,
        scratch_shapes=[pltpu.VMEM((count, LANES), jnp.float32), pltpu.VMEM((count, width), jnp.float32)],
        name="analyse_grid",
    )(table, cycle_weight, cycle_order, whole)
    arrived = lax.all_to_all(folded, everyone, split_axis=0, concat_axis=0, tiled=True)

    rows = jnp.transpose(legendre, (0, 2, 1)).reshape(per_owner * northern, degrees)
    values = pl.pallas_call(
        functools.partial(spectral, lon_count, owners),
        out_shape=jax.ShapeDtypeStruct((devices, 4 * cycles, 2 * per_owner), jnp.bfloat16),
        in_specs=[vmem, smem, vmem, vmem, vmem],
        out_specs=vmem,
        scratch_shapes=[
            pltpu.VMEM((lon_count, LANES, 2 * degrees), jnp.float32),
            pltpu.VMEM((4, 2 * per_owner, degrees), jnp.bfloat16),
        ],
        name="spectral",
    )(table, cycle_order, arrived, rows, love)
    returned = lax.all_to_all(values, everyone, split_axis=0, concat_axis=0, tiled=True)

    return pl.pallas_call(
        functools.partial(synthesise_grid, lon_count, owners, total),
        out_shape=jax.ShapeDtypeStruct(loads.shape, jnp.float32),
        in_specs=[vmem, vmem],
        out_specs=vmem,
        scratch_shapes=[
            pltpu.VMEM((2, 4 * cycles * blocks, 2 * owners * per_owner), jnp.bfloat16),
            pltpu.VMEM((2, LANES, 2 * owners * per_owner), jnp.bfloat16),
        ],
        name="synthesise_grid",
    )(table, returned)


def per_device(loads, legendre, love, cycle_weight, order_list, cycle_order):
    sizes = (lax.axis_size("band"), lax.axis_size("lon"), loads.shape[2], loads.shape[3], legendre.shape[0], legendre.shape[1])
    form = per_device_kernels if fits(*sizes) else per_device_plain
    return form(loads, legendre, love, cycle_weight, order_list, cycle_order)


def cycle_basis(order_ids, positions, total):
    phase = positions[:, None] * order_ids[None, :] % total
    angle = phase.astype(jnp.float32) * (2.0 * math.pi / total)
    scale = 1.0 / math.sqrt(total)
    return (jnp.cos(angle) * scale, jnp.sin(angle) * scale)


def per_device_plain(loads, legendre, love, cycle_weight, order_list, cycle_order):
    highest = lax.Precision.HIGHEST
    owners = lax.axis_size("band")
    lon_count = lax.axis_size("lon")
    band_index = lax.axis_index("band")
    lon_index = lax.axis_index("lon")
    cycle_pairs = loads.shape[2]
    points = loads.shape[3]
    total = points * lon_count
    orders = order_list.shape[0]
    per_owner = legendre.shape[0]
    degree_count = legendre.shape[1]
    northern = legendre.shape[2]
    quarter = per_owner // lon_count
    positions = lon_index * points + jnp.arange(points, dtype=jnp.int32)
    cosine, sine = cycle_basis(order_list, positions, total)
    my_cycles = lax.dynamic_slice_in_dim(cycle_order, band_index * cycle_pairs, cycle_pairs)
    picker = my_cycles[:, None] == jnp.arange(northern, dtype=jnp.int32)[None, :]
    weights = jnp.sum(jnp.where(picker, cycle_weight[None, :], 0.0), axis=1)
    forward = jnp.stack([cosine, -sine], axis=1)
    spectrum = jnp.einsum("fhjx,xrm->fhjrm", loads, forward, precision=highest)
    spectrum = spectrum.reshape(2, 2, cycle_pairs, 2, owners, per_owner)
    summed = lax.psum_scatter(spectrum, "lon", scatter_dimension=5, tiled=True)
    cycle_scale = weights[None, :, None, None, None]
    symmetric = ((summed[:, 0] + summed[:, 1]) * cycle_scale).astype(jnp.bfloat16)
    antisym = ((summed[:, 0] - summed[:, 1]) * cycle_scale).astype(jnp.bfloat16)
    folded = jnp.stack([symmetric, antisym], axis=1)
    slot_width = folded.shape[5]
    outgoing = jnp.transpose(folded, (4, 5, 0, 1, 3, 2)).reshape(owners, slot_width, 8, cycle_pairs)
    arrived = lax.all_to_all(outgoing, "band", split_axis=0, concat_axis=3, tiled=True).reshape(
        slot_width, 8, northern
    )
    columns = lax.all_gather(arrived, "lon", axis=0, tiled=True)
    inverse_rows = jnp.argsort(cycle_order)
    columns_sorted = jnp.take(columns, inverse_rows, axis=2)
    my_orders = lax.dynamic_slice_in_dim(order_list, band_index * per_owner, per_owner)
    degrees = lon_index * degree_count + jnp.arange(degree_count, dtype=jnp.int32)
    analysed = jnp.einsum(
        "olk,ock->ocl", legendre, columns_sorted, preferred_element_type=jnp.float32
    )
    analysed = analysed.reshape(per_owner, 2, 2, 2, degree_count)
    even = (degrees[None, :] - my_orders[:, None]) % 2 == 0
    valid = degrees[None, :] >= my_orders[:, None]
    selected = jnp.where(even[:, None, None, :], analysed[:, :, 0], analysed[:, :, 1])
    selected = selected * valid[:, None, None, :].astype(jnp.float32)
    response = jnp.einsum("gfl,ofrl->ogrl", love, selected, precision=highest).astype(jnp.bfloat16)
    even_part = jnp.where((even & valid)[:, None, None, :], response, jnp.zeros_like(response))
    odd_part = jnp.where((~even & valid)[:, None, None, :], response, jnp.zeros_like(response))
    stacked = jnp.stack([even_part, odd_part], axis=2).reshape(per_owner, 8, degree_count)
    partial_sorted = jnp.einsum(
        "olk,ocl->ock", legendre, stacked, preferred_element_type=jnp.float32
    )
    partial_value = jnp.take(partial_sorted, cycle_order, axis=2)
    reduced = lax.psum_scatter(partial_value, "lon", scatter_dimension=0, tiled=True)
    returned = lax.all_to_all(reduced, "band", split_axis=2, concat_axis=0, tiled=True)
    gathered = lax.all_gather(returned[None], "lon", axis=0, tiled=True).reshape(
        orders, 8, cycle_pairs
    )
    slot_ids = jnp.transpose(order_list.reshape(owners, lon_count, quarter), (1, 0, 2)).reshape(
        orders
    )
    cosine_back, sine_back = cycle_basis(slot_ids, positions, total)
    pieces = gathered.reshape(orders, 2, 2, 2, cycle_pairs)
    cycle_values = jnp.stack(
        [pieces[:, :, 0] + pieces[:, :, 1], pieces[:, :, 0] - pieces[:, :, 1]], axis=2
    )
    factor = jnp.where(slot_ids == 0, 1.0, 2.0).astype(jnp.float32)
    inverse = jnp.stack([cosine_back.T, -sine_back.T], axis=0)
    scaled = cycle_values * factor[:, None, None, None, None]
    return jnp.einsum("sghrp,rsx->ghpx", scaled, inverse, precision=highest)


def solution(mesh):
    return jax.shard_map(
        per_device,
        mesh=mesh,
        in_specs=(
            P(None, None, "band", "lon"),
            P("band", "lon", None),
            P(None, None, "lon"),
            P(),
            P(),
            P(),
        ),
        out_specs=P(None, None, "band", "lon"),
        check_vma=False,
    )
```

```python
import functools
import math

import jax
import jax.numpy as jnp
from jax import lax
from jax.experimental import pallas as pl
from jax.experimental.pallas import tpu as pltpu
from jax.sharding import PartitionSpec as P

LANES = 128
ROWS = 8
VMEM_LIMIT = 12 << 20
NT = (((1,), (1,)), ((), ()))


def iota(shape, axis):
    return lax.broadcasted_iota(jnp.int32, shape, axis)


def turn(phase, total):
    shift = (total // 4).bit_length() - 1
    quadrant = (phase + total // 8) >> shift
    x = (phase - (quadrant << shift)).astype(jnp.float32) * (2.0 * math.pi / total)
    z = x * x
    s = ((-1.9515295891e-4 * z + 8.3321608736e-3) * z - 1.6666654611e-1) * z * x + x
    c = ((2.443315711809948e-5 * z - 1.388731625493765e-3) * z + 4.166664568298827e-2) * z * z
    c = c - 0.5 * z + 1.0
    odd = (quadrant & 1) == 1
    cosine = jnp.where(odd, s, c)
    sine = jnp.where(odd, c, s)
    cosine = jnp.where(((quadrant + 1) & 2) == 2, -cosine, cosine)
    sine = jnp.where((quadrant & 2) == 2, -sine, sine)
    return cosine, sine


def split(x):
    high = x.astype(jnp.bfloat16)
    return high, (x - high.astype(jnp.float32)).astype(jnp.bfloat16)


def dot(a, b):
    return jnp.dot(a, b, preferred_element_type=jnp.float32)


def dot_nt(a, b):
    return lax.dot_general(a, b, NT, preferred_element_type=jnp.float32)


def analyse_grid(right_ref, turn_ref, weight_ref, *refs):
    parts, out_ref, points_ref, mid_ref = refs[:-3], refs[-3], refs[-2], refs[-1]
    lon_count = len(parts)
    cycles = parts[0].shape[2]
    blocks = parts[0].shape[3] // LANES
    owners = out_ref.shape[0] // lon_count
    count, width = turn_ref.shape[1:]
    quarter = width // owners
    pieces = LANES // quarter
    step = 2 * cycles

    for q, part in enumerate(parts):
        for a in range(blocks):
            for f in range(2):
                north = part[f, 0, :, a * LANES : (a + 1) * LANES]
                south = part[f, 1, :, a * LANES : (a + 1) * LANES]
                at = ((q * blocks + a) * 2 + f) * step
                points_ref[at : at + step] = jnp.concatenate([north + south, north - south], axis=0)
    high, low = split(points_ref[...])
    mid_ref[...] = dot(jnp.concatenate([high, low, high], axis=1), right_ref[...])

    sums = [[jnp.zeros((step, width), jnp.float32) for _ in range(2)] for _ in range(2)]
    for a in range(count):
        ca, sa = turn_ref[0, a : a + 1], turn_ref[1, a : a + 1]
        for f in range(2):
            at = (a * 2 + f) * step
            tc = mid_ref[at : at + step, :width]
            ts = mid_ref[at : at + step, width:]
            sums[f][0] = sums[f][0] + (ca * tc - sa * ts)
            sums[f][1] = sums[f][1] - (sa * tc + ca * ts)

    slot = iota((1, LANES), 1) // quarter
    weight = weight_ref[...]
    for owner in range(owners):
        t, i = owner // pieces, owner % pieces
        block = None
        for e in range(4):
            piece = sums[e // 2][e % 2][:, t * LANES : (t + 1) * LANES]
            move = (e - i) * quarter % LANES
            piece = pltpu.roll(piece, move, 1) if move else piece
            block = piece if block is None else jnp.where(slot == e, piece, block)
        block = (block * weight).astype(out_ref.dtype)
        for q in range(lon_count):
            out_ref[owner * lon_count + q] = block


def tables(lon_count, cycles, degrees, blocks, total, orders_ref, weight_ref, cycle_ref, *out_refs):
    right_ref, first_ref, column_ref, pick_ref, put_ref, rows_ref, turn_ref, basis_ref = out_refs
    owners, per_owner = orders_ref.shape
    quarter = per_owner // lon_count
    pieces = LANES // quarter
    northern = owners * cycles
    group = degrees // northern
    wide = group * northern
    band, lon = lax.axis_index("band"), lax.axis_index("lon")
    lane = iota((1, LANES), 1)

    mine = pltpu.roll(orders_ref[...], (LANES - quarter * lon) % LANES, 1)
    slot = lane // quarter
    shifted = [mine if i == 0 else pltpu.roll(mine, quarter * i, 1) for i in range(pieces)]
    rows = []
    for t in range(owners // pieces):
        row = shifted[0][t * pieces : t * pieces + 1]
        for i in range(1, pieces):
            row = jnp.where(slot == i, shifted[i][t * pieces + i : t * pieces + i + 1], row)
        rows.append(row)
    orders = jnp.concatenate(rows, axis=1)
    width = orders.shape[1]
    for c, table in enumerate(turn((iota((LANES, width), 0) * orders) & (total - 1), total)):
        high, low = split(table)
        for k, value in enumerate((high, high, low)):
            right_ref[k * LANES : (k + 1) * LANES, c * width : (c + 1) * width] = value
    for k in range(lon_count):
        origin = (lon + lon_count - k) % lon_count
        step = iota((blocks, width), 0) + origin * blocks
        for c, table in enumerate(turn((step * LANES * orders) & (total - 1), total)):
            first_ref[c, k * blocks : (k + 1) * blocks] = table
    sub = iota((2 * cycles, LANES), 0) % cycles
    weight = jnp.zeros((2 * cycles, LANES), jnp.float32)
    for j in range(cycles):
        weight = jnp.where(sub == j, weight_ref[cycle_ref[band * cycles + j]], weight)
    column_ref[...] = weight * (1.0 / math.sqrt(total))

    def cycle_lanes(repeat):
        place = (lane // (repeat * cycles)) * cycles + lane % cycles
        row = jnp.full((1, LANES), -1, jnp.int32)
        for i in range(northern):
            row = jnp.where(place == i, cycle_ref[i], row)
        return row

    parity_lane = (lane // cycles) % 2
    found = iota((northern, LANES), 0) == cycle_lanes(2)
    for p in range(2):
        one = jnp.where(found & (parity_lane == p), 1.0, 0.0)
        pick_ref[p * wide : (p + 1) * wide] = jnp.concatenate([one] * group, axis=0).astype(jnp.bfloat16)

    leaving = cycle_lanes(4).astype(jnp.float32)
    cycle_rows = jnp.transpose(jnp.broadcast_to(leaving, (LANES, LANES))).astype(jnp.int32)
    found = cycle_rows == iota((LANES, LANES), 1) % northern
    part = (iota((LANES, LANES), 0) // cycles) % 4
    for i in range(4):
        put = jnp.where(found & (part == i), 1.0, 0.0)
        put_ref[i] = jnp.concatenate([put] * (wide // LANES), axis=1).astype(jnp.bfloat16)

    own = orders_ref[pl.ds(band, 1), :].astype(jnp.float32)
    rows_ref[...] = jnp.transpose(jnp.broadcast_to(own, (LANES, per_owner))).astype(jnp.int32)

    scale = 1.0 / math.sqrt(total)
    count = owners * per_owner
    for b in range(owners):
        order = orders_ref[b : b + 1, :]
        factor = jnp.where(order == 0, scale, 2.0 * scale)
        step = iota((blocks, per_owner), 0) + lon * blocks
        cos_a, sin_a = turn((step * LANES * order) & (total - 1), total)
        turn_ref[0, b] = cos_a * factor
        turn_ref[1, b] = sin_a * factor
        cos_b, sin_b = turn((iota((LANES, per_owner), 0) * order) & (total - 1), total)
        for c, table in ((0, cos_b), (1, sin_b)):
            high, low = split(table)
            at = c * count + b * per_owner
            basis_ref[0, :, at : at + per_owner] = high
            basis_ref[1, :, at : at + per_owner] = low


def spectral(lon_count, owners, pick_ref, put_ref, rows_ref, folded_ref, legendre_ref, love_ref, out_ref, spread_ref, kept_ref):
    per_owner = rows_ref.shape[0]
    quarter = per_owner // lon_count
    degrees = legendre_ref.shape[1]
    cycles = folded_ref.shape[1] // 2
    northern = owners * cycles
    group = degrees // northern
    wide = group * northern
    lon = lax.axis_index("lon")
    pick = pick_ref[...]

    pad = jnp.zeros((LANES - 2 * northern, LANES), jnp.float32)
    for q in range(lon_count):
        pieces = [folded_ref[b * lon_count + q].astype(jnp.float32) for b in range(owners)]
        turned = jnp.transpose(jnp.concatenate(pieces + [pad], axis=0)).astype(jnp.bfloat16)
        spread_ref[q] = dot_nt(turned, pick)

    degree = lon * degrees + iota((ROWS, degrees), 1)
    diagonal = iota((ROWS, wide), 0) == iota((ROWS, wide), 1) // northern
    love = [[love_ref[g, f : f + 1, :] for f in range(2)] for g in range(2)]

    for q in range(lon_count):
        for pair in range(quarter // (2 * group)):
            halves = []
            for half in range(2):
                first = (pair * 2 + half) * group
                left = []
                for f in range(2):
                    for p in range(2):
                        for c in range(2):
                            at = (f * 2 + c) * quarter + first
                            left.append(
                                jnp.where(diagonal, spread_ref[q, at : at + group, p * wide : (p + 1) * wide], 0.0)
                            )
                left = jnp.concatenate(left, axis=0).astype(jnp.bfloat16)
                start = (q * quarter + first) * northern
                table = legendre_ref[start : start + wide]
                analysed = dot(left, table)
                order = rows_ref[q * quarter + first : q * quarter + first + group]
                gap = degree - jnp.concatenate([order] * (degrees // LANES), axis=1)
                valid = gap >= 0
                keep = [valid & ((gap & 1) == p) for p in range(2)]
                mixed = []
                for g in range(2):
                    for p in range(2):
                        for c in range(2):
                            lo = (p * 2 + c) * group
                            hi = ((2 + p) * 2 + c) * group
                            value = love[g][0] * analysed[lo : lo + group] + love[g][1] * analysed[hi : hi + group]
                            mixed.append(jnp.where(keep[p], value, 0.0))
                mixed = jnp.concatenate(mixed, axis=0).astype(jnp.bfloat16)
                halves.append(dot_nt(mixed, table))
            at = q * quarter + pair * 2 * group
            for g in range(2):
                for c in range(2):
                    rows = []
                    for half in range(2):
                        even = halves[half][(g * 4 + c) * group : (g * 4 + c + 1) * group]
                        odd = halves[half][(g * 4 + 2 + c) * group : (g * 4 + 3 + c) * group]
                        rows.append((even, odd))
                    for h in range(2):
                        both = [even + odd if h == 0 else even - odd for even, odd in rows]
                        both = [jnp.where(diagonal, value, 0.0) for value in both]
                        kept_ref[g * 2 + h, c * per_owner + at : c * per_owner + at + 2 * group, :] = jnp.concatenate(
                            both, axis=0
                        ).astype(jnp.bfloat16)

    total = None
    for i in range(4):
        term = dot_nt(put_ref[i], kept_ref[i])
        total = term if total is None else total + term
    total = total.astype(out_ref.dtype)
    for b in range(owners):
        for q in range(lon_count):
            out_ref[b * lon_count + q] = total[b * 4 * cycles : (b + 1) * 4 * cycles]


def synthesise_grid(lon_count, turn_ref, basis_ref, values_ref, out_ref, left_ref):
    owners, blocks, per_owner = turn_ref.shape[1:]
    rows = values_ref.shape[1]
    cycles = out_ref.shape[2]
    count = owners * per_owner
    for b in range(owners):
        value = values_ref[b * lon_count].astype(jnp.float32)
        for q in range(1, lon_count):
            value = value + values_ref[b * lon_count + q].astype(jnp.float32)
        re, im = value[:, :per_owner], value[:, per_owner:]
        at = b * per_owner
        for a in range(blocks):
            ca, sa = turn_ref[0, b, a : a + 1], turn_ref[1, b, a : a + 1]
            for c, term in ((0, ca * re - sa * im), (1, -(sa * re + ca * im))):
                high, low = split(term)
                left_ref[0, a * rows : (a + 1) * rows, c * count + at : c * count + at + per_owner] = high
                left_ref[1, a * rows : (a + 1) * rows, c * count + at : c * count + at + per_owner] = low
    grid = dot_nt(left_ref[0], basis_ref[0])
    grid = grid + dot_nt(left_ref[1], basis_ref[0])
    grid = grid + dot_nt(left_ref[0], basis_ref[1])
    for a in range(blocks):
        for g in range(2):
            for h in range(2):
                at = a * rows + (g * 2 + h) * cycles
                out_ref[g, h, :, a * LANES : (a + 1) * LANES] = grid[at : at + cycles]


def fits(owners, lon_count, cycles, points, per_owner, degrees):
    northern = owners * cycles
    total = points * lon_count
    return (
        per_owner == LANES
        and 4 * per_owner == lon_count * LANES
        and 2 * cycles == ROWS
        and 4 * northern == LANES
        and ROWS * northern == degrees
        and degrees % LANES == 0
        and owners == ROWS
        and points % LANES == 0
        and total & (total - 1) == 0
        and owners * per_owner * LANES < 1 << 24
    )


def per_device_kernels(loads, legendre, love, cycle_weight, order_list, cycle_order):
    owners = lax.axis_size("band")
    lon_count = lax.axis_size("lon")
    cycles, points = loads.shape[2], loads.shape[3]
    per_owner, degrees, northern = legendre.shape
    total = points * lon_count
    devices = owners * lon_count
    blocks = points // LANES
    everyone = ("band", "lon")
    vmem = pl.BlockSpec(memory_space=pltpu.VMEM)
    smem = pl.BlockSpec(memory_space=pltpu.SMEM)
    table = order_list.reshape(owners, per_owner)

    def kernel(body, out_shape, in_specs, scratch_shapes, flops):
        return pl.pallas_call(
            body,
            out_shape=out_shape,
            in_specs=in_specs,
            out_specs=jax.tree.map(lambda _: vmem, out_shape),
            scratch_shapes=scratch_shapes,
            compiler_params=pltpu.CompilerParams(vmem_limit_bytes=VMEM_LIMIT),
            cost_estimate=pl.CostEstimate(flops=flops, bytes_accessed=1 << 20, transcendentals=0),
            name=getattr(body, "func", body).__name__,
        )

    parts = [loads]
    for k in range(1, lon_count):
        parts.append(lax.ppermute(loads, "lon", [(i, (i + k) % lon_count) for i in range(lon_count)]))
    count = lon_count * blocks
    width = owners * per_owner // lon_count
    right, first, column, pick, put, order_rows, turns, basis = kernel(
        functools.partial(tables, lon_count, cycles, degrees, blocks, total),
        (
            jax.ShapeDtypeStruct((3 * LANES, 2 * width), jnp.bfloat16),
            jax.ShapeDtypeStruct((2, count, width), jnp.float32),
            jax.ShapeDtypeStruct((2 * cycles, LANES), jnp.float32),
            jax.ShapeDtypeStruct((2 * degrees, LANES), jnp.bfloat16),
            jax.ShapeDtypeStruct((4, LANES, degrees), jnp.bfloat16),
            jax.ShapeDtypeStruct((per_owner, LANES), jnp.int32),
            jax.ShapeDtypeStruct((2, owners, blocks, per_owner), jnp.float32),
            jax.ShapeDtypeStruct((2, LANES, 2 * owners * per_owner), jnp.bfloat16),
        ),
        [vmem, smem, smem],
        [],
        1 << 31,
    )(table, cycle_weight, cycle_order)
    folded = kernel(
        analyse_grid,
        jax.ShapeDtypeStruct((devices, 2 * cycles, LANES), jnp.bfloat16),
        [vmem] * (3 + lon_count),
        [
            pltpu.VMEM((count * 4 * cycles, LANES), jnp.float32),
            pltpu.VMEM((count * 4 * cycles, 2 * width), jnp.float32),
        ],
        1 << 31,
    )(right, first, column, *parts)
    arrived = lax.all_to_all(folded, everyone, split_axis=0, concat_axis=0, tiled=True)

    rows = jnp.transpose(legendre, (0, 2, 1)).reshape(per_owner * northern, degrees)
    values = kernel(
        functools.partial(spectral, lon_count, owners),
        jax.ShapeDtypeStruct((devices, 4 * cycles, 2 * per_owner), jnp.bfloat16),
        [vmem] * 6,
        [
            pltpu.VMEM((lon_count, LANES, 2 * degrees), jnp.float32),
            pltpu.VMEM((4, 2 * per_owner, degrees), jnp.bfloat16),
        ],
        1 << 32,
    )(pick, put, order_rows, arrived, rows, love)
    returned = lax.all_to_all(values, everyone, split_axis=0, concat_axis=0, tiled=True)

    return kernel(
        functools.partial(synthesise_grid, lon_count),
        jax.ShapeDtypeStruct(loads.shape, jnp.float32),
        [vmem] * 3,
        [pltpu.VMEM((2, 4 * cycles * blocks, 2 * owners * per_owner), jnp.bfloat16)],
        1 << 31,
    )(turns, basis, returned)


def per_device(loads, legendre, love, cycle_weight, order_list, cycle_order):
    sizes = (lax.axis_size("band"), lax.axis_size("lon"), loads.shape[2], loads.shape[3], legendre.shape[0], legendre.shape[1])
    form = per_device_kernels if fits(*sizes) else per_device_plain
    return form(loads, legendre, love, cycle_weight, order_list, cycle_order)


def cycle_basis(order_ids, positions, total):
    phase = positions[:, None] * order_ids[None, :] % total
    angle = phase.astype(jnp.float32) * (2.0 * math.pi / total)
    scale = 1.0 / math.sqrt(total)
    return (jnp.cos(angle) * scale, jnp.sin(angle) * scale)


def per_device_plain(loads, legendre, love, cycle_weight, order_list, cycle_order):
    highest = lax.Precision.HIGHEST
    owners = lax.axis_size("band")
    lon_count = lax.axis_size("lon")
    band_index = lax.axis_index("band")
    lon_index = lax.axis_index("lon")
    cycle_pairs = loads.shape[2]
    points = loads.shape[3]
    total = points * lon_count
    orders = order_list.shape[0]
    per_owner = legendre.shape[0]
    degree_count = legendre.shape[1]
    northern = legendre.shape[2]
    quarter = per_owner // lon_count
    positions = lon_index * points + jnp.arange(points, dtype=jnp.int32)
    cosine, sine = cycle_basis(order_list, positions, total)
    my_cycles = lax.dynamic_slice_in_dim(cycle_order, band_index * cycle_pairs, cycle_pairs)
    picker = my_cycles[:, None] == jnp.arange(northern, dtype=jnp.int32)[None, :]
    weights = jnp.sum(jnp.where(picker, cycle_weight[None, :], 0.0), axis=1)
    forward = jnp.stack([cosine, -sine], axis=1)
    spectrum = jnp.einsum("fhjx,xrm->fhjrm", loads, forward, precision=highest)
    spectrum = spectrum.reshape(2, 2, cycle_pairs, 2, owners, per_owner)
    summed = lax.psum_scatter(spectrum, "lon", scatter_dimension=5, tiled=True)
    cycle_scale = weights[None, :, None, None, None]
    symmetric = ((summed[:, 0] + summed[:, 1]) * cycle_scale).astype(jnp.bfloat16)
    antisym = ((summed[:, 0] - summed[:, 1]) * cycle_scale).astype(jnp.bfloat16)
    folded = jnp.stack([symmetric, antisym], axis=1)
    slot_width = folded.shape[5]
    outgoing = jnp.transpose(folded, (4, 5, 0, 1, 3, 2)).reshape(owners, slot_width, 8, cycle_pairs)
    arrived = lax.all_to_all(outgoing, "band", split_axis=0, concat_axis=3, tiled=True).reshape(
        slot_width, 8, northern
    )
    columns = lax.all_gather(arrived, "lon", axis=0, tiled=True)
    inverse_rows = jnp.argsort(cycle_order)
    columns_sorted = jnp.take(columns, inverse_rows, axis=2)
    my_orders = lax.dynamic_slice_in_dim(order_list, band_index * per_owner, per_owner)
    degrees = lon_index * degree_count + jnp.arange(degree_count, dtype=jnp.int32)
    analysed = jnp.einsum(
        "olk,ock->ocl", legendre, columns_sorted, preferred_element_type=jnp.float32
    )
    analysed = analysed.reshape(per_owner, 2, 2, 2, degree_count)
    even = (degrees[None, :] - my_orders[:, None]) % 2 == 0
    valid = degrees[None, :] >= my_orders[:, None]
    selected = jnp.where(even[:, None, None, :], analysed[:, :, 0], analysed[:, :, 1])
    selected = selected * valid[:, None, None, :].astype(jnp.float32)
    response = jnp.einsum("gfl,ofrl->ogrl", love, selected, precision=highest).astype(jnp.bfloat16)
    even_part = jnp.where((even & valid)[:, None, None, :], response, jnp.zeros_like(response))
    odd_part = jnp.where((~even & valid)[:, None, None, :], response, jnp.zeros_like(response))
    stacked = jnp.stack([even_part, odd_part], axis=2).reshape(per_owner, 8, degree_count)
    partial_sorted = jnp.einsum(
        "olk,ocl->ock", legendre, stacked, preferred_element_type=jnp.float32
    )
    partial_value = jnp.take(partial_sorted, cycle_order, axis=2)
    reduced = lax.psum_scatter(partial_value, "lon", scatter_dimension=0, tiled=True)
    returned = lax.all_to_all(reduced, "band", split_axis=2, concat_axis=0, tiled=True)
    gathered = lax.all_gather(returned[None], "lon", axis=0, tiled=True).reshape(
        orders, 8, cycle_pairs
    )
    slot_ids = jnp.transpose(order_list.reshape(owners, lon_count, quarter), (1, 0, 2)).reshape(
        orders
    )
    cosine_back, sine_back = cycle_basis(slot_ids, positions, total)
    pieces = gathered.reshape(orders, 2, 2, 2, cycle_pairs)
    cycle_values = jnp.stack(
        [pieces[:, :, 0] + pieces[:, :, 1], pieces[:, :, 0] - pieces[:, :, 1]], axis=2
    )
    factor = jnp.where(slot_ids == 0, 1.0, 2.0).astype(jnp.float32)
    inverse = jnp.stack([cosine_back.T, -sine_back.T], axis=0)
    scaled = cycle_values * factor[:, None, None, None, None]
    return jnp.einsum("sghrp,rsx->ghpx", scaled, inverse, precision=highest)


def solution(mesh):
    return jax.shard_map(
        per_device,
        mesh=mesh,
        in_specs=(
            P(None, None, "band", "lon"),
            P("band", "lon", None),
            P(None, None, "lon"),
            P(),
            P(),
            P(),
        ),
        out_specs=P(None, None, "band", "lon"),
        check_vma=False,
    )
```

```python
import functools
import math

import jax
import jax.numpy as jnp
from jax import lax
from jax.experimental import pallas as pl
from jax.experimental.pallas import tpu as pltpu
from jax.sharding import PartitionSpec as P

LANES = 128
ROWS = 8
VMEM_LIMIT = 12 << 20
NT = (((1,), (1,)), ((), ()))


def iota(shape, axis):
    return lax.broadcasted_iota(jnp.int32, shape, axis)


def turn(phase, total):
    shift = (total // 4).bit_length() - 1
    quadrant = (phase + total // 8) >> shift
    x = (phase - (quadrant << shift)).astype(jnp.float32) * (2.0 * math.pi / total)
    z = x * x
    s = ((-1.9515295891e-4 * z + 8.3321608736e-3) * z - 1.6666654611e-1) * z * x + x
    c = ((2.443315711809948e-5 * z - 1.388731625493765e-3) * z + 4.166664568298827e-2) * z * z
    c = c - 0.5 * z + 1.0
    odd = (quadrant & 1) == 1
    cosine = jnp.where(odd, s, c)
    sine = jnp.where(odd, c, s)
    cosine = jnp.where(((quadrant + 1) & 2) == 2, -cosine, cosine)
    sine = jnp.where((quadrant & 2) == 2, -sine, sine)
    return cosine, sine


def split(x):
    high = x.astype(jnp.bfloat16)
    return high, (x - high.astype(jnp.float32)).astype(jnp.bfloat16)


def dot(a, b):
    return jnp.dot(a, b, preferred_element_type=jnp.float32)


def dot_nt(a, b):
    return lax.dot_general(a, b, NT, preferred_element_type=jnp.float32)


def analyse_grid(right_ref, turn_ref, weight_ref, *refs):
    parts, out_ref, points_ref, mid_ref = refs[:-3], refs[-3], refs[-2], refs[-1]
    lon_count = len(parts)
    cycles = parts[0].shape[2]
    blocks = parts[0].shape[3] // LANES
    owners = out_ref.shape[0] // lon_count
    count, width = turn_ref.shape[1:]
    quarter = width // owners
    pieces = LANES // quarter
    step = 2 * cycles

    for q, part in enumerate(parts):
        for a in range(blocks):
            for f in range(2):
                north = part[f, 0, :, a * LANES : (a + 1) * LANES]
                south = part[f, 1, :, a * LANES : (a + 1) * LANES]
                at = ((q * blocks + a) * 2 + f) * step
                points_ref[at : at + step] = jnp.concatenate([north + south, north - south], axis=0)
    high, low = split(points_ref[...])
    mid_ref[...] = dot(jnp.concatenate([high, low, high], axis=1), right_ref[...])

    sums = [[jnp.zeros((step, width), jnp.float32) for _ in range(2)] for _ in range(2)]
    for a in range(count):
        ca, sa = turn_ref[0, a : a + 1], turn_ref[1, a : a + 1]
        for f in range(2):
            at = (a * 2 + f) * step
            tc = mid_ref[at : at + step, :width]
            ts = mid_ref[at : at + step, width:]
            sums[f][0] = sums[f][0] + (ca * tc - sa * ts)
            sums[f][1] = sums[f][1] - (sa * tc + ca * ts)

    slot = iota((1, LANES), 1) // quarter
    weight = weight_ref[...]
    for owner in range(owners):
        t, i = owner // pieces, owner % pieces
        block = None
        for e in range(4):
            piece = sums[e // 2][e % 2][:, t * LANES : (t + 1) * LANES]
            move = (e - i) * quarter % LANES
            piece = pltpu.roll(piece, move, 1) if move else piece
            block = piece if block is None else jnp.where(slot == e, piece, block)
        block = (block * weight).astype(out_ref.dtype)
        for q in range(lon_count):
            out_ref[owner * lon_count + q] = block


def tables(lon_count, cycles, degrees, blocks, total, orders_ref, weight_ref, cycle_ref, *out_refs):
    right_ref, first_ref, column_ref, pick_ref, put_ref, rows_ref, turn_ref, basis_ref = out_refs
    owners, per_owner = orders_ref.shape
    quarter = per_owner // lon_count
    pieces = LANES // quarter
    northern = owners * cycles
    group = degrees // northern
    wide = group * northern
    band, lon = lax.axis_index("band"), lax.axis_index("lon")
    lane = iota((1, LANES), 1)

    mine = pltpu.roll(orders_ref[...], (LANES - quarter * lon) % LANES, 1)
    slot = lane // quarter
    shifted = [mine if i == 0 else pltpu.roll(mine, quarter * i, 1) for i in range(pieces)]
    rows = []
    for t in range(owners // pieces):
        row = shifted[0][t * pieces : t * pieces + 1]
        for i in range(1, pieces):
            row = jnp.where(slot == i, shifted[i][t * pieces + i : t * pieces + i + 1], row)
        rows.append(row)
    orders = jnp.concatenate(rows, axis=1)
    width = orders.shape[1]
    for c, table in enumerate(turn((iota((LANES, width), 0) * orders) & (total - 1), total)):
        high, low = split(table)
        for k, value in enumerate((high, high, low)):
            right_ref[k * LANES : (k + 1) * LANES, c * width : (c + 1) * width] = value
    for k in range(lon_count):
        origin = (lon + lon_count - k) % lon_count
        step = iota((blocks, width), 0) + origin * blocks
        for c, table in enumerate(turn((step * LANES * orders) & (total - 1), total)):
            first_ref[c, k * blocks : (k + 1) * blocks] = table
    sub = iota((2 * cycles, LANES), 0) % cycles
    weight = jnp.zeros((2 * cycles, LANES), jnp.float32)
    for j in range(cycles):
        weight = jnp.where(sub == j, weight_ref[cycle_ref[band * cycles + j]], weight)
    column_ref[...] = weight * (1.0 / math.sqrt(total))

    def cycle_lanes(repeat):
        place = (lane // (repeat * cycles)) * cycles + lane % cycles
        row = jnp.full((1, LANES), -1, jnp.int32)
        for i in range(northern):
            row = jnp.where(place == i, cycle_ref[i], row)
        return row

    parity_lane = (lane // cycles) % 2
    found = iota((northern, LANES), 0) == cycle_lanes(2)
    for p in range(2):
        one = jnp.where(found & (parity_lane == p), 1.0, 0.0)
        copies = jnp.concatenate([one] * (LANES // northern), axis=0)
        pick_ref[p * LANES : (p + 1) * LANES] = copies.astype(jnp.bfloat16)

    leaving = cycle_lanes(4).astype(jnp.float32)
    cycle_rows = jnp.transpose(jnp.broadcast_to(leaving, (LANES, LANES))).astype(jnp.int32)
    found = cycle_rows == iota((LANES, LANES), 1) % northern
    part = (iota((LANES, LANES), 0) // cycles) % 4
    for i in range(4):
        put = jnp.where(found & (part == i), 1.0, 0.0)
        put_ref[i] = jnp.concatenate([put] * (wide // LANES), axis=1).astype(jnp.bfloat16)

    own = orders_ref[pl.ds(band, 1), :].astype(jnp.float32)
    rows_ref[...] = jnp.transpose(jnp.broadcast_to(own, (LANES, per_owner))).astype(jnp.int32)

    scale = 1.0 / math.sqrt(total)
    count = owners * per_owner
    for b in range(owners):
        order = orders_ref[b : b + 1, :]
        factor = jnp.where(order == 0, scale, 2.0 * scale)
        step = iota((blocks, per_owner), 0) + lon * blocks
        cos_a, sin_a = turn((step * LANES * order) & (total - 1), total)
        turn_ref[0, b] = cos_a * factor
        turn_ref[1, b] = sin_a * factor
        cos_b, sin_b = turn((iota((LANES, per_owner), 0) * order) & (total - 1), total)
        for c, table in ((0, cos_b), (1, sin_b)):
            high, low = split(table)
            at = c * count + b * per_owner
            basis_ref[0, :, at : at + per_owner] = high
            basis_ref[1, :, at : at + per_owner] = low


def spectral(lon_count, owners, pick_ref, put_ref, rows_ref, folded_ref, legendre_ref, love_ref, out_ref, spread_ref, kept_ref):
    per_owner = rows_ref.shape[0]
    quarter = per_owner // lon_count
    degrees = legendre_ref.shape[1]
    cycles = folded_ref.shape[1] // 2
    northern = owners * cycles
    group = degrees // northern
    wide = group * northern
    lon = lax.axis_index("lon")
    pick = pick_ref[...]

    pad = jnp.zeros((LANES - 2 * northern, LANES), jnp.float32)
    turned = []
    for q in range(lon_count):
        pieces = [folded_ref[b * lon_count + q].astype(jnp.float32) for b in range(owners)]
        turned.append(jnp.transpose(jnp.concatenate(pieces + [pad], axis=0)))
    spread_ref[...] = dot_nt(jnp.concatenate(turned, axis=0).astype(jnp.bfloat16), pick)

    degree = lon * degrees + iota((ROWS, degrees), 1)
    diagonal = iota((ROWS, wide), 0) == iota((ROWS, wide), 1) // northern
    love = [[love_ref[g, f : f + 1, :] for f in range(2)] for g in range(2)]
    groups = per_owner // group

    def analyse(n):
        q, first = n * group // quarter, n * group % quarter
        left = []
        for f in range(2):
            for p in range(2):
                for c in range(2):
                    at = q * LANES + (f * 2 + c) * quarter + first
                    piece = spread_ref[at : at + group, p * LANES : (p + 1) * LANES]
                    left.append(jnp.where(diagonal, jnp.concatenate([piece] * (wide // LANES), axis=1), 0.0))
        left = jnp.concatenate(left, axis=0).astype(jnp.bfloat16)
        return dot(left, legendre_ref[n * wide : (n + 1) * wide])

    def respond(n, analysed):
        order = rows_ref[n * group : (n + 1) * group]
        gap = degree - jnp.concatenate([order] * (degrees // LANES), axis=1)
        valid = gap >= 0
        keep = [valid & ((gap & 1) == p) for p in range(2)]
        mixed = []
        for g in range(2):
            for p in range(2):
                for c in range(2):
                    lo = (p * 2 + c) * group
                    hi = ((2 + p) * 2 + c) * group
                    value = love[g][0] * analysed[lo : lo + group] + love[g][1] * analysed[hi : hi + group]
                    mixed.append(jnp.where(keep[p], value, 0.0))
        mixed = jnp.concatenate(mixed, axis=0).astype(jnp.bfloat16)
        return dot_nt(mixed, legendre_ref[n * wide : (n + 1) * wide])

    def keep_pair(n, halves):
        for g in range(2):
            for c in range(2):
                lo, hi = (g * 4 + c) * group, (g * 4 + 2 + c) * group
                rows = [(half[lo : lo + group], half[hi : hi + group]) for half in halves]
                at = c * per_owner + n * group
                for h in range(2):
                    both = [even + odd if h == 0 else even - odd for even, odd in rows]
                    both = [jnp.where(diagonal, value, 0.0) for value in both]
                    kept_ref[g * 2 + h, at : at + 2 * group, :] = jnp.concatenate(both, axis=0).astype(jnp.bfloat16)

    analysed, partial = {}, {}
    for n in range(groups + 2):
        if n < groups:
            analysed[n] = analyse(n)
        if 1 <= n <= groups:
            partial[n - 1] = respond(n - 1, analysed.pop(n - 1))
        if n >= 3 and n % 2 == 1:
            keep_pair(n - 3, [partial.pop(n - 3), partial.pop(n - 2)])

    total = None
    for i in range(4):
        term = dot_nt(put_ref[i], kept_ref[i])
        total = term if total is None else total + term
    total = total.astype(out_ref.dtype)
    for b in range(owners):
        for q in range(lon_count):
            out_ref[b * lon_count + q] = total[b * 4 * cycles : (b + 1) * 4 * cycles]


def synthesise_grid(lon_count, turn_ref, basis_ref, values_ref, out_ref, left_ref):
    owners, blocks, per_owner = turn_ref.shape[1:]
    rows = values_ref.shape[1]
    cycles = out_ref.shape[2]
    count = owners * per_owner
    half = blocks * rows
    for b in range(owners):
        value = values_ref[b * lon_count].astype(jnp.float32)
        for q in range(1, lon_count):
            value = value + values_ref[b * lon_count + q].astype(jnp.float32)
        re, im = value[:, :per_owner], value[:, per_owner:]
        at = b * per_owner
        for a in range(blocks):
            ca, sa = turn_ref[0, b, a : a + 1], turn_ref[1, b, a : a + 1]
            for c, term in ((0, ca * re - sa * im), (1, -(sa * re + ca * im))):
                high, low = split(term)
                left_ref[a * rows : (a + 1) * rows, c * count + at : c * count + at + per_owner] = high
                left_ref[half + a * rows : half + (a + 1) * rows, c * count + at : c * count + at + per_owner] = low
    grid = dot_nt(left_ref[...], basis_ref[0])
    grid = grid[:half] + grid[half:] + dot_nt(left_ref[:half], basis_ref[1])
    for a in range(blocks):
        for g in range(2):
            for h in range(2):
                at = a * rows + (g * 2 + h) * cycles
                out_ref[g, h, :, a * LANES : (a + 1) * LANES] = grid[at : at + cycles]


def fits(owners, lon_count, cycles, points, per_owner, degrees):
    northern = owners * cycles
    total = points * lon_count
    return (
        per_owner == LANES
        and 4 * per_owner == lon_count * LANES
        and 2 * cycles == ROWS
        and 4 * northern == LANES
        and ROWS * northern == degrees
        and degrees % LANES == 0
        and owners == ROWS
        and points % LANES == 0
        and total & (total - 1) == 0
        and owners * per_owner * LANES < 1 << 24
    )


def per_device_kernels(loads, legendre, love, cycle_weight, order_list, cycle_order):
    owners = lax.axis_size("band")
    lon_count = lax.axis_size("lon")
    cycles, points = loads.shape[2], loads.shape[3]
    per_owner, degrees, northern = legendre.shape
    total = points * lon_count
    devices = owners * lon_count
    blocks = points // LANES
    everyone = ("band", "lon")
    vmem = pl.BlockSpec(memory_space=pltpu.VMEM)
    smem = pl.BlockSpec(memory_space=pltpu.SMEM)
    table = order_list.reshape(owners, per_owner)

    def kernel(body, out_shape, in_specs, scratch_shapes, flops):
        return pl.pallas_call(
            body,
            out_shape=out_shape,
            in_specs=in_specs,
            out_specs=jax.tree.map(lambda _: vmem, out_shape),
            scratch_shapes=scratch_shapes,
            compiler_params=pltpu.CompilerParams(vmem_limit_bytes=VMEM_LIMIT),
            cost_estimate=pl.CostEstimate(flops=flops, bytes_accessed=1 << 20, transcendentals=0),
            name=getattr(body, "func", body).__name__,
        )

    parts = [loads]
    for k in range(1, lon_count):
        parts.append(lax.ppermute(loads, "lon", [(i, (i + k) % lon_count) for i in range(lon_count)]))
    count = lon_count * blocks
    width = owners * per_owner // lon_count
    right, first, column, pick, put, order_rows, turns, basis = kernel(
        functools.partial(tables, lon_count, cycles, degrees, blocks, total),
        (
            jax.ShapeDtypeStruct((3 * LANES, 2 * width), jnp.bfloat16),
            jax.ShapeDtypeStruct((2, count, width), jnp.float32),
            jax.ShapeDtypeStruct((2 * cycles, LANES), jnp.float32),
            jax.ShapeDtypeStruct((2 * LANES, LANES), jnp.bfloat16),
            jax.ShapeDtypeStruct((4, LANES, degrees), jnp.bfloat16),
            jax.ShapeDtypeStruct((per_owner, LANES), jnp.int32),
            jax.ShapeDtypeStruct((2, owners, blocks, per_owner), jnp.float32),
            jax.ShapeDtypeStruct((2, LANES, 2 * owners * per_owner), jnp.bfloat16),
        ),
        [vmem, smem, smem],
        [],
        1 << 31,
    )(table, cycle_weight, cycle_order)
    folded = kernel(
        analyse_grid,
        jax.ShapeDtypeStruct((devices, 2 * cycles, LANES), jnp.bfloat16),
        [vmem] * (3 + lon_count),
        [
            pltpu.VMEM((count * 4 * cycles, LANES), jnp.float32),
            pltpu.VMEM((count * 4 * cycles, 2 * width), jnp.float32),
        ],
        1 << 31,
    )(right, first, column, *parts)
    arrived = lax.all_to_all(folded, everyone, split_axis=0, concat_axis=0, tiled=True)

    rows = jnp.transpose(legendre, (0, 2, 1)).reshape(per_owner * northern, degrees)
    values = kernel(
        functools.partial(spectral, lon_count, owners),
        jax.ShapeDtypeStruct((devices, 4 * cycles, 2 * per_owner), jnp.bfloat16),
        [vmem] * 6,
        [
            pltpu.VMEM((lon_count * LANES, 2 * LANES), jnp.float32),
            pltpu.VMEM((4, 2 * per_owner, degrees), jnp.bfloat16),
        ],
        1 << 32,
    )(pick, put, order_rows, arrived, rows, love)
    returned = lax.all_to_all(values, everyone, split_axis=0, concat_axis=0, tiled=True)

    return kernel(
        functools.partial(synthesise_grid, lon_count),
        jax.ShapeDtypeStruct(loads.shape, jnp.float32),
        [vmem] * 3,
        [pltpu.VMEM((2 * 4 * cycles * blocks, 2 * owners * per_owner), jnp.bfloat16)],
        1 << 31,
    )(turns, basis, returned)


def per_device(loads, legendre, love, cycle_weight, order_list, cycle_order):
    sizes = (lax.axis_size("band"), lax.axis_size("lon"), loads.shape[2], loads.shape[3], legendre.shape[0], legendre.shape[1])
    form = per_device_kernels if fits(*sizes) else per_device_plain
    return form(loads, legendre, love, cycle_weight, order_list, cycle_order)


def cycle_basis(order_ids, positions, total):
    phase = positions[:, None] * order_ids[None, :] % total
    angle = phase.astype(jnp.float32) * (2.0 * math.pi / total)
    scale = 1.0 / math.sqrt(total)
    return (jnp.cos(angle) * scale, jnp.sin(angle) * scale)


def per_device_plain(loads, legendre, love, cycle_weight, order_list, cycle_order):
    highest = lax.Precision.HIGHEST
    owners = lax.axis_size("band")
    lon_count = lax.axis_size("lon")
    band_index = lax.axis_index("band")
    lon_index = lax.axis_index("lon")
    cycle_pairs = loads.shape[2]
    points = loads.shape[3]
    total = points * lon_count
    orders = order_list.shape[0]
    per_owner = legendre.shape[0]
    degree_count = legendre.shape[1]
    northern = legendre.shape[2]
    quarter = per_owner // lon_count
    positions = lon_index * points + jnp.arange(points, dtype=jnp.int32)
    cosine, sine = cycle_basis(order_list, positions, total)
    my_cycles = lax.dynamic_slice_in_dim(cycle_order, band_index * cycle_pairs, cycle_pairs)
    picker = my_cycles[:, None] == jnp.arange(northern, dtype=jnp.int32)[None, :]
    weights = jnp.sum(jnp.where(picker, cycle_weight[None, :], 0.0), axis=1)
    forward = jnp.stack([cosine, -sine], axis=1)
    spectrum = jnp.einsum("fhjx,xrm->fhjrm", loads, forward, precision=highest)
    spectrum = spectrum.reshape(2, 2, cycle_pairs, 2, owners, per_owner)
    summed = lax.psum_scatter(spectrum, "lon", scatter_dimension=5, tiled=True)
    cycle_scale = weights[None, :, None, None, None]
    symmetric = ((summed[:, 0] + summed[:, 1]) * cycle_scale).astype(jnp.bfloat16)
    antisym = ((summed[:, 0] - summed[:, 1]) * cycle_scale).astype(jnp.bfloat16)
    folded = jnp.stack([symmetric, antisym], axis=1)
    slot_width = folded.shape[5]
    outgoing = jnp.transpose(folded, (4, 5, 0, 1, 3, 2)).reshape(owners, slot_width, 8, cycle_pairs)
    arrived = lax.all_to_all(outgoing, "band", split_axis=0, concat_axis=3, tiled=True).reshape(
        slot_width, 8, northern
    )
    columns = lax.all_gather(arrived, "lon", axis=0, tiled=True)
    inverse_rows = jnp.argsort(cycle_order)
    columns_sorted = jnp.take(columns, inverse_rows, axis=2)
    my_orders = lax.dynamic_slice_in_dim(order_list, band_index * per_owner, per_owner)
    degrees = lon_index * degree_count + jnp.arange(degree_count, dtype=jnp.int32)
    analysed = jnp.einsum(
        "olk,ock->ocl", legendre, columns_sorted, preferred_element_type=jnp.float32
    )
    analysed = analysed.reshape(per_owner, 2, 2, 2, degree_count)
    even = (degrees[None, :] - my_orders[:, None]) % 2 == 0
    valid = degrees[None, :] >= my_orders[:, None]
    selected = jnp.where(even[:, None, None, :], analysed[:, :, 0], analysed[:, :, 1])
    selected = selected * valid[:, None, None, :].astype(jnp.float32)
    response = jnp.einsum("gfl,ofrl->ogrl", love, selected, precision=highest).astype(jnp.bfloat16)
    even_part = jnp.where((even & valid)[:, None, None, :], response, jnp.zeros_like(response))
    odd_part = jnp.where((~even & valid)[:, None, None, :], response, jnp.zeros_like(response))
    stacked = jnp.stack([even_part, odd_part], axis=2).reshape(per_owner, 8, degree_count)
    partial_sorted = jnp.einsum(
        "olk,ocl->ock", legendre, stacked, preferred_element_type=jnp.float32
    )
    partial_value = jnp.take(partial_sorted, cycle_order, axis=2)
    reduced = lax.psum_scatter(partial_value, "lon", scatter_dimension=0, tiled=True)
    returned = lax.all_to_all(reduced, "band", split_axis=2, concat_axis=0, tiled=True)
    gathered = lax.all_gather(returned[None], "lon", axis=0, tiled=True).reshape(
        orders, 8, cycle_pairs
    )
    slot_ids = jnp.transpose(order_list.reshape(owners, lon_count, quarter), (1, 0, 2)).reshape(
        orders
    )
    cosine_back, sine_back = cycle_basis(slot_ids, positions, total)
    pieces = gathered.reshape(orders, 2, 2, 2, cycle_pairs)
    cycle_values = jnp.stack(
        [pieces[:, :, 0] + pieces[:, :, 1], pieces[:, :, 0] - pieces[:, :, 1]], axis=2
    )
    factor = jnp.where(slot_ids == 0, 1.0, 2.0).astype(jnp.float32)
    inverse = jnp.stack([cosine_back.T, -sine_back.T], axis=0)
    scaled = cycle_values * factor[:, None, None, None, None]
    return jnp.einsum("sghrp,rsx->ghpx", scaled, inverse, precision=highest)


def solution(mesh):
    return jax.shard_map(
        per_device,
        mesh=mesh,
        in_specs=(
            P(None, None, "band", "lon"),
            P("band", "lon", None),
            P(None, None, "lon"),
            P(),
            P(),
            P(),
        ),
        out_specs=P(None, None, "band", "lon"),
        check_vma=False,
    )
```

```python
import functools
import math

import jax
import jax.numpy as jnp
from jax import lax
from jax.experimental import pallas as pl
from jax.experimental.pallas import tpu as pltpu
from jax.sharding import PartitionSpec as P

LANES = 128
ROWS = 8
VMEM_LIMIT = 12 << 20
NT = (((1,), (1,)), ((), ()))


def iota(shape, axis):
    return lax.broadcasted_iota(jnp.int32, shape, axis)


def turn(phase, total):
    shift = (total // 4).bit_length() - 1
    quadrant = (phase + total // 8) >> shift
    x = (phase - (quadrant << shift)).astype(jnp.float32) * (2.0 * math.pi / total)
    z = x * x
    s = ((-1.9515295891e-4 * z + 8.3321608736e-3) * z - 1.6666654611e-1) * z * x + x
    c = ((2.443315711809948e-5 * z - 1.388731625493765e-3) * z + 4.166664568298827e-2) * z * z
    c = c - 0.5 * z + 1.0
    odd = (quadrant & 1) == 1
    cosine = jnp.where(odd, s, c)
    sine = jnp.where(odd, c, s)
    cosine = jnp.where(((quadrant + 1) & 2) == 2, -cosine, cosine)
    sine = jnp.where((quadrant & 2) == 2, -sine, sine)
    return cosine, sine


def split(x):
    high = x.astype(jnp.bfloat16)
    return high, (x - high.astype(jnp.float32)).astype(jnp.bfloat16)


def dot(a, b):
    return jnp.dot(a, b, preferred_element_type=jnp.float32)


def dot_nt(a, b):
    return lax.dot_general(a, b, NT, preferred_element_type=jnp.float32)


def analyse_grid(right_ref, turn_ref, weight_ref, *refs):
    parts, out_ref, points_ref, mid_ref = refs[:-3], refs[-3], refs[-2], refs[-1]
    lon_count = len(parts)
    cycles = parts[0].shape[2]
    blocks = parts[0].shape[3] // LANES
    owners = out_ref.shape[0] // lon_count
    count, width = turn_ref.shape[1:]
    quarter = width // owners
    pieces = LANES // quarter
    step = 2 * cycles

    for q, part in enumerate(parts):
        for a in range(blocks):
            for f in range(2):
                north = part[f, 0, :, a * LANES : (a + 1) * LANES]
                south = part[f, 1, :, a * LANES : (a + 1) * LANES]
                at = ((q * blocks + a) * 2 + f) * step
                points_ref[at : at + step] = jnp.concatenate([north + south, north - south], axis=0)
    high, low = split(points_ref[...])
    mid_ref[...] = dot(jnp.concatenate([high, low, high], axis=1), right_ref[...])

    sums = [[jnp.zeros((step, width), jnp.float32) for _ in range(2)] for _ in range(2)]
    for a in range(count):
        ca, sa = turn_ref[0, a : a + 1], turn_ref[1, a : a + 1]
        for f in range(2):
            at = (a * 2 + f) * step
            tc = mid_ref[at : at + step, :width]
            ts = mid_ref[at : at + step, width:]
            sums[f][0] = sums[f][0] + (ca * tc - sa * ts)
            sums[f][1] = sums[f][1] - (sa * tc + ca * ts)

    slot = iota((1, LANES), 1) // quarter
    weight = weight_ref[...]
    for owner in range(owners):
        t, i = owner // pieces, owner % pieces
        block = None
        for e in range(4):
            piece = sums[e // 2][e % 2][:, t * LANES : (t + 1) * LANES]
            move = (e - i) * quarter % LANES
            piece = pltpu.roll(piece, move, 1) if move else piece
            block = piece if block is None else jnp.where(slot == e, piece, block)
        block = (block * weight).astype(out_ref.dtype)
        for q in range(lon_count):
            out_ref[owner * lon_count + q] = block


def tables(lon_count, cycles, degrees, blocks, total, orders_ref, weight_ref, cycle_ref, *out_refs):
    right_ref, first_ref, column_ref, pick_ref, put_ref, rows_ref, turn_ref, basis_ref = out_refs
    owners, per_owner = orders_ref.shape
    quarter = per_owner // lon_count
    pieces = LANES // quarter
    northern = owners * cycles
    group = degrees // northern
    wide = group * northern
    band, lon = lax.axis_index("band"), lax.axis_index("lon")
    lane = iota((1, LANES), 1)

    mine = pltpu.roll(orders_ref[...], (LANES - quarter * lon) % LANES, 1)
    slot = lane // quarter
    shifted = [mine if i == 0 else pltpu.roll(mine, quarter * i, 1) for i in range(pieces)]
    rows = []
    for t in range(owners // pieces):
        row = shifted[0][t * pieces : t * pieces + 1]
        for i in range(1, pieces):
            row = jnp.where(slot == i, shifted[i][t * pieces + i : t * pieces + i + 1], row)
        rows.append(row)
    orders = jnp.concatenate(rows, axis=1)
    width = orders.shape[1]
    for c, table in enumerate(turn((iota((LANES, width), 0) * orders) & (total - 1), total)):
        high, low = split(table)
        for k, value in enumerate((high, high, low)):
            right_ref[k * LANES : (k + 1) * LANES, c * width : (c + 1) * width] = value
    for k in range(lon_count):
        origin = (lon + lon_count - k) % lon_count
        step = iota((blocks, width), 0) + origin * blocks
        for c, table in enumerate(turn((step * LANES * orders) & (total - 1), total)):
            first_ref[c, k * blocks : (k + 1) * blocks] = table
    sub = iota((2 * cycles, LANES), 0) % cycles
    weight = jnp.zeros((2 * cycles, LANES), jnp.float32)
    for j in range(cycles):
        weight = jnp.where(sub == j, weight_ref[cycle_ref[band * cycles + j]], weight)
    column_ref[...] = weight * (1.0 / math.sqrt(total))

    def cycle_lanes(repeat):
        place = (lane // (repeat * cycles)) * cycles + lane % cycles
        row = jnp.full((1, LANES), -1, jnp.int32)
        for i in range(northern):
            row = jnp.where(place == i, cycle_ref[i], row)
        return row

    parity_lane = (lane // cycles) % 2
    found = iota((northern, LANES), 0) == cycle_lanes(2)
    for p in range(2):
        one = jnp.where(found & (parity_lane == p), 1.0, 0.0)
        copies = jnp.concatenate([one] * (LANES // northern), axis=0)
        pick_ref[p * LANES : (p + 1) * LANES] = copies.astype(jnp.bfloat16)

    leaving = cycle_lanes(4).astype(jnp.float32)
    cycle_rows = jnp.transpose(jnp.broadcast_to(leaving, (LANES, LANES))).astype(jnp.int32)
    found = cycle_rows == iota((LANES, LANES), 1) % northern
    part = (iota((LANES, LANES), 0) // cycles) % 4
    for i in range(4):
        put = jnp.where(found & (part == i), 1.0, 0.0)
        put_ref[i] = jnp.concatenate([put] * (wide // LANES), axis=1).astype(jnp.bfloat16)

    own = orders_ref[pl.ds(band, 1), :].astype(jnp.float32)
    rows_ref[...] = jnp.transpose(jnp.broadcast_to(own, (LANES, per_owner))).astype(jnp.int32)

    share = per_owner // 2
    first_lanes = lane < share

    def halves(x, y):
        return jnp.where(first_lanes, x, pltpu.roll(y, share, 1)), jnp.where(first_lanes, pltpu.roll(x, share, 1), y)

    scale = 1.0 / math.sqrt(total)
    for b in range(owners):
        order = orders_ref[b : b + 1, :]
        factor = jnp.where(order == 0, scale, 2.0 * scale)
        step = iota((blocks, per_owner), 0) + lon * blocks
        cos_a, sin_a = turn((step * LANES * order) & (total - 1), total)
        cos_a, sin_a = cos_a * factor, sin_a * factor
        for half, table in enumerate(halves(cos_a, -cos_a)):
            turn_ref[half, 0, b] = table
        for half, table in enumerate(halves(-sin_a, -sin_a)):
            turn_ref[half, 1, b] = table
        cos_b, sin_b = turn((iota((LANES, per_owner), 0) * order) & (total - 1), total)
        for half, table in enumerate(halves(cos_b, sin_b)):
            high, low = split(table)
            basis_ref[half, 0, :, b * per_owner : (b + 1) * per_owner] = high
            basis_ref[half, 1, :, b * per_owner : (b + 1) * per_owner] = low


def spectral(lon_count, owners, pick_ref, put_ref, rows_ref, folded_ref, legendre_ref, love_ref, out_ref, spread_ref, kept_ref):
    per_owner = rows_ref.shape[0]
    quarter = per_owner // lon_count
    degrees = legendre_ref.shape[1]
    cycles = folded_ref.shape[1] // 2
    northern = owners * cycles
    group = degrees // northern
    wide = group * northern
    lon = lax.axis_index("lon")
    share = per_owner // 2
    pick = pick_ref[...]

    pad = jnp.zeros((LANES - 2 * northern, LANES), jnp.float32)
    turned = []
    for q in range(lon_count):
        pieces = [folded_ref[b * lon_count + q].astype(jnp.float32) for b in range(owners)]
        turned.append(jnp.transpose(jnp.concatenate(pieces + [pad], axis=0)))
    spread_ref[...] = dot_nt(jnp.concatenate(turned, axis=0).astype(jnp.bfloat16), pick)

    degree = lon * degrees + iota((ROWS, degrees), 1)
    diagonal = iota((ROWS, wide), 0) == iota((ROWS, wide), 1) // northern
    love = [[love_ref[g, f : f + 1, :] for f in range(2)] for g in range(2)]
    groups = per_owner // group

    def analyse(n):
        q, first = n * group // quarter, n * group % quarter
        left = []
        for f in range(2):
            for p in range(2):
                for c in range(2):
                    at = q * LANES + (f * 2 + c) * quarter + first
                    piece = spread_ref[at : at + group, p * LANES : (p + 1) * LANES]
                    left.append(jnp.where(diagonal, jnp.concatenate([piece] * (wide // LANES), axis=1), 0.0))
        left = jnp.concatenate(left, axis=0).astype(jnp.bfloat16)
        return dot(left, legendre_ref[n * wide : (n + 1) * wide])

    def respond(n, analysed):
        order = rows_ref[n * group : (n + 1) * group]
        gap = degree - jnp.concatenate([order] * (degrees // LANES), axis=1)
        valid = gap >= 0
        keep = [valid & ((gap & 1) == p) for p in range(2)]
        mixed = []
        for g in range(2):
            for p in range(2):
                for c in range(2):
                    lo = (p * 2 + c) * group
                    hi = ((2 + p) * 2 + c) * group
                    value = love[g][0] * analysed[lo : lo + group] + love[g][1] * analysed[hi : hi + group]
                    mixed.append(jnp.where(keep[p], value, 0.0))
        mixed = jnp.concatenate(mixed, axis=0).astype(jnp.bfloat16)
        return dot_nt(mixed, legendre_ref[n * wide : (n + 1) * wide])

    def keep_pair(n, halves):
        for g in range(2):
            for c in range(2):
                lo, hi = (g * 4 + c) * group, (g * 4 + 2 + c) * group
                rows = [(half[lo : lo + group], half[hi : hi + group]) for half in halves]
                at = (n * group // share * 2 + c) * share + n * group % share
                for h in range(2):
                    both = [even + odd if h == 0 else even - odd for even, odd in rows]
                    both = [jnp.where(diagonal, value, 0.0) for value in both]
                    kept_ref[g * 2 + h, at : at + 2 * group, :] = jnp.concatenate(both, axis=0).astype(jnp.bfloat16)

    analysed, partial = {}, {}
    for n in range(groups + 2):
        if n < groups:
            analysed[n] = analyse(n)
        if 1 <= n <= groups:
            partial[n - 1] = respond(n - 1, analysed.pop(n - 1))
        if n >= 3 and n % 2 == 1:
            keep_pair(n - 3, [partial.pop(n - 3), partial.pop(n - 2)])

    total = None
    for i in range(4):
        term = dot_nt(put_ref[i], kept_ref[i])
        total = term if total is None else total + term
    total = total.astype(out_ref.dtype)
    for b in range(owners):
        for q in range(lon_count):
            lanes = slice(q % 2 * 2 * share, (q % 2 + 1) * 2 * share)
            out_ref[b * lon_count + q] = total[b * 4 * cycles : (b + 1) * 4 * cycles, lanes]


def add_degrees(lon_count, values_ref, out_ref):
    for b in range(out_ref.shape[0]):
        value = values_ref[b * lon_count].astype(jnp.float32)
        for q in range(1, lon_count):
            value = value + values_ref[b * lon_count + q].astype(jnp.float32)
        out_ref[b] = value


def half_grid(which, turn_ref, basis_ref, value_ref, left_ref):
    owners, rows, lanes = value_ref.shape
    blocks = turn_ref.shape[3]
    height = blocks * rows
    for b in range(owners):
        value = value_ref[b]
        other = pltpu.roll(value, lanes // 2, 1)
        for a in range(blocks):
            term = value * turn_ref[which, 0, b, a : a + 1] + other * turn_ref[which, 1, b, a : a + 1]
            high, low = split(term)
            left_ref[a * rows : (a + 1) * rows, b * lanes : (b + 1) * lanes] = high
            left_ref[height + a * rows : height + (a + 1) * rows, b * lanes : (b + 1) * lanes] = low
    grid = dot_nt(left_ref[...], basis_ref[which, 0])
    return grid[:height] + grid[height:] + dot_nt(left_ref[:height], basis_ref[which, 1])


def own_grid(turn_ref, basis_ref, value_ref, out_ref, left_ref):
    out_ref[...] = half_grid(lax.axis_index("lon") % 2, turn_ref, basis_ref, value_ref, left_ref)


def synthesise_grid(turn_ref, basis_ref, value_ref, grid_ref, out_ref, left_ref):
    rows = value_ref.shape[1]
    cycles = out_ref.shape[2]
    grid = grid_ref[...] + half_grid(1 - lax.axis_index("lon") % 2, turn_ref, basis_ref, value_ref, left_ref)
    for a in range(grid.shape[0] // rows):
        for g in range(2):
            for h in range(2):
                at = a * rows + (g * 2 + h) * cycles
                out_ref[g, h, :, a * LANES : (a + 1) * LANES] = grid[at : at + cycles]


def fits(owners, lon_count, cycles, points, per_owner, degrees):
    northern = owners * cycles
    total = points * lon_count
    return (
        per_owner == LANES
        and 4 * per_owner == lon_count * LANES
        and lon_count % 2 == 0
        and 2 * cycles == ROWS
        and 4 * northern == LANES
        and ROWS * northern == degrees
        and degrees % LANES == 0
        and owners == ROWS
        and points % LANES == 0
        and total & (total - 1) == 0
        and owners * per_owner * LANES < 1 << 24
    )


def per_device_kernels(loads, legendre, love, cycle_weight, order_list, cycle_order):
    owners = lax.axis_size("band")
    lon_count = lax.axis_size("lon")
    cycles, points = loads.shape[2], loads.shape[3]
    per_owner, degrees, northern = legendre.shape
    total = points * lon_count
    devices = owners * lon_count
    blocks = points // LANES
    everyone = ("band", "lon")
    vmem = pl.BlockSpec(memory_space=pltpu.VMEM)
    smem = pl.BlockSpec(memory_space=pltpu.SMEM)
    table = order_list.reshape(owners, per_owner)

    def kernel(body, out_shape, in_specs, scratch_shapes, flops):
        return pl.pallas_call(
            body,
            out_shape=out_shape,
            in_specs=in_specs,
            out_specs=jax.tree.map(lambda _: vmem, out_shape),
            scratch_shapes=scratch_shapes,
            compiler_params=pltpu.CompilerParams(vmem_limit_bytes=VMEM_LIMIT),
            cost_estimate=pl.CostEstimate(flops=flops, bytes_accessed=1 << 20, transcendentals=0),
            name=getattr(body, "func", body).__name__,
        )

    parts = [loads]
    for k in range(1, lon_count):
        parts.append(lax.ppermute(loads, "lon", [(i, (i + k) % lon_count) for i in range(lon_count)]))
    count = lon_count * blocks
    width = owners * per_owner // lon_count
    right, first, column, pick, put, order_rows, turns, basis = kernel(
        functools.partial(tables, lon_count, cycles, degrees, blocks, total),
        (
            jax.ShapeDtypeStruct((3 * LANES, 2 * width), jnp.bfloat16),
            jax.ShapeDtypeStruct((2, count, width), jnp.float32),
            jax.ShapeDtypeStruct((2 * cycles, LANES), jnp.float32),
            jax.ShapeDtypeStruct((2 * LANES, LANES), jnp.bfloat16),
            jax.ShapeDtypeStruct((4, LANES, degrees), jnp.bfloat16),
            jax.ShapeDtypeStruct((per_owner, LANES), jnp.int32),
            jax.ShapeDtypeStruct((2, 2, owners, blocks, per_owner), jnp.float32),
            jax.ShapeDtypeStruct((2, 2, LANES, owners * per_owner), jnp.bfloat16),
        ),
        [vmem, smem, smem],
        [],
        1 << 31,
    )(table, cycle_weight, cycle_order)
    folded = kernel(
        analyse_grid,
        jax.ShapeDtypeStruct((devices, 2 * cycles, LANES), jnp.bfloat16),
        [vmem] * (3 + lon_count),
        [
            pltpu.VMEM((count * 4 * cycles, LANES), jnp.float32),
            pltpu.VMEM((count * 4 * cycles, 2 * width), jnp.float32),
        ],
        1 << 31,
    )(right, first, column, *parts)
    arrived = lax.all_to_all(folded, everyone, split_axis=0, concat_axis=0, tiled=True)

    rows = jnp.transpose(legendre, (0, 2, 1)).reshape(per_owner * northern, degrees)
    values = kernel(
        functools.partial(spectral, lon_count, owners),
        jax.ShapeDtypeStruct((devices, 4 * cycles, per_owner), jnp.bfloat16),
        [vmem] * 6,
        [
            pltpu.VMEM((lon_count * LANES, 2 * LANES), jnp.float32),
            pltpu.VMEM((4, 2 * per_owner, degrees), jnp.bfloat16),
        ],
        1 << 32,
    )(pick, put, order_rows, arrived, rows, love)
    returned = lax.all_to_all(values, everyone, split_axis=0, concat_axis=0, tiled=True)

    own = kernel(
        functools.partial(add_degrees, lon_count),
        jax.ShapeDtypeStruct((owners, 4 * cycles, per_owner), jnp.float32),
        [vmem],
        [],
        1 << 28,
    )(returned)
    other = lax.ppermute(own, "lon", [(i, i ^ 1) for i in range(lon_count)])
    left = [pltpu.VMEM((2 * 4 * cycles * blocks, owners * per_owner), jnp.bfloat16)]
    grid = kernel(
        own_grid, jax.ShapeDtypeStruct((4 * cycles * blocks, LANES), jnp.float32), [vmem] * 3, left, 1 << 30
    )(turns, basis, own)
    return kernel(synthesise_grid, jax.ShapeDtypeStruct(loads.shape, jnp.float32), [vmem] * 4, left, 1 << 30)(
        turns, basis, other, grid
    )


def per_device(loads, legendre, love, cycle_weight, order_list, cycle_order):
    sizes = (lax.axis_size("band"), lax.axis_size("lon"), loads.shape[2], loads.shape[3], legendre.shape[0], legendre.shape[1])
    form = per_device_kernels if fits(*sizes) else per_device_plain
    return form(loads, legendre, love, cycle_weight, order_list, cycle_order)


def cycle_basis(order_ids, positions, total):
    phase = positions[:, None] * order_ids[None, :] % total
    angle = phase.astype(jnp.float32) * (2.0 * math.pi / total)
    scale = 1.0 / math.sqrt(total)
    return (jnp.cos(angle) * scale, jnp.sin(angle) * scale)


def per_device_plain(loads, legendre, love, cycle_weight, order_list, cycle_order):
    highest = lax.Precision.HIGHEST
    owners = lax.axis_size("band")
    lon_count = lax.axis_size("lon")
    band_index = lax.axis_index("band")
    lon_index = lax.axis_index("lon")
    cycle_pairs = loads.shape[2]
    points = loads.shape[3]
    total = points * lon_count
    orders = order_list.shape[0]
    per_owner = legendre.shape[0]
    degree_count = legendre.shape[1]
    northern = legendre.shape[2]
    quarter = per_owner // lon_count
    positions = lon_index * points + jnp.arange(points, dtype=jnp.int32)
    cosine, sine = cycle_basis(order_list, positions, total)
    my_cycles = lax.dynamic_slice_in_dim(cycle_order, band_index * cycle_pairs, cycle_pairs)
    picker = my_cycles[:, None] == jnp.arange(northern, dtype=jnp.int32)[None, :]
    weights = jnp.sum(jnp.where(picker, cycle_weight[None, :], 0.0), axis=1)
    forward = jnp.stack([cosine, -sine], axis=1)
    spectrum = jnp.einsum("fhjx,xrm->fhjrm", loads, forward, precision=highest)
    spectrum = spectrum.reshape(2, 2, cycle_pairs, 2, owners, per_owner)
    summed = lax.psum_scatter(spectrum, "lon", scatter_dimension=5, tiled=True)
    cycle_scale = weights[None, :, None, None, None]
    symmetric = ((summed[:, 0] + summed[:, 1]) * cycle_scale).astype(jnp.bfloat16)
    antisym = ((summed[:, 0] - summed[:, 1]) * cycle_scale).astype(jnp.bfloat16)
    folded = jnp.stack([symmetric, antisym], axis=1)
    slot_width = folded.shape[5]
    outgoing = jnp.transpose(folded, (4, 5, 0, 1, 3, 2)).reshape(owners, slot_width, 8, cycle_pairs)
    arrived = lax.all_to_all(outgoing, "band", split_axis=0, concat_axis=3, tiled=True).reshape(
        slot_width, 8, northern
    )
    columns = lax.all_gather(arrived, "lon", axis=0, tiled=True)
    inverse_rows = jnp.argsort(cycle_order)
    columns_sorted = jnp.take(columns, inverse_rows, axis=2)
    my_orders = lax.dynamic_slice_in_dim(order_list, band_index * per_owner, per_owner)
    degrees = lon_index * degree_count + jnp.arange(degree_count, dtype=jnp.int32)
    analysed = jnp.einsum(
        "olk,ock->ocl", legendre, columns_sorted, preferred_element_type=jnp.float32
    )
    analysed = analysed.reshape(per_owner, 2, 2, 2, degree_count)
    even = (degrees[None, :] - my_orders[:, None]) % 2 == 0
    valid = degrees[None, :] >= my_orders[:, None]
    selected = jnp.where(even[:, None, None, :], analysed[:, :, 0], analysed[:, :, 1])
    selected = selected * valid[:, None, None, :].astype(jnp.float32)
    response = jnp.einsum("gfl,ofrl->ogrl", love, selected, precision=highest).astype(jnp.bfloat16)
    even_part = jnp.where((even & valid)[:, None, None, :], response, jnp.zeros_like(response))
    odd_part = jnp.where((~even & valid)[:, None, None, :], response, jnp.zeros_like(response))
    stacked = jnp.stack([even_part, odd_part], axis=2).reshape(per_owner, 8, degree_count)
    partial_sorted = jnp.einsum(
        "olk,ocl->ock", legendre, stacked, preferred_element_type=jnp.float32
    )
    partial_value = jnp.take(partial_sorted, cycle_order, axis=2)
    reduced = lax.psum_scatter(partial_value, "lon", scatter_dimension=0, tiled=True)
    returned = lax.all_to_all(reduced, "band", split_axis=2, concat_axis=0, tiled=True)
    gathered = lax.all_gather(returned[None], "lon", axis=0, tiled=True).reshape(
        orders, 8, cycle_pairs
    )
    slot_ids = jnp.transpose(order_list.reshape(owners, lon_count, quarter), (1, 0, 2)).reshape(
        orders
    )
    cosine_back, sine_back = cycle_basis(slot_ids, positions, total)
    pieces = gathered.reshape(orders, 2, 2, 2, cycle_pairs)
    cycle_values = jnp.stack(
        [pieces[:, :, 0] + pieces[:, :, 1], pieces[:, :, 0] - pieces[:, :, 1]], axis=2
    )
    factor = jnp.where(slot_ids == 0, 1.0, 2.0).astype(jnp.float32)
    inverse = jnp.stack([cosine_back.T, -sine_back.T], axis=0)
    scaled = cycle_values * factor[:, None, None, None, None]
    return jnp.einsum("sghrp,rsx->ghpx", scaled, inverse, precision=highest)


def solution(mesh):
    return jax.shard_map(
        per_device,
        mesh=mesh,
        in_specs=(
            P(None, None, "band", "lon"),
            P("band", "lon", None),
            P(None, None, "lon"),
            P(),
            P(),
            P(),
        ),
        out_specs=P(None, None, "band", "lon"),
        check_vma=False,
    )
```

```python
import functools
import math

import jax
import jax.numpy as jnp
from jax import lax
from jax.experimental import pallas as pl
from jax.experimental.pallas import tpu as pltpu
from jax.sharding import PartitionSpec as P

LANES = 128
ROWS = 8
VMEM_LIMIT = 12 << 20
NT = (((1,), (1,)), ((), ()))


def iota(shape, axis):
    return lax.broadcasted_iota(jnp.int32, shape, axis)


def turn(phase, total):
    shift = (total // 4).bit_length() - 1
    quadrant = (phase + total // 8) >> shift
    x = (phase - (quadrant << shift)).astype(jnp.float32) * (2.0 * math.pi / total)
    z = x * x
    s = ((-1.9515295891e-4 * z + 8.3321608736e-3) * z - 1.6666654611e-1) * z * x + x
    c = ((2.443315711809948e-5 * z - 1.388731625493765e-3) * z + 4.166664568298827e-2) * z * z
    c = c - 0.5 * z + 1.0
    odd = (quadrant & 1) == 1
    cosine = jnp.where(odd, s, c)
    sine = jnp.where(odd, c, s)
    cosine = jnp.where(((quadrant + 1) & 2) == 2, -cosine, cosine)
    sine = jnp.where((quadrant & 2) == 2, -sine, sine)
    return cosine, sine


def split(x):
    high = x.astype(jnp.bfloat16)
    return high, (x - high.astype(jnp.float32)).astype(jnp.bfloat16)


def dot(a, b):
    return jnp.dot(a, b, preferred_element_type=jnp.float32)


def dot_nt(a, b):
    return lax.dot_general(a, b, NT, preferred_element_type=jnp.float32)


def analyse_grid(right_ref, turn_ref, weight_ref, *refs):
    parts, out_ref, points_ref, mid_ref = refs[:-3], refs[-3], refs[-2], refs[-1]
    cycles = parts[0].shape[2]
    blocks = parts[0].shape[3] // LANES
    count, width = turn_ref.shape[1:]
    owners = width // (LANES // 2)
    lon_count = out_ref.shape[0] // owners
    quarter = width // owners // 2
    pieces = LANES // quarter
    step = 2 * cycles

    for q, part in enumerate(parts):
        for a in range(blocks):
            for f in range(2):
                north = part[f, 0, :, a * LANES : (a + 1) * LANES]
                south = part[f, 1, :, a * LANES : (a + 1) * LANES]
                at = ((q * blocks + a) * 2 + f) * step
                points_ref[at : at + step] = jnp.concatenate([north + south, north - south], axis=0)
    high, low = split(points_ref[...])
    mid_ref[...] = dot(jnp.concatenate([high, low, high], axis=1), right_ref[...])

    sums = [[jnp.zeros((step, width), jnp.float32) for _ in range(2)] for _ in range(2)]
    for a in range(count):
        ca, sa = turn_ref[0, a : a + 1], turn_ref[1, a : a + 1]
        for f in range(2):
            at = (a * 2 + f) * step
            tc = mid_ref[at : at + step, :width]
            ts = mid_ref[at : at + step, width:]
            sums[f][0] = sums[f][0] + (ca * tc - sa * ts)
            sums[f][1] = sums[f][1] - (sa * tc + ca * ts)

    slot = iota((1, LANES), 1) // quarter
    weight = weight_ref[...]
    for owner in range(owners):
        for side in range(2):
            t, i = (2 * owner + side) // pieces, (2 * owner + side) % pieces
            block = None
            for e in range(4):
                piece = sums[e // 2][e % 2][:, t * LANES : (t + 1) * LANES]
                move = (e - i) * quarter % LANES
                piece = pltpu.roll(piece, move, 1) if move else piece
                block = piece if block is None else jnp.where(slot == e, piece, block)
            block = block * weight
            for q in range(side, lon_count, 2):
                out_ref[owner * lon_count + q] = block


def add_points(parts_ref, out_ref):
    sides, owners = out_ref.shape[:2]
    lon_count = parts_ref.shape[0] // owners
    for c in range(sides):
        for b in range(owners):
            value = parts_ref[b * lon_count + c]
            for q in range(c + sides, lon_count, sides):
                value = value + parts_ref[b * lon_count + q]
            out_ref[c, b] = value.astype(out_ref.dtype)


def order_tables(blocks, total, orders_ref, right_ref, first_ref, rows_ref, turn_ref, basis_ref):
    owners, per_owner = orders_ref.shape
    share = per_owner // 2
    band, lon = lax.axis_index("band"), lax.axis_index("lon")
    side = lon % 2
    lane = iota((1, LANES), 1)
    first_lanes = lane < share

    mine = pltpu.roll(orders_ref[...], (LANES - share * side) % LANES, 1)
    moved = pltpu.roll(mine, share, 1)
    orders = jnp.concatenate(
        [jnp.where(first_lanes, mine[b : b + 1], moved[b + 1 : b + 2]) for b in range(0, owners, 2)], axis=1
    )
    width = orders.shape[1]
    for c, table in enumerate(turn((iota((LANES, width), 0) * orders) & (total - 1), total)):
        high, low = split(table)
        for k, value in enumerate((high, high, low)):
            right_ref[k * LANES : (k + 1) * LANES, c * width : (c + 1) * width] = value
    for k in range(2):
        origin = lon if k == 0 else lon + 1 - 2 * side
        step = iota((blocks, width), 0) + origin * blocks
        for c, table in enumerate(turn((step * LANES * orders) & (total - 1), total)):
            first_ref[c, k * blocks : (k + 1) * blocks] = table

    own = orders_ref[pl.ds(band, 1), :].astype(jnp.float32)
    rows_ref[...] = jnp.transpose(jnp.broadcast_to(own, (LANES, per_owner))).astype(jnp.int32)

    quarter = per_owner // 4
    slot = lane // quarter
    arranged = orders_ref[...]
    ahead, behind = pltpu.roll(arranged, LANES - quarter, 1), pltpu.roll(arranged, quarter, 1)
    arranged = jnp.where(slot == 1, ahead, jnp.where(slot == 2, behind, arranged))

    def halves(x, y):
        return jnp.where(first_lanes, x, pltpu.roll(y, share, 1)), jnp.where(first_lanes, pltpu.roll(x, share, 1), y)

    scale = 1.0 / math.sqrt(total)
    for b in range(owners):
        order = arranged[b : b + 1]
        factor = jnp.where(order == 0, scale, 2.0 * scale)
        step = iota((blocks, per_owner), 0) + lon * blocks
        cos_a, sin_a = turn((step * LANES * order) & (total - 1), total)
        cos_a, sin_a = cos_a * factor, sin_a * factor
        for half, table in enumerate(halves(cos_a, -cos_a)):
            turn_ref[half, 0, b] = table
        for half, table in enumerate(halves(-sin_a, -sin_a)):
            turn_ref[half, 1, b] = table
        cos_b, sin_b = turn((iota((LANES, per_owner), 0) * order) & (total - 1), total)
        for half, table in enumerate(halves(cos_b, sin_b)):
            high, low = split(table)
            basis_ref[half, 0, :, b * per_owner : (b + 1) * per_owner] = high
            basis_ref[half, 1, :, b * per_owner : (b + 1) * per_owner] = low


def cycle_tables(owners, cycles, degrees, total, weight_ref, cycle_ref, column_ref, pick_ref, put_ref):
    northern = owners * cycles
    wide = degrees // northern * northern
    band = lax.axis_index("band")
    lane = iota((1, LANES), 1)
    sub = iota((2 * cycles, LANES), 0) % cycles
    weight = jnp.zeros((2 * cycles, LANES), jnp.float32)
    for j in range(cycles):
        weight = jnp.where(sub == j, weight_ref[cycle_ref[band * cycles + j]], weight)
    column_ref[...] = weight * (1.0 / math.sqrt(total))

    def cycle_lanes(repeat):
        place = (lane // (repeat * cycles)) * cycles + lane % cycles
        row = jnp.full((1, LANES), -1, jnp.int32)
        for i in range(northern):
            row = jnp.where(place == i, cycle_ref[i], row)
        return row

    parity_lane = (lane // cycles) % 2
    found = iota((northern, LANES), 0) == cycle_lanes(2)
    for p in range(2):
        one = jnp.where(found & (parity_lane == p), 1.0, 0.0)
        copies = jnp.concatenate([one] * (LANES // northern), axis=0)
        pick_ref[p * LANES : (p + 1) * LANES] = copies.astype(jnp.bfloat16)

    leaving = cycle_lanes(4).astype(jnp.float32)
    cycle_rows = jnp.transpose(jnp.broadcast_to(leaving, (LANES, LANES))).astype(jnp.int32)
    found = cycle_rows == iota((LANES, LANES), 1) % northern
    part = (iota((LANES, LANES), 0) // cycles) % 4
    for i in range(4):
        put = jnp.where(found & (part == i), 1.0, 0.0)
        put_ref[i] = jnp.concatenate([put] * (wide // LANES), axis=1).astype(jnp.bfloat16)


def spectral_half(side, pick_ref, put_ref, rows_ref, folded_ref, legendre_ref, love_ref, spread_ref, kept_ref):
    parts, owners, height = folded_ref.shape[:3]
    quarter = rows_ref.shape[0] // 4
    degrees = legendre_ref.shape[1]
    northern = owners * height // 2
    group = degrees // northern
    wide = group * northern
    lon = lax.axis_index("lon")

    pad = jnp.zeros((LANES - 2 * northern, LANES), jnp.float32)
    turned = []
    for q in range(parts):
        pieces = [folded_ref[q, b].astype(jnp.float32) for b in range(owners)]
        turned.append(jnp.transpose(jnp.concatenate(pieces + [pad], axis=0)))
    spread_ref[...] = dot_nt(jnp.concatenate(turned, axis=0).astype(jnp.bfloat16), pick_ref[...])

    degree = lon * degrees + iota((ROWS, degrees), 1)
    diagonal = iota((ROWS, wide), 0) == iota((ROWS, wide), 1) // northern
    love = [[love_ref[g, f : f + 1, :] for f in range(2)] for g in range(2)]
    groups = parts * quarter // group

    def place(n):
        q, first = n * group // quarter, n * group % quarter
        return q, first, (2 * q + side) * quarter + first

    def table(n):
        start = pl.multiple_of(place(n)[2] * northern, wide)
        return legendre_ref[pl.ds(start, wide)]

    def analyse(n):
        q, first, _ = place(n)
        left = []
        for f in range(2):
            for p in range(2):
                for c in range(2):
                    at = q * LANES + (f * 2 + c) * quarter + first
                    piece = spread_ref[at : at + group, p * LANES : (p + 1) * LANES]
                    left.append(jnp.where(diagonal, jnp.concatenate([piece] * (wide // LANES), axis=1), 0.0))
        return dot(jnp.concatenate(left, axis=0).astype(jnp.bfloat16), table(n))

    def respond(n, analysed):
        order = rows_ref[pl.ds(pl.multiple_of(place(n)[2], group), group)]
        gap = degree - jnp.concatenate([order] * (degrees // LANES), axis=1)
        valid = gap >= 0
        keep = [valid & ((gap & 1) == p) for p in range(2)]
        mixed = []
        for g in range(2):
            for p in range(2):
                for c in range(2):
                    lo = (p * 2 + c) * group
                    hi = ((2 + p) * 2 + c) * group
                    value = love[g][0] * analysed[lo : lo + group] + love[g][1] * analysed[hi : hi + group]
                    mixed.append(jnp.where(keep[p], value, 0.0))
        return dot_nt(jnp.concatenate(mixed, axis=0).astype(jnp.bfloat16), table(n))

    def keep_pair(n, halves):
        for g in range(2):
            for c in range(2):
                lo, hi = (g * 4 + c) * group, (g * 4 + 2 + c) * group
                rows = [(half[lo : lo + group], half[hi : hi + group]) for half in halves]
                at = c * parts * quarter + n * group
                for h in range(2):
                    both = [even + odd if h == 0 else even - odd for even, odd in rows]
                    both = [jnp.where(diagonal, value, 0.0) for value in both]
                    kept_ref[g * 2 + h, at : at + 2 * group, :] = jnp.concatenate(both, axis=0).astype(jnp.bfloat16)

    analysed, partial = {}, {}
    for n in range(groups + 2):
        if n < groups:
            analysed[n] = analyse(n)
        if 1 <= n <= groups:
            partial[n - 1] = respond(n - 1, analysed.pop(n - 1))
        if n >= 3 and n % 2 == 1:
            keep_pair(n - 3, [partial.pop(n - 3), partial.pop(n - 2)])

    total = None
    for i in range(4):
        term = dot_nt(put_ref[i], kept_ref[i])
        total = term if total is None else total + term
    return total.astype(jnp.bfloat16)


def own_spectral(pick_ref, put_ref, rows_ref, folded_ref, legendre_ref, love_ref, out_ref, spread_ref, kept_ref):
    side = lax.axis_index("lon") % 2
    out_ref[...] = spectral_half(
        side, pick_ref, put_ref, rows_ref, folded_ref, legendre_ref, love_ref, spread_ref, kept_ref
    )


def spectral(pick_ref, put_ref, rows_ref, folded_ref, legendre_ref, love_ref, own_ref, out_ref, spread_ref, kept_ref):
    side = lax.axis_index("lon") % 2
    other = spectral_half(
        1 - side, pick_ref, put_ref, rows_ref, folded_ref, legendre_ref, love_ref, spread_ref, kept_ref
    )
    owners = folded_ref.shape[1]
    lon_count = out_ref.shape[0] // owners
    height = out_ref.shape[1]
    for b in range(owners):
        for q in range(0, lon_count, 2):
            out_ref[b * lon_count + q + side] = own_ref[b * height : (b + 1) * height]
            out_ref[b * lon_count + q + 1 - side] = other[b * height : (b + 1) * height]


def add_degrees(lon_count, values_ref, out_ref):
    for b in range(out_ref.shape[0]):
        value = values_ref[b * lon_count].astype(jnp.float32)
        for q in range(1, lon_count):
            value = value + values_ref[b * lon_count + q].astype(jnp.float32)
        out_ref[b] = value


def half_grid(which, turn_ref, basis_ref, value_ref, left_ref):
    owners, rows, lanes = value_ref.shape
    blocks = turn_ref.shape[3]
    height = blocks * rows
    for b in range(owners):
        value = value_ref[b]
        other = pltpu.roll(value, lanes // 2, 1)
        for a in range(blocks):
            term = value * turn_ref[which, 0, b, a : a + 1] + other * turn_ref[which, 1, b, a : a + 1]
            high, low = split(term)
            left_ref[a * rows : (a + 1) * rows, b * lanes : (b + 1) * lanes] = high
            left_ref[height + a * rows : height + (a + 1) * rows, b * lanes : (b + 1) * lanes] = low
    grid = dot_nt(left_ref[...], basis_ref[which, 0])
    return grid[:height] + grid[height:] + dot_nt(left_ref[:height], basis_ref[which, 1])


def own_grid(turn_ref, basis_ref, value_ref, out_ref, left_ref):
    out_ref[...] = half_grid(lax.axis_index("lon") % 2, turn_ref, basis_ref, value_ref, left_ref)


def synthesise_grid(turn_ref, basis_ref, value_ref, grid_ref, out_ref, left_ref):
    rows = value_ref.shape[1]
    cycles = out_ref.shape[2]
    grid = grid_ref[...] + half_grid(1 - lax.axis_index("lon") % 2, turn_ref, basis_ref, value_ref, left_ref)
    for a in range(grid.shape[0] // rows):
        for g in range(2):
            for h in range(2):
                at = a * rows + (g * 2 + h) * cycles
                out_ref[g, h, :, a * LANES : (a + 1) * LANES] = grid[at : at + cycles]


def fits(owners, lon_count, cycles, points, per_owner, degrees):
    northern = owners * cycles
    total = points * lon_count
    return (
        per_owner == LANES
        and 4 * per_owner == lon_count * LANES
        and lon_count % 2 == 0
        and 2 * cycles == ROWS
        and 4 * northern == LANES
        and ROWS * northern == degrees
        and degrees % LANES == 0
        and owners == ROWS
        and points % LANES == 0
        and total & (total - 1) == 0
        and owners * per_owner * LANES < 1 << 24
    )


def per_device_kernels(loads, legendre, love, cycle_weight, order_list, cycle_order):
    owners = lax.axis_size("band")
    lon_count = lax.axis_size("lon")
    cycles, points = loads.shape[2], loads.shape[3]
    per_owner, degrees, northern = legendre.shape
    total = points * lon_count
    devices = owners * lon_count
    blocks = points // LANES
    everyone = ("band", "lon")
    vmem = pl.BlockSpec(memory_space=pltpu.VMEM)
    smem = pl.BlockSpec(memory_space=pltpu.SMEM)
    table = order_list.reshape(owners, per_owner)

    def kernel(body, out_shape, in_specs, scratch_shapes, flops):
        return pl.pallas_call(
            body,
            out_shape=out_shape,
            in_specs=in_specs,
            out_specs=jax.tree.map(lambda _: vmem, out_shape),
            scratch_shapes=scratch_shapes,
            compiler_params=pltpu.CompilerParams(vmem_limit_bytes=VMEM_LIMIT),
            cost_estimate=pl.CostEstimate(flops=flops, bytes_accessed=1 << 20, transcendentals=0),
            name=getattr(body, "func", body).__name__,
        )

    partner = [(i, i ^ 1) for i in range(lon_count)]
    parts = [loads, lax.ppermute(loads, "lon", partner)]
    count = 2 * blocks
    width = owners * per_owner // 2
    right, first, order_rows, turns, basis = kernel(
        functools.partial(order_tables, blocks, total),
        (
            jax.ShapeDtypeStruct((3 * LANES, 2 * width), jnp.bfloat16),
            jax.ShapeDtypeStruct((2, count, width), jnp.float32),
            jax.ShapeDtypeStruct((per_owner, LANES), jnp.int32),
            jax.ShapeDtypeStruct((2, 2, owners, blocks, per_owner), jnp.float32),
            jax.ShapeDtypeStruct((2, 2, LANES, owners * per_owner), jnp.bfloat16),
        ),
        [vmem],
        [],
        1 << 31,
    )(table)
    column, pick, put = kernel(
        functools.partial(cycle_tables, owners, cycles, degrees, total),
        (
            jax.ShapeDtypeStruct((2 * cycles, LANES), jnp.float32),
            jax.ShapeDtypeStruct((2 * LANES, LANES), jnp.bfloat16),
            jax.ShapeDtypeStruct((4, LANES, degrees), jnp.bfloat16),
        ),
        [smem, smem],
        [],
        1 << 30,
    )(cycle_weight, cycle_order)
    sums = kernel(
        analyse_grid,
        jax.ShapeDtypeStruct((devices, 2 * cycles, LANES), jnp.float32),
        [vmem] * (3 + len(parts)),
        [
            pltpu.VMEM((count * 4 * cycles, LANES), jnp.float32),
            pltpu.VMEM((count * 4 * cycles, 2 * width), jnp.float32),
        ],
        1 << 31,
    )(right, first, column, *parts)
    arrived = lax.all_to_all(sums, everyone, split_axis=0, concat_axis=0, tiled=True)
    folded = kernel(
        add_points,
        jax.ShapeDtypeStruct((2, owners, 2 * cycles, LANES), jnp.bfloat16),
        [vmem],
        [],
        1 << 28,
    )(arrived)
    others = lax.ppermute(folded, "lon", partner)

    rows = jnp.transpose(legendre, (0, 2, 1)).reshape(per_owner * northern, degrees)
    scratch = [
        pltpu.VMEM((2 * LANES, 2 * LANES), jnp.float32),
        pltpu.VMEM((4, per_owner, degrees), jnp.bfloat16),
    ]
    height = owners * 4 * cycles
    mine = kernel(own_spectral, jax.ShapeDtypeStruct((height, per_owner), jnp.bfloat16), [vmem] * 6, scratch, 1 << 31)(
        pick, put, order_rows, folded, rows, love
    )
    values = kernel(
        spectral, jax.ShapeDtypeStruct((devices, 4 * cycles, per_owner), jnp.bfloat16), [vmem] * 7, scratch, 1 << 31
    )(pick, put, order_rows, others, rows, love, mine)
    returned = lax.all_to_all(values, everyone, split_axis=0, concat_axis=0, tiled=True)

    own = kernel(
        functools.partial(add_degrees, lon_count),
        jax.ShapeDtypeStruct((owners, 4 * cycles, per_owner), jnp.float32),
        [vmem],
        [],
        1 << 28,
    )(returned)
    other = lax.ppermute(own, "lon", partner)
    left = [pltpu.VMEM((2 * 4 * cycles * blocks, owners * per_owner), jnp.bfloat16)]
    grid = kernel(
        own_grid, jax.ShapeDtypeStruct((4 * cycles * blocks, LANES), jnp.float32), [vmem] * 3, left, 1 << 30
    )(turns, basis, own)
    return kernel(synthesise_grid, jax.ShapeDtypeStruct(loads.shape, jnp.float32), [vmem] * 4, left, 1 << 30)(
        turns, basis, other, grid
    )


def per_device(loads, legendre, love, cycle_weight, order_list, cycle_order):
    sizes = (lax.axis_size("band"), lax.axis_size("lon"), loads.shape[2], loads.shape[3], legendre.shape[0], legendre.shape[1])
    form = per_device_kernels if fits(*sizes) else per_device_plain
    return form(loads, legendre, love, cycle_weight, order_list, cycle_order)


def cycle_basis(order_ids, positions, total):
    phase = positions[:, None] * order_ids[None, :] % total
    angle = phase.astype(jnp.float32) * (2.0 * math.pi / total)
    scale = 1.0 / math.sqrt(total)
    return (jnp.cos(angle) * scale, jnp.sin(angle) * scale)


def per_device_plain(loads, legendre, love, cycle_weight, order_list, cycle_order):
    highest = lax.Precision.HIGHEST
    owners = lax.axis_size("band")
    lon_count = lax.axis_size("lon")
    band_index = lax.axis_index("band")
    lon_index = lax.axis_index("lon")
    cycle_pairs = loads.shape[2]
    points = loads.shape[3]
    total = points * lon_count
    orders = order_list.shape[0]
    per_owner = legendre.shape[0]
    degree_count = legendre.shape[1]
    northern = legendre.shape[2]
    quarter = per_owner // lon_count
    positions = lon_index * points + jnp.arange(points, dtype=jnp.int32)
    cosine, sine = cycle_basis(order_list, positions, total)
    my_cycles = lax.dynamic_slice_in_dim(cycle_order, band_index * cycle_pairs, cycle_pairs)
    picker = my_cycles[:, None] == jnp.arange(northern, dtype=jnp.int32)[None, :]
    weights = jnp.sum(jnp.where(picker, cycle_weight[None, :], 0.0), axis=1)
    forward = jnp.stack([cosine, -sine], axis=1)
    spectrum = jnp.einsum("fhjx,xrm->fhjrm", loads, forward, precision=highest)
    spectrum = spectrum.reshape(2, 2, cycle_pairs, 2, owners, per_owner)
    summed = lax.psum_scatter(spectrum, "lon", scatter_dimension=5, tiled=True)
    cycle_scale = weights[None, :, None, None, None]
    symmetric = ((summed[:, 0] + summed[:, 1]) * cycle_scale).astype(jnp.bfloat16)
    antisym = ((summed[:, 0] - summed[:, 1]) * cycle_scale).astype(jnp.bfloat16)
    folded = jnp.stack([symmetric, antisym], axis=1)
    slot_width = folded.shape[5]
    outgoing = jnp.transpose(folded, (4, 5, 0, 1, 3, 2)).reshape(owners, slot_width, 8, cycle_pairs)
    arrived = lax.all_to_all(outgoing, "band", split_axis=0, concat_axis=3, tiled=True).reshape(
        slot_width, 8, northern
    )
    columns = lax.all_gather(arrived, "lon", axis=0, tiled=True)
    inverse_rows = jnp.argsort(cycle_order)
    columns_sorted = jnp.take(columns, inverse_rows, axis=2)
    my_orders = lax.dynamic_slice_in_dim(order_list, band_index * per_owner, per_owner)
    degrees = lon_index * degree_count + jnp.arange(degree_count, dtype=jnp.int32)
    analysed = jnp.einsum(
        "olk,ock->ocl", legendre, columns_sorted, preferred_element_type=jnp.float32
    )
    analysed = analysed.reshape(per_owner, 2, 2, 2, degree_count)
    even = (degrees[None, :] - my_orders[:, None]) % 2 == 0
    valid = degrees[None, :] >= my_orders[:, None]
    selected = jnp.where(even[:, None, None, :], analysed[:, :, 0], analysed[:, :, 1])
    selected = selected * valid[:, None, None, :].astype(jnp.float32)
    response = jnp.einsum("gfl,ofrl->ogrl", love, selected, precision=highest).astype(jnp.bfloat16)
    even_part = jnp.where((even & valid)[:, None, None, :], response, jnp.zeros_like(response))
    odd_part = jnp.where((~even & valid)[:, None, None, :], response, jnp.zeros_like(response))
    stacked = jnp.stack([even_part, odd_part], axis=2).reshape(per_owner, 8, degree_count)
    partial_sorted = jnp.einsum(
        "olk,ocl->ock", legendre, stacked, preferred_element_type=jnp.float32
    )
    partial_value = jnp.take(partial_sorted, cycle_order, axis=2)
    reduced = lax.psum_scatter(partial_value, "lon", scatter_dimension=0, tiled=True)
    returned = lax.all_to_all(reduced, "band", split_axis=2, concat_axis=0, tiled=True)
    gathered = lax.all_gather(returned[None], "lon", axis=0, tiled=True).reshape(
        orders, 8, cycle_pairs
    )
    slot_ids = jnp.transpose(order_list.reshape(owners, lon_count, quarter), (1, 0, 2)).reshape(
        orders
    )
    cosine_back, sine_back = cycle_basis(slot_ids, positions, total)
    pieces = gathered.reshape(orders, 2, 2, 2, cycle_pairs)
    cycle_values = jnp.stack(
        [pieces[:, :, 0] + pieces[:, :, 1], pieces[:, :, 0] - pieces[:, :, 1]], axis=2
    )
    factor = jnp.where(slot_ids == 0, 1.0, 2.0).astype(jnp.float32)
    inverse = jnp.stack([cosine_back.T, -sine_back.T], axis=0)
    scaled = cycle_values * factor[:, None, None, None, None]
    return jnp.einsum("sghrp,rsx->ghpx", scaled, inverse, precision=highest)


def solution(mesh):
    return jax.shard_map(
        per_device,
        mesh=mesh,
        in_specs=(
            P(None, None, "band", "lon"),
            P("band", "lon", None),
            P(None, None, "lon"),
            P(),
            P(),
            P(),
        ),
        out_specs=P(None, None, "band", "lon"),
        check_vma=False,
    )
```

```python
import functools
import math

import jax
import jax.numpy as jnp
from jax import lax
from jax.experimental import pallas as pl
from jax.experimental.pallas import tpu as pltpu
from jax.sharding import PartitionSpec as P

LANES = 128
ROWS = 8
VMEM_LIMIT = 12 << 20
NT = (((1,), (1,)), ((), ()))


def iota(shape, axis):
    return lax.broadcasted_iota(jnp.int32, shape, axis)


def turn(phase, total):
    shift = (total // 4).bit_length() - 1
    quadrant = (phase + total // 8) >> shift
    x = (phase - (quadrant << shift)).astype(jnp.float32) * (2.0 * math.pi / total)
    z = x * x
    s = ((-1.9515295891e-4 * z + 8.3321608736e-3) * z - 1.6666654611e-1) * z * x + x
    c = ((2.443315711809948e-5 * z - 1.388731625493765e-3) * z + 4.166664568298827e-2) * z * z
    c = c - 0.5 * z + 1.0
    odd = (quadrant & 1) == 1
    cosine = jnp.where(odd, s, c)
    sine = jnp.where(odd, c, s)
    cosine = jnp.where(((quadrant + 1) & 2) == 2, -cosine, cosine)
    sine = jnp.where((quadrant & 2) == 2, -sine, sine)
    return cosine, sine


def split(x):
    high = x.astype(jnp.bfloat16)
    return high, (x - high.astype(jnp.float32)).astype(jnp.bfloat16)


def dot(a, b):
    return jnp.dot(a, b, preferred_element_type=jnp.float32)


def dot_nt(a, b):
    return lax.dot_general(a, b, NT, preferred_element_type=jnp.float32)


def analyse_grid(total, right_ref, turn_ref, weight_ref, cycle_ref, *refs):
    parts, out_ref, points_ref, mid_ref = refs[:-3], refs[-3], refs[-2], refs[-1]
    cycles = parts[0].shape[2]
    blocks = parts[0].shape[3] // LANES
    count, width = turn_ref.shape[1:]
    owners = width // (LANES // 2)
    lon_count = out_ref.shape[0] // owners
    quarter = width // owners // 2
    pieces = LANES // quarter
    step = 2 * cycles

    for q, part in enumerate(parts):
        for a in range(blocks):
            for f in range(2):
                north = part[f, 0, :, a * LANES : (a + 1) * LANES]
                south = part[f, 1, :, a * LANES : (a + 1) * LANES]
                at = ((q * blocks + a) * 2 + f) * step
                points_ref[at : at + step] = jnp.concatenate([north + south, north - south], axis=0)
    high, low = split(points_ref[...])
    mid_ref[...] = dot(jnp.concatenate([high, low, high], axis=1), right_ref[...])

    sums = [[jnp.zeros((step, width), jnp.float32) for _ in range(2)] for _ in range(2)]
    for a in range(count):
        ca, sa = turn_ref[0, a : a + 1], turn_ref[1, a : a + 1]
        for f in range(2):
            at = (a * 2 + f) * step
            tc = mid_ref[at : at + step, :width]
            ts = mid_ref[at : at + step, width:]
            sums[f][0] = sums[f][0] + (ca * tc - sa * ts)
            sums[f][1] = sums[f][1] - (sa * tc + ca * ts)

    slot = iota((1, LANES), 1) // quarter
    northern = cycle_ref.shape[1]
    lane = iota((step, northern), 1)
    row = lax.axis_index("band") * cycles + iota((step, northern), 0) % cycles
    listed = jnp.sum(jnp.where(lane == row, cycle_ref[...].astype(jnp.float32), 0.0), axis=1, keepdims=True)
    weight = jnp.sum(jnp.where(lane == listed.astype(jnp.int32), weight_ref[...], 0.0), axis=1, keepdims=True)
    weight = weight * (1.0 / math.sqrt(total))
    for owner in range(owners):
        for side in range(2):
            t, i = (2 * owner + side) // pieces, (2 * owner + side) % pieces
            block = None
            for e in range(4):
                piece = sums[e // 2][e % 2][:, t * LANES : (t + 1) * LANES]
                move = (e - i) * quarter % LANES
                piece = pltpu.roll(piece, move, 1) if move else piece
                block = piece if block is None else jnp.where(slot == e, piece, block)
            block = block * weight
            for q in range(side, lon_count, 2):
                out_ref[owner * lon_count + q] = block


def add_points(parts_ref, out_ref):
    sides, owners = out_ref.shape[:2]
    lon_count = parts_ref.shape[0] // owners
    for c in range(sides):
        for b in range(owners):
            value = parts_ref[b * lon_count + c]
            for q in range(c + sides, lon_count, sides):
                value = value + parts_ref[b * lon_count + q]
            out_ref[c, b] = value.astype(out_ref.dtype)


def products(fine, coarse):
    for k in range(coarse[0].shape[0]):
        cc, cs = coarse[0][k : k + 1], coarse[1][k : k + 1]
        yield fine[0] * cc - fine[1] * cs, fine[1] * cc + fine[0] * cs


def forward_tables(blocks, total, orders_ref, right_ref, first_ref):
    owners, per_owner = orders_ref.shape
    share = per_owner // 2
    lon = lax.axis_index("lon")
    side = lon % 2
    first_lanes = iota((1, LANES), 1) < share

    mine = pltpu.roll(orders_ref[...], (LANES - share * side) % LANES, 1)
    moved = pltpu.roll(mine, share, 1)
    orders = jnp.concatenate(
        [jnp.where(first_lanes, mine[b : b + 1], moved[b + 1 : b + 2]) for b in range(0, owners, 2)], axis=1
    )
    width = orders.shape[1]
    fine = turn(iota((ROWS, width), 0) * orders, total)
    coarse = turn((iota((LANES // ROWS, width), 0) * ROWS * orders) & (total - 1), total)
    kept = []
    for k, pair in enumerate(products(fine, coarse)):
        kept.append([split(table) for table in pair])
        if k % 2 == 0:
            continue
        for c in range(2):
            high, low = [jnp.concatenate([kept[k - 1][c][i], kept[k][c][i]], axis=0) for i in range(2)]
            for i, value in enumerate((high, high, low)):
                at = i * LANES + (k - 1) * ROWS
                right_ref[at : at + 2 * ROWS, c * width : (c + 1) * width] = value
    for k in range(2):
        origin = lon if k == 0 else lon + 1 - 2 * side
        step = iota((blocks, width), 0) + origin * blocks
        for c, table in enumerate(turn((step * LANES * orders) & (total - 1), total)):
            first_ref[c, k * blocks : (k + 1) * blocks] = table


def later_tables(cycles, blocks, total, orders_ref, cycle_ref, after_ref, pick_ref, put_ref, rows_ref, turn_ref, basis_ref):
    del after_ref
    owners, per_owner = orders_ref.shape
    northern = owners * cycles
    wide = put_ref.shape[2]
    share = per_owner // 2
    band, lon = lax.axis_index("band"), lax.axis_index("lon")
    lane = iota((1, LANES), 1)
    first_lanes = lane < share

    listed = jnp.broadcast_to(cycle_ref[...].astype(jnp.float32), (LANES, northern)).astype(jnp.bfloat16)
    index = iota((LANES, northern), 0)

    def places(repeat):
        place = index // (repeat * cycles) * cycles + index % cycles
        return jnp.where(place == iota((LANES, northern), 1), 1.0, 0.0).astype(jnp.bfloat16)

    arriving = dot_nt(listed[: 2 * ROWS], places(2))[:1].astype(jnp.int32)
    found = (iota((northern, LANES), 0) == arriving) & (lane < 2 * northern)
    for p in range(2):
        one = jnp.where(found & (lane // cycles % 2 == p), 1.0, 0.0)
        copies = jnp.concatenate([one] * (LANES // northern), axis=0)
        pick_ref[p * LANES : (p + 1) * LANES] = copies.astype(jnp.bfloat16)
    leaving = dot_nt(places(4), listed).astype(jnp.int32)
    found = leaving == iota((LANES, LANES), 1) % northern
    part = iota((LANES, LANES), 0) // cycles % 4
    for i in range(4):
        put = jnp.where(found & (part == i), 1.0, 0.0)
        put_ref[i] = jnp.concatenate([put] * (wide // LANES), axis=1).astype(jnp.bfloat16)

    own = orders_ref[pl.ds(band, 1), :].astype(jnp.float32)
    rows_ref[...] = jnp.transpose(jnp.broadcast_to(own, (LANES, per_owner))).astype(jnp.int32)

    quarter = per_owner // 4
    slot = lane // quarter
    arranged = orders_ref[...]
    ahead, behind = pltpu.roll(arranged, LANES - quarter, 1), pltpu.roll(arranged, quarter, 1)
    arranged = jnp.where(slot == 1, ahead, jnp.where(slot == 2, behind, arranged))
    swapped = pltpu.roll(arranged, share, 1)
    doubled = [jnp.where(first_lanes, arranged, swapped), jnp.where(first_lanes, swapped, arranged)]

    scale = 1.0 / math.sqrt(total)
    for half in range(2):
        for b in range(owners):
            order = doubled[half][b : b + 1]
            factor = jnp.where(order == 0, scale, 2.0 * scale)
            step = iota((blocks, per_owner), 0) + lon * blocks
            cos_a, sin_a = turn((step * LANES * order) & (total - 1), total)
            turn_ref[half, 0, b] = jnp.where(first_lanes, cos_a, -cos_a) * factor
            turn_ref[half, 1, b] = -sin_a * factor
            back = jnp.where(first_lanes, 0, total - total // 4)
            fine = turn((iota((ROWS, per_owner), 0) * order + back) & (total - 1), total)
            coarse = turn((iota((LANES // ROWS, per_owner), 0) * ROWS * order) & (total - 1), total)
            kept = []
            for k in range(LANES // ROWS):
                value = fine[0] * coarse[0][k : k + 1] - fine[1] * coarse[1][k : k + 1]
                kept.append(split(value))
                if k % 2 == 1:
                    for i in range(2):
                        basis_ref[
                            half, i, (k - 1) * ROWS : (k + 1) * ROWS, b * per_owner : (b + 1) * per_owner
                        ] = jnp.concatenate([kept[k - 1][i], kept[k][i]], axis=0)


def spectral(
    pick_ref, put_ref, rows_ref, own_ref, other_ref, legendre_ref, love_ref, out_ref, spread_ref, kept_ref
):
    parts, owners, height = own_ref.shape[:3]
    quarter = rows_ref.shape[0] // (2 * parts)
    degrees = legendre_ref.shape[1]
    northern = owners * height // 2
    group = degrees // northern
    wide = group * northern
    lon = lax.axis_index("lon")
    side = lon % 2

    pad = jnp.zeros((LANES - 2 * northern, LANES), jnp.float32)
    turned = []
    for folded_ref in (own_ref, other_ref):
        for q in range(parts):
            pieces = [folded_ref[q, b].astype(jnp.float32) for b in range(owners)]
            turned.append(jnp.transpose(jnp.concatenate(pieces + [pad], axis=0)))
    spread_ref[...] = dot_nt(jnp.concatenate(turned, axis=0).astype(jnp.bfloat16), pick_ref[...])

    degree = lon * degrees + iota((ROWS, degrees), 1)
    diagonal = iota((ROWS, wide), 0) == iota((ROWS, wide), 1) // northern
    love = [[love_ref[g, f : f + 1, :] for f in range(2)] for g in range(2)]
    groups = 2 * parts * quarter // group

    def place(n):
        q, first = n * group // quarter, n * group % quarter
        taken = side if q < parts else 1 - side
        return q, first, (2 * (q % parts) + taken) * quarter + first

    def table(n):
        start = pl.multiple_of(place(n)[2] * northern, wide)
        return legendre_ref[pl.ds(start, wide)]

    def analyse(n):
        q, first, _ = place(n)
        left = []
        for f in range(2):
            for p in range(2):
                for c in range(2):
                    at = q * LANES + (f * 2 + c) * quarter + first
                    piece = spread_ref[at : at + group, p * LANES : (p + 1) * LANES]
                    left.append(jnp.where(diagonal, jnp.concatenate([piece] * (wide // LANES), axis=1), 0.0))
        return dot(jnp.concatenate(left, axis=0).astype(jnp.bfloat16), table(n))

    def respond(n, analysed):
        order = rows_ref[pl.ds(pl.multiple_of(place(n)[2], group), group)]
        gap = degree - jnp.concatenate([order] * (degrees // LANES), axis=1)
        valid = gap >= 0
        keep = [valid & ((gap & 1) == p) for p in range(2)]
        mixed = []
        for g in range(2):
            for p in range(2):
                for c in range(2):
                    lo = (p * 2 + c) * group
                    hi = ((2 + p) * 2 + c) * group
                    value = love[g][0] * analysed[lo : lo + group] + love[g][1] * analysed[hi : hi + group]
                    mixed.append(jnp.where(keep[p], value, 0.0))
        return dot_nt(jnp.concatenate(mixed, axis=0).astype(jnp.bfloat16), table(n))

    def keep_pair(n, halves):
        for g in range(2):
            for c in range(2):
                lo, hi = (g * 4 + c) * group, (g * 4 + 2 + c) * group
                rows = [(half[lo : lo + group], half[hi : hi + group]) for half in halves]
                share = parts * quarter
                at = (n * group // share * 2 + c) * share + n * group % share
                for h in range(2):
                    both = [even + odd if h == 0 else even - odd for even, odd in rows]
                    both = [jnp.where(diagonal, value, 0.0) for value in both]
                    kept_ref[g * 2 + h, at : at + 2 * group, :] = jnp.concatenate(both, axis=0).astype(jnp.bfloat16)

    analysed, partial = {}, {}
    for n in range(groups + 2):
        if n < groups:
            analysed[n] = analyse(n)
        if 1 <= n <= groups:
            partial[n - 1] = respond(n - 1, analysed.pop(n - 1))
        if n >= 3 and n % 2 == 1:
            keep_pair(n - 3, [partial.pop(n - 3), partial.pop(n - 2)])

    total = None
    for i in range(4):
        term = dot_nt(put_ref[i], kept_ref[i])
        total = term if total is None else total + term
    total = total.astype(out_ref.dtype)
    lon_count = out_ref.shape[0] // owners
    rows, lanes = out_ref.shape[1:]
    for b in range(owners):
        for q in range(0, lon_count, 2):
            out_ref[b * lon_count + q + side] = total[b * rows : (b + 1) * rows, :lanes]
            out_ref[b * lon_count + q + 1 - side] = total[b * rows : (b + 1) * rows, lanes:]


def add_degrees(lon_count, values_ref, out_ref):
    for b in range(out_ref.shape[0]):
        value = values_ref[b * lon_count].astype(jnp.float32)
        for q in range(1, lon_count):
            value = value + values_ref[b * lon_count + q].astype(jnp.float32)
        out_ref[b] = value


def half_grid(which, turn_ref, basis_ref, value_ref, left_ref):
    owners, rows, lanes = value_ref.shape
    blocks = turn_ref.shape[3]
    height = blocks * rows
    for b in range(owners):
        value = value_ref[b]
        other = pltpu.roll(value, lanes // 2, 1)
        for a in range(blocks):
            term = value * turn_ref[which, 0, b, a : a + 1] + other * turn_ref[which, 1, b, a : a + 1]
            high, low = split(term)
            left_ref[a * rows : (a + 1) * rows, b * lanes : (b + 1) * lanes] = high
            left_ref[height + a * rows : height + (a + 1) * rows, b * lanes : (b + 1) * lanes] = low
    grid = dot_nt(left_ref[...], basis_ref[which, 0])
    return grid[:height] + grid[height:] + dot_nt(left_ref[:height], basis_ref[which, 1])


def own_grid(turn_ref, basis_ref, value_ref, out_ref, left_ref):
    out_ref[...] = half_grid(lax.axis_index("lon") % 2, turn_ref, basis_ref, value_ref, left_ref)


def synthesise_grid(turn_ref, basis_ref, value_ref, grid_ref, out_ref, left_ref):
    rows = value_ref.shape[1]
    cycles = out_ref.shape[2]
    grid = grid_ref[...] + half_grid(1 - lax.axis_index("lon") % 2, turn_ref, basis_ref, value_ref, left_ref)
    for a in range(grid.shape[0] // rows):
        for g in range(2):
            for h in range(2):
                at = a * rows + (g * 2 + h) * cycles
                out_ref[g, h, :, a * LANES : (a + 1) * LANES] = grid[at : at + cycles]


def fits(owners, lon_count, cycles, points, per_owner, degrees):
    northern = owners * cycles
    total = points * lon_count
    return (
        per_owner == LANES
        and 4 * per_owner == lon_count * LANES
        and lon_count % 2 == 0
        and 2 * cycles == ROWS
        and 4 * northern == LANES
        and ROWS * northern == degrees
        and degrees % LANES == 0
        and owners == ROWS
        and points % LANES == 0
        and total & (total - 1) == 0
        and owners * per_owner * LANES < 1 << 24
    )


def per_device_kernels(loads, legendre, love, cycle_weight, order_list, cycle_order):
    owners = lax.axis_size("band")
    lon_count = lax.axis_size("lon")
    cycles, points = loads.shape[2], loads.shape[3]
    per_owner, degrees, northern = legendre.shape
    total = points * lon_count
    devices = owners * lon_count
    blocks = points // LANES
    everyone = ("band", "lon")
    vmem = pl.BlockSpec(memory_space=pltpu.VMEM)
    table = order_list.reshape(owners, per_owner)
    cycle_list = cycle_order.reshape(1, northern)

    def kernel(body, out_shape, in_specs, scratch_shapes, flops):
        return pl.pallas_call(
            body,
            out_shape=out_shape,
            in_specs=in_specs,
            out_specs=jax.tree.map(lambda _: vmem, out_shape),
            scratch_shapes=scratch_shapes,
            compiler_params=pltpu.CompilerParams(vmem_limit_bytes=VMEM_LIMIT),
            cost_estimate=pl.CostEstimate(flops=flops, bytes_accessed=1 << 20, transcendentals=0),
            name=getattr(body, "func", body).__name__,
        )

    partner = [(i, i ^ 1) for i in range(lon_count)]
    parts = [loads, lax.ppermute(loads, "lon", partner)]
    count = 2 * blocks
    width = owners * per_owner // 2
    right, first = kernel(
        functools.partial(forward_tables, blocks, total),
        (
            jax.ShapeDtypeStruct((3 * LANES, 2 * width), jnp.bfloat16),
            jax.ShapeDtypeStruct((2, count, width), jnp.float32),
        ),
        [vmem],
        [],
        1 << 31,
    )(table)
    sums = kernel(
        functools.partial(analyse_grid, total),
        jax.ShapeDtypeStruct((devices, 2 * cycles, LANES), jnp.float32),
        [vmem] * (4 + len(parts)),
        [
            pltpu.VMEM((count * 4 * cycles, LANES), jnp.float32),
            pltpu.VMEM((count * 4 * cycles, 2 * width), jnp.float32),
        ],
        1 << 34,
    )(right, first, cycle_weight.reshape(1, northern), cycle_list, *parts)
    arrived = lax.all_to_all(sums, everyone, split_axis=0, concat_axis=0, tiled=True)
    folded = kernel(
        add_points,
        jax.ShapeDtypeStruct((2, owners, 2 * cycles, LANES), jnp.bfloat16),
        [vmem],
        [],
        1 << 28,
    )(arrived)
    others = lax.ppermute(folded, "lon", partner)
    pick, put, order_rows, turns, basis = kernel(
        functools.partial(later_tables, cycles, blocks, total),
        (
            jax.ShapeDtypeStruct((2 * LANES, LANES), jnp.bfloat16),
            jax.ShapeDtypeStruct((4, LANES, degrees), jnp.bfloat16),
            jax.ShapeDtypeStruct((per_owner, LANES), jnp.int32),
            jax.ShapeDtypeStruct((2, 2, owners, blocks, per_owner), jnp.float32),
            jax.ShapeDtypeStruct((2, 2, LANES, owners * per_owner), jnp.bfloat16),
        ),
        [vmem, vmem, vmem],
        [],
        1 << 26,
    )(table, cycle_list, folded)

    rows = jnp.transpose(legendre, (0, 2, 1)).reshape(per_owner * northern, degrees)
    values = kernel(
        spectral,
        jax.ShapeDtypeStruct((devices, 4 * cycles, per_owner), jnp.bfloat16),
        [vmem] * 7,
        [
            pltpu.VMEM((4 * LANES, 2 * LANES), jnp.float32),
            pltpu.VMEM((4, 2 * per_owner, degrees), jnp.bfloat16),
        ],
        1 << 31,
    )(pick, put, order_rows, folded, others, rows, love)
    returned = lax.all_to_all(values, everyone, split_axis=0, concat_axis=0, tiled=True)

    own = kernel(
        functools.partial(add_degrees, lon_count),
        jax.ShapeDtypeStruct((owners, 4 * cycles, per_owner), jnp.float32),
        [vmem],
        [],
        1 << 28,
    )(returned)
    other = lax.ppermute(own, "lon", partner)
    left = [pltpu.VMEM((2 * 4 * cycles * blocks, owners * per_owner), jnp.bfloat16)]
    grid = kernel(
        own_grid, jax.ShapeDtypeStruct((4 * cycles * blocks, LANES), jnp.float32), [vmem] * 3, left, 1 << 30
    )(turns, basis, own)
    return kernel(synthesise_grid, jax.ShapeDtypeStruct(loads.shape, jnp.float32), [vmem] * 4, left, 1 << 30)(
        turns, basis, other, grid
    )


def per_device(loads, legendre, love, cycle_weight, order_list, cycle_order):
    sizes = (lax.axis_size("band"), lax.axis_size("lon"), loads.shape[2], loads.shape[3], legendre.shape[0], legendre.shape[1])
    form = per_device_kernels if fits(*sizes) else per_device_plain
    return form(loads, legendre, love, cycle_weight, order_list, cycle_order)


def cycle_basis(order_ids, positions, total):
    phase = positions[:, None] * order_ids[None, :] % total
    angle = phase.astype(jnp.float32) * (2.0 * math.pi / total)
    scale = 1.0 / math.sqrt(total)
    return (jnp.cos(angle) * scale, jnp.sin(angle) * scale)


def per_device_plain(loads, legendre, love, cycle_weight, order_list, cycle_order):
    highest = lax.Precision.HIGHEST
    owners = lax.axis_size("band")
    lon_count = lax.axis_size("lon")
    band_index = lax.axis_index("band")
    lon_index = lax.axis_index("lon")
    cycle_pairs = loads.shape[2]
    points = loads.shape[3]
    total = points * lon_count
    orders = order_list.shape[0]
    per_owner = legendre.shape[0]
    degree_count = legendre.shape[1]
    northern = legendre.shape[2]
    quarter = per_owner // lon_count
    positions = lon_index * points + jnp.arange(points, dtype=jnp.int32)
    cosine, sine = cycle_basis(order_list, positions, total)
    my_cycles = lax.dynamic_slice_in_dim(cycle_order, band_index * cycle_pairs, cycle_pairs)
    picker = my_cycles[:, None] == jnp.arange(northern, dtype=jnp.int32)[None, :]
    weights = jnp.sum(jnp.where(picker, cycle_weight[None, :], 0.0), axis=1)
    forward = jnp.stack([cosine, -sine], axis=1)
    spectrum = jnp.einsum("fhjx,xrm->fhjrm", loads, forward, precision=highest)
    spectrum = spectrum.reshape(2, 2, cycle_pairs, 2, owners, per_owner)
    summed = lax.psum_scatter(spectrum, "lon", scatter_dimension=5, tiled=True)
    cycle_scale = weights[None, :, None, None, None]
    symmetric = ((summed[:, 0] + summed[:, 1]) * cycle_scale).astype(jnp.bfloat16)
    antisym = ((summed[:, 0] - summed[:, 1]) * cycle_scale).astype(jnp.bfloat16)
    folded = jnp.stack([symmetric, antisym], axis=1)
    slot_width = folded.shape[5]
    outgoing = jnp.transpose(folded, (4, 5, 0, 1, 3, 2)).reshape(owners, slot_width, 8, cycle_pairs)
    arrived = lax.all_to_all(outgoing, "band", split_axis=0, concat_axis=3, tiled=True).reshape(
        slot_width, 8, northern
    )
    columns = lax.all_gather(arrived, "lon", axis=0, tiled=True)
    inverse_rows = jnp.argsort(cycle_order)
    columns_sorted = jnp.take(columns, inverse_rows, axis=2)
    my_orders = lax.dynamic_slice_in_dim(order_list, band_index * per_owner, per_owner)
    degrees = lon_index * degree_count + jnp.arange(degree_count, dtype=jnp.int32)
    analysed = jnp.einsum(
        "olk,ock->ocl", legendre, columns_sorted, preferred_element_type=jnp.float32
    )
    analysed = analysed.reshape(per_owner, 2, 2, 2, degree_count)
    even = (degrees[None, :] - my_orders[:, None]) % 2 == 0
    valid = degrees[None, :] >= my_orders[:, None]
    selected = jnp.where(even[:, None, None, :], analysed[:, :, 0], analysed[:, :, 1])
    selected = selected * valid[:, None, None, :].astype(jnp.float32)
    response = jnp.einsum("gfl,ofrl->ogrl", love, selected, precision=highest).astype(jnp.bfloat16)
    even_part = jnp.where((even & valid)[:, None, None, :], response, jnp.zeros_like(response))
    odd_part = jnp.where((~even & valid)[:, None, None, :], response, jnp.zeros_like(response))
    stacked = jnp.stack([even_part, odd_part], axis=2).reshape(per_owner, 8, degree_count)
    partial_sorted = jnp.einsum(
        "olk,ocl->ock", legendre, stacked, preferred_element_type=jnp.float32
    )
    partial_value = jnp.take(partial_sorted, cycle_order, axis=2)
    reduced = lax.psum_scatter(partial_value, "lon", scatter_dimension=0, tiled=True)
    returned = lax.all_to_all(reduced, "band", split_axis=2, concat_axis=0, tiled=True)
    gathered = lax.all_gather(returned[None], "lon", axis=0, tiled=True).reshape(
        orders, 8, cycle_pairs
    )
    slot_ids = jnp.transpose(order_list.reshape(owners, lon_count, quarter), (1, 0, 2)).reshape(
        orders
    )
    cosine_back, sine_back = cycle_basis(slot_ids, positions, total)
    pieces = gathered.reshape(orders, 2, 2, 2, cycle_pairs)
    cycle_values = jnp.stack(
        [pieces[:, :, 0] + pieces[:, :, 1], pieces[:, :, 0] - pieces[:, :, 1]], axis=2
    )
    factor = jnp.where(slot_ids == 0, 1.0, 2.0).astype(jnp.float32)
    inverse = jnp.stack([cosine_back.T, -sine_back.T], axis=0)
    scaled = cycle_values * factor[:, None, None, None, None]
    return jnp.einsum("sghrp,rsx->ghpx", scaled, inverse, precision=highest)


def solution(mesh):
    return jax.shard_map(
        per_device,
        mesh=mesh,
        in_specs=(
            P(None, None, "band", "lon"),
            P("band", "lon", None),
            P(None, None, "lon"),
            P(),
            P(),
            P(),
        ),
        out_specs=P(None, None, "band", "lon"),
        check_vma=False,
    )
```

```python
import functools
import math

import jax
import jax.numpy as jnp
from jax import lax
from jax.experimental import pallas as pl
from jax.experimental.pallas import tpu as pltpu
from jax.sharding import PartitionSpec as P

LANES = 128
ROWS = 8
VMEM_LIMIT = 12 << 20
NT = (((1,), (1,)), ((), ()))


def iota(shape, axis):
    return lax.broadcasted_iota(jnp.int32, shape, axis)


def turn(phase, total):
    shift = (total // 4).bit_length() - 1
    quadrant = (phase + total // 8) >> shift
    x = (phase - (quadrant << shift)).astype(jnp.float32) * (2.0 * math.pi / total)
    z = x * x
    s = ((-1.9515295891e-4 * z + 8.3321608736e-3) * z - 1.6666654611e-1) * z * x + x
    c = ((2.443315711809948e-5 * z - 1.388731625493765e-3) * z + 4.166664568298827e-2) * z * z
    c = c - 0.5 * z + 1.0
    odd = (quadrant & 1) == 1
    cosine = jnp.where(odd, s, c)
    sine = jnp.where(odd, c, s)
    cosine = jnp.where(((quadrant + 1) & 2) == 2, -cosine, cosine)
    sine = jnp.where((quadrant & 2) == 2, -sine, sine)
    return cosine, sine


def split(x):
    high = x.astype(jnp.bfloat16)
    return high, (x - high.astype(jnp.float32)).astype(jnp.bfloat16)


def dot(a, b):
    return jnp.dot(a, b, preferred_element_type=jnp.float32)


def dot_nt(a, b):
    return lax.dot_general(a, b, NT, preferred_element_type=jnp.float32)


def analyse_grid(total, after_ref, right_ref, turn_ref, weight_ref, cycle_ref, *refs):
    del after_ref
    parts, out_ref, points_ref, mid_ref = refs[:-3], refs[-3], refs[-2], refs[-1]
    cycles = parts[0].shape[2]
    blocks = parts[0].shape[3] // LANES
    count, width = turn_ref.shape[1:]
    owners = width // (LANES // 2)
    lon_count = out_ref.shape[0] // owners
    quarter = width // owners // 2
    pieces = LANES // quarter
    step = 2 * cycles

    for q, part in enumerate(parts):
        for a in range(blocks):
            for f in range(2):
                north = part[f, 0, :, a * LANES : (a + 1) * LANES]
                south = part[f, 1, :, a * LANES : (a + 1) * LANES]
                at = ((q * blocks + a) * 2 + f) * step
                points_ref[at : at + step] = jnp.concatenate([north + south, north - south], axis=0)
    high, low = split(points_ref[...])
    mid_ref[...] = dot(jnp.concatenate([high, low, high], axis=1), right_ref[...])

    sums = [[jnp.zeros((step, width), jnp.float32) for _ in range(2)] for _ in range(2)]
    for a in range(count):
        ca, sa = turn_ref[0, a : a + 1], turn_ref[1, a : a + 1]
        for f in range(2):
            at = (a * 2 + f) * step
            tc = mid_ref[at : at + step, :width]
            ts = mid_ref[at : at + step, width:]
            sums[f][0] = sums[f][0] + (ca * tc - sa * ts)
            sums[f][1] = sums[f][1] - (sa * tc + ca * ts)

    slot = iota((1, LANES), 1) // quarter
    northern = cycle_ref.shape[1]
    lane = iota((step, northern), 1)
    row = lax.axis_index("band") * cycles + iota((step, northern), 0) % cycles
    listed = jnp.sum(jnp.where(lane == row, cycle_ref[...].astype(jnp.float32), 0.0), axis=1, keepdims=True)
    weight = jnp.sum(jnp.where(lane == listed.astype(jnp.int32), weight_ref[...], 0.0), axis=1, keepdims=True)
    weight = weight * (1.0 / math.sqrt(total))
    for owner in range(owners):
        for side in range(2):
            t, i = (2 * owner + side) // pieces, (2 * owner + side) % pieces
            block = None
            for e in range(4):
                piece = sums[e // 2][e % 2][:, t * LANES : (t + 1) * LANES]
                move = (e - i) * quarter % LANES
                piece = pltpu.roll(piece, move, 1) if move else piece
                block = piece if block is None else jnp.where(slot == e, piece, block)
            block = block * weight
            for q in range(side, lon_count, 2):
                out_ref[owner * lon_count + q] = block


def add_points(parts_ref, out_ref):
    sides, owners = out_ref.shape[:2]
    lon_count = parts_ref.shape[0] // owners
    for c in range(sides):
        for b in range(owners):
            value = parts_ref[b * lon_count + c]
            for q in range(c + sides, lon_count, sides):
                value = value + parts_ref[b * lon_count + q]
            out_ref[c, b] = value.astype(out_ref.dtype)


def products(fine, coarse):
    for k in range(coarse[0].shape[0]):
        cc, cs = coarse[0][k : k + 1], coarse[1][k : k + 1]
        yield fine[0] * cc - fine[1] * cs, fine[1] * cc + fine[0] * cs


def opening(out_ref):
    out_ref[...] = jnp.zeros_like(out_ref)


def forward_tables(blocks, total, orders_ref, after_ref, right_ref, first_ref):
    del after_ref
    owners, per_owner = orders_ref.shape
    share = per_owner // 2
    lon = lax.axis_index("lon")
    side = lon % 2
    first_lanes = iota((1, LANES), 1) < share

    mine = pltpu.roll(orders_ref[...], (LANES - share * side) % LANES, 1)
    moved = pltpu.roll(mine, share, 1)
    orders = jnp.concatenate(
        [jnp.where(first_lanes, mine[b : b + 1], moved[b + 1 : b + 2]) for b in range(0, owners, 2)], axis=1
    )
    width = orders.shape[1]
    fine = turn(iota((ROWS, width), 0) * orders, total)
    coarse = turn((iota((LANES // ROWS, width), 0) * ROWS * orders) & (total - 1), total)
    kept = []
    for k, pair in enumerate(products(fine, coarse)):
        kept.append([split(table) for table in pair])
        if k % 2 == 0:
            continue
        for c in range(2):
            high, low = [jnp.concatenate([kept[k - 1][c][i], kept[k][c][i]], axis=0) for i in range(2)]
            for i, value in enumerate((high, high, low)):
                at = i * LANES + (k - 1) * ROWS
                right_ref[at : at + 2 * ROWS, c * width : (c + 1) * width] = value
    for k in range(2):
        origin = lon if k == 0 else lon + 1 - 2 * side
        step = iota((blocks, width), 0) + origin * blocks
        for c, table in enumerate(turn((step * LANES * orders) & (total - 1), total)):
            first_ref[c, k * blocks : (k + 1) * blocks] = table


def cycle_tables(owners, cycles, after_ref, cycle_ref, pick_ref, put_ref):
    del after_ref
    northern = owners * cycles
    wide = put_ref.shape[2]
    lane = iota((1, LANES), 1)

    listed = jnp.broadcast_to(cycle_ref[...].astype(jnp.float32), (LANES, northern)).astype(jnp.bfloat16)
    index = iota((LANES, northern), 0)

    def places(repeat):
        place = index // (repeat * cycles) * cycles + index % cycles
        return jnp.where(place == iota((LANES, northern), 1), 1.0, 0.0).astype(jnp.bfloat16)

    arriving = dot_nt(listed[: 2 * ROWS], places(2))[:1].astype(jnp.int32)
    found = (iota((northern, LANES), 0) == arriving) & (lane < 2 * northern)
    for p in range(2):
        one = jnp.where(found & (lane // cycles % 2 == p), 1.0, 0.0)
        copies = jnp.concatenate([one] * (LANES // northern), axis=0)
        pick_ref[p * LANES : (p + 1) * LANES] = copies.astype(jnp.bfloat16)
    leaving = dot_nt(places(4), listed).astype(jnp.int32)
    found = leaving == iota((LANES, LANES), 1) % northern
    part = iota((LANES, LANES), 0) // cycles % 4
    for i in range(4):
        put = jnp.where(found & (part == i), 1.0, 0.0)
        put_ref[i] = jnp.concatenate([put] * (wide // LANES), axis=1).astype(jnp.bfloat16)


def half_tables(which, total, orders_ref, turn_ref, basis_ref):
    owners, per_owner = orders_ref.shape
    blocks = turn_ref.shape[2]
    share, quarter = per_owner // 2, per_owner // 4
    lon = lax.axis_index("lon")
    lane = iota((1, LANES), 1)
    first_lanes = lane < share
    slot = lane // quarter

    orders = orders_ref[...]
    moved = [orders] + [pltpu.roll(orders, quarter * i, 1) for i in range(1, 4)]
    even = [moved[0], moved[3], moved[2], moved[1]]
    odd = [moved[3], moved[2], moved[1], moved[0]]
    doubled = jnp.zeros_like(orders)
    for i in range(4):
        doubled = jnp.where(slot == i, jnp.where(which == 0, even[i], odd[i]), doubled)

    scale = 1.0 / math.sqrt(total)
    back = jnp.where(first_lanes, 0, total - total // 4)
    for b in range(owners):
        order = doubled[b : b + 1]
        factor = jnp.where(order == 0, scale, 2.0 * scale)
        step = iota((blocks, per_owner), 0) + lon * blocks
        cos_a, sin_a = turn((step * LANES * order) & (total - 1), total)
        turn_ref[0, b] = jnp.where(first_lanes, cos_a, -cos_a) * factor
        turn_ref[1, b] = -sin_a * factor
        fine = turn((iota((ROWS, per_owner), 0) * order + back) & (total - 1), total)
        coarse = turn((iota((LANES // ROWS, per_owner), 0) * ROWS * order) & (total - 1), total)
        kept = []
        for k in range(LANES // ROWS):
            value = fine[0] * coarse[0][k : k + 1] - fine[1] * coarse[1][k : k + 1]
            kept.append(split(value))
            if k % 2 == 1:
                rows = slice((k - 1) * ROWS, (k + 1) * ROWS)
                for i in range(2):
                    both = jnp.concatenate([kept[k - 1][i], kept[k][i]], axis=0)
                    basis_ref[i, rows, b * per_owner : (b + 1) * per_owner] = both


def own_tables(total, orders_ref, after_ref, rows_ref, turn_ref, basis_ref):
    del after_ref
    per_owner = orders_ref.shape[1]
    own = orders_ref[pl.ds(lax.axis_index("band"), 1), :].astype(jnp.float32)
    rows_ref[...] = jnp.transpose(jnp.broadcast_to(own, (LANES, per_owner))).astype(jnp.int32)
    half_tables(lax.axis_index("lon") % 2, total, orders_ref, turn_ref, basis_ref)


def other_tables(total, orders_ref, after_ref, turn_ref, basis_ref):
    del after_ref
    half_tables(1 - lax.axis_index("lon") % 2, total, orders_ref, turn_ref, basis_ref)


def spectral(
    pick_ref, put_ref, rows_ref, own_ref, other_ref, legendre_ref, love_ref, out_ref, spread_ref, kept_ref
):
    parts, owners, height = own_ref.shape[:3]
    quarter = rows_ref.shape[0] // (2 * parts)
    degrees = legendre_ref.shape[1]
    northern = owners * height // 2
    group = degrees // northern
    wide = group * northern
    lon = lax.axis_index("lon")
    side = lon % 2

    pad = jnp.zeros((LANES - 2 * northern, LANES), jnp.float32)
    turned = []
    for folded_ref in (own_ref, other_ref):
        for q in range(parts):
            pieces = [folded_ref[q, b].astype(jnp.float32) for b in range(owners)]
            turned.append(jnp.transpose(jnp.concatenate(pieces + [pad], axis=0)))
    spread_ref[...] = dot_nt(jnp.concatenate(turned, axis=0).astype(jnp.bfloat16), pick_ref[...])

    degree = lon * degrees + iota((ROWS, degrees), 1)
    diagonal = iota((ROWS, wide), 0) == iota((ROWS, wide), 1) // northern
    love = [[love_ref[g, f : f + 1, :] for f in range(2)] for g in range(2)]
    groups = 2 * parts * quarter // group

    def place(n):
        q, first = n * group // quarter, n * group % quarter
        taken = side if q < parts else 1 - side
        return q, first, (2 * (q % parts) + taken) * quarter + first

    def table(n):
        start = pl.multiple_of(place(n)[2] * northern, wide)
        return legendre_ref[pl.ds(start, wide)]

    def analyse(n):
        q, first, _ = place(n)
        left = []
        for f in range(2):
            for p in range(2):
                for c in range(2):
                    at = q * LANES + (f * 2 + c) * quarter + first
                    piece = spread_ref[at : at + group, p * LANES : (p + 1) * LANES]
                    left.append(jnp.where(diagonal, jnp.concatenate([piece] * (wide // LANES), axis=1), 0.0))
        return dot(jnp.concatenate(left, axis=0).astype(jnp.bfloat16), table(n))

    def respond(n, analysed):
        order = rows_ref[pl.ds(pl.multiple_of(place(n)[2], group), group)]
        gap = degree - jnp.concatenate([order] * (degrees // LANES), axis=1)
        valid = gap >= 0
        keep = [valid & ((gap & 1) == p) for p in range(2)]
        mixed = []
        for g in range(2):
            for p in range(2):
                for c in range(2):
                    lo = (p * 2 + c) * group
                    hi = ((2 + p) * 2 + c) * group
                    value = love[g][0] * analysed[lo : lo + group] + love[g][1] * analysed[hi : hi + group]
                    mixed.append(jnp.where(keep[p], value, 0.0))
        return dot_nt(jnp.concatenate(mixed, axis=0).astype(jnp.bfloat16), table(n))

    def keep_pair(n, halves):
        for g in range(2):
            for c in range(2):
                lo, hi = (g * 4 + c) * group, (g * 4 + 2 + c) * group
                rows = [(half[lo : lo + group], half[hi : hi + group]) for half in halves]
                share = parts * quarter
                at = (n * group // share * 2 + c) * share + n * group % share
                for h in range(2):
                    both = [even + odd if h == 0 else even - odd for even, odd in rows]
                    both = [jnp.where(diagonal, value, 0.0) for value in both]
                    kept_ref[g * 2 + h, at : at + 2 * group, :] = jnp.concatenate(both, axis=0).astype(jnp.bfloat16)

    analysed, partial = {}, {}
    for n in range(groups + 2):
        if n < groups:
            analysed[n] = analyse(n)
        if 1 <= n <= groups:
            partial[n - 1] = respond(n - 1, analysed.pop(n - 1))
        if n >= 3 and n % 2 == 1:
            keep_pair(n - 3, [partial.pop(n - 3), partial.pop(n - 2)])

    total = None
    for i in range(4):
        term = dot_nt(put_ref[i], kept_ref[i])
        total = term if total is None else total + term
    total = total.astype(out_ref.dtype)
    lon_count = out_ref.shape[0] // owners
    rows, lanes = out_ref.shape[1:]
    for b in range(owners):
        for q in range(0, lon_count, 2):
            out_ref[b * lon_count + q + side] = total[b * rows : (b + 1) * rows, :lanes]
            out_ref[b * lon_count + q + 1 - side] = total[b * rows : (b + 1) * rows, lanes:]


def add_degrees(lon_count, values_ref, out_ref):
    for b in range(out_ref.shape[0]):
        value = values_ref[b * lon_count].astype(jnp.float32)
        for q in range(1, lon_count):
            value = value + values_ref[b * lon_count + q].astype(jnp.float32)
        out_ref[b] = value


def half_grid(turn_ref, basis_ref, value_ref, left_ref):
    owners, rows, lanes = value_ref.shape
    blocks = turn_ref.shape[2]
    height = blocks * rows
    for b in range(owners):
        value = value_ref[b]
        other = pltpu.roll(value, lanes // 2, 1)
        for a in range(blocks):
            term = value * turn_ref[0, b, a : a + 1] + other * turn_ref[1, b, a : a + 1]
            high, low = split(term)
            left_ref[a * rows : (a + 1) * rows, b * lanes : (b + 1) * lanes] = high
            left_ref[height + a * rows : height + (a + 1) * rows, b * lanes : (b + 1) * lanes] = low
    grid = dot_nt(left_ref[...], basis_ref[0])
    return grid[:height] + grid[height:] + dot_nt(left_ref[:height], basis_ref[1])


def own_grid(turn_ref, basis_ref, value_ref, out_ref, left_ref):
    out_ref[...] = half_grid(turn_ref, basis_ref, value_ref, left_ref)


def synthesise_grid(turn_ref, basis_ref, value_ref, grid_ref, out_ref, left_ref):
    rows = value_ref.shape[1]
    cycles = out_ref.shape[2]
    grid = grid_ref[...] + half_grid(turn_ref, basis_ref, value_ref, left_ref)
    for a in range(grid.shape[0] // rows):
        for g in range(2):
            for h in range(2):
                at = a * rows + (g * 2 + h) * cycles
                out_ref[g, h, :, a * LANES : (a + 1) * LANES] = grid[at : at + cycles]


def fits(owners, lon_count, cycles, points, per_owner, degrees):
    northern = owners * cycles
    total = points * lon_count
    return (
        per_owner == LANES
        and 4 * per_owner == lon_count * LANES
        and lon_count % 2 == 0
        and 2 * cycles == ROWS
        and 4 * northern == LANES
        and ROWS * northern == degrees
        and degrees % LANES == 0
        and owners == ROWS
        and points % LANES == 0
        and total & (total - 1) == 0
        and owners * per_owner * LANES < 1 << 24
    )


def per_device_kernels(loads, legendre, love, cycle_weight, order_list, cycle_order):
    owners = lax.axis_size("band")
    lon_count = lax.axis_size("lon")
    cycles, points = loads.shape[2], loads.shape[3]
    per_owner, degrees, northern = legendre.shape
    total = points * lon_count
    devices = owners * lon_count
    blocks = points // LANES
    everyone = ("band", "lon")
    vmem = pl.BlockSpec(memory_space=pltpu.VMEM)
    table = order_list.reshape(owners, per_owner)
    cycle_list = cycle_order.reshape(1, northern)

    def kernel(body, out_shape, in_specs, scratch_shapes, flops):
        return pl.pallas_call(
            body,
            out_shape=out_shape,
            in_specs=in_specs,
            out_specs=jax.tree.map(lambda _: vmem, out_shape),
            scratch_shapes=scratch_shapes,
            compiler_params=pltpu.CompilerParams(vmem_limit_bytes=VMEM_LIMIT),
            cost_estimate=pl.CostEstimate(flops=flops, bytes_accessed=1 << 20, transcendentals=0),
            name=getattr(body, "func", body).__name__,
        )

    partner = [(i, i ^ 1) for i in range(lon_count)]
    parts = [loads, lax.ppermute(loads, "lon", partner)]
    count = 2 * blocks
    width = owners * per_owner // 2
    opened = kernel(opening, jax.ShapeDtypeStruct((ROWS, LANES), jnp.float32), [], [], 1 << 34)()
    right, first = kernel(
        functools.partial(forward_tables, blocks, total),
        (
            jax.ShapeDtypeStruct((3 * LANES, 2 * width), jnp.bfloat16),
            jax.ShapeDtypeStruct((2, count, width), jnp.float32),
        ),
        [vmem, vmem],
        [],
        1 << 31,
    )(table, opened)
    pick, put = kernel(
        functools.partial(cycle_tables, owners, cycles),
        (
            jax.ShapeDtypeStruct((2 * LANES, LANES), jnp.bfloat16),
            jax.ShapeDtypeStruct((4, LANES, degrees), jnp.bfloat16),
        ),
        [vmem, vmem],
        [],
        1 << 28,
    )(first, cycle_list)
    sums = kernel(
        functools.partial(analyse_grid, total),
        jax.ShapeDtypeStruct((devices, 2 * cycles, LANES), jnp.float32),
        [vmem] * (5 + len(parts)),
        [
            pltpu.VMEM((count * 4 * cycles, LANES), jnp.float32),
            pltpu.VMEM((count * 4 * cycles, 2 * width), jnp.float32),
        ],
        1 << 34,
    )(pick, right, first, cycle_weight.reshape(1, northern), cycle_list, *parts)
    arrived = lax.all_to_all(sums, everyone, split_axis=0, concat_axis=0, tiled=True)
    folded = kernel(
        add_points,
        jax.ShapeDtypeStruct((2, owners, 2 * cycles, LANES), jnp.bfloat16),
        [vmem],
        [],
        1 << 28,
    )(arrived)
    others = lax.ppermute(folded, "lon", partner)
    halves = (
        jax.ShapeDtypeStruct((2, owners, blocks, per_owner), jnp.float32),
        jax.ShapeDtypeStruct((2, LANES, owners * per_owner), jnp.bfloat16),
    )
    order_rows, own_turns, own_basis = kernel(
        functools.partial(own_tables, total),
        (jax.ShapeDtypeStruct((per_owner, LANES), jnp.int32), *halves),
        [vmem, vmem],
        [],
        1 << 26,
    )(table, folded)

    rows = jnp.transpose(legendre, (0, 2, 1)).reshape(per_owner * northern, degrees)
    values = kernel(
        spectral,
        jax.ShapeDtypeStruct((devices, 4 * cycles, per_owner), jnp.bfloat16),
        [vmem] * 7,
        [
            pltpu.VMEM((4 * LANES, 2 * LANES), jnp.float32),
            pltpu.VMEM((4, 2 * per_owner, degrees), jnp.bfloat16),
        ],
        1 << 31,
    )(pick, put, order_rows, folded, others, rows, love)
    returned = lax.all_to_all(values, everyone, split_axis=0, concat_axis=0, tiled=True)

    own = kernel(
        functools.partial(add_degrees, lon_count),
        jax.ShapeDtypeStruct((owners, 4 * cycles, per_owner), jnp.float32),
        [vmem],
        [],
        1 << 28,
    )(returned)
    other = lax.ppermute(own, "lon", partner)
    left = [pltpu.VMEM((2 * 4 * cycles * blocks, owners * per_owner), jnp.bfloat16)]
    other_turns, other_basis = kernel(functools.partial(other_tables, total), halves, [vmem] * 2, [], 1 << 20)(table, own)
    grid = kernel(
        own_grid, jax.ShapeDtypeStruct((4 * cycles * blocks, LANES), jnp.float32), [vmem] * 3, left, 1 << 20
    )(own_turns, own_basis, own)
    return kernel(synthesise_grid, jax.ShapeDtypeStruct(loads.shape, jnp.float32), [vmem] * 4, left, 1 << 30)(
        other_turns, other_basis, other, grid
    )


def per_device(loads, legendre, love, cycle_weight, order_list, cycle_order):
    sizes = (lax.axis_size("band"), lax.axis_size("lon"), loads.shape[2], loads.shape[3], legendre.shape[0], legendre.shape[1])
    form = per_device_kernels if fits(*sizes) else per_device_plain
    return form(loads, legendre, love, cycle_weight, order_list, cycle_order)


def cycle_basis(order_ids, positions, total):
    phase = positions[:, None] * order_ids[None, :] % total
    angle = phase.astype(jnp.float32) * (2.0 * math.pi / total)
    scale = 1.0 / math.sqrt(total)
    return (jnp.cos(angle) * scale, jnp.sin(angle) * scale)


def per_device_plain(loads, legendre, love, cycle_weight, order_list, cycle_order):
    highest = lax.Precision.HIGHEST
    owners = lax.axis_size("band")
    lon_count = lax.axis_size("lon")
    band_index = lax.axis_index("band")
    lon_index = lax.axis_index("lon")
    cycle_pairs = loads.shape[2]
    points = loads.shape[3]
    total = points * lon_count
    orders = order_list.shape[0]
    per_owner = legendre.shape[0]
    degree_count = legendre.shape[1]
    northern = legendre.shape[2]
    quarter = per_owner // lon_count
    positions = lon_index * points + jnp.arange(points, dtype=jnp.int32)
    cosine, sine = cycle_basis(order_list, positions, total)
    my_cycles = lax.dynamic_slice_in_dim(cycle_order, band_index * cycle_pairs, cycle_pairs)
    picker = my_cycles[:, None] == jnp.arange(northern, dtype=jnp.int32)[None, :]
    weights = jnp.sum(jnp.where(picker, cycle_weight[None, :], 0.0), axis=1)
    forward = jnp.stack([cosine, -sine], axis=1)
    spectrum = jnp.einsum("fhjx,xrm->fhjrm", loads, forward, precision=highest)
    spectrum = spectrum.reshape(2, 2, cycle_pairs, 2, owners, per_owner)
    summed = lax.psum_scatter(spectrum, "lon", scatter_dimension=5, tiled=True)
    cycle_scale = weights[None, :, None, None, None]
    symmetric = ((summed[:, 0] + summed[:, 1]) * cycle_scale).astype(jnp.bfloat16)
    antisym = ((summed[:, 0] - summed[:, 1]) * cycle_scale).astype(jnp.bfloat16)
    folded = jnp.stack([symmetric, antisym], axis=1)
    slot_width = folded.shape[5]
    outgoing = jnp.transpose(folded, (4, 5, 0, 1, 3, 2)).reshape(owners, slot_width, 8, cycle_pairs)
    arrived = lax.all_to_all(outgoing, "band", split_axis=0, concat_axis=3, tiled=True).reshape(
        slot_width, 8, northern
    )
    columns = lax.all_gather(arrived, "lon", axis=0, tiled=True)
    inverse_rows = jnp.argsort(cycle_order)
    columns_sorted = jnp.take(columns, inverse_rows, axis=2)
    my_orders = lax.dynamic_slice_in_dim(order_list, band_index * per_owner, per_owner)
    degrees = lon_index * degree_count + jnp.arange(degree_count, dtype=jnp.int32)
    analysed = jnp.einsum(
        "olk,ock->ocl", legendre, columns_sorted, preferred_element_type=jnp.float32
    )
    analysed = analysed.reshape(per_owner, 2, 2, 2, degree_count)
    even = (degrees[None, :] - my_orders[:, None]) % 2 == 0
    valid = degrees[None, :] >= my_orders[:, None]
    selected = jnp.where(even[:, None, None, :], analysed[:, :, 0], analysed[:, :, 1])
    selected = selected * valid[:, None, None, :].astype(jnp.float32)
    response = jnp.einsum("gfl,ofrl->ogrl", love, selected, precision=highest).astype(jnp.bfloat16)
    even_part = jnp.where((even & valid)[:, None, None, :], response, jnp.zeros_like(response))
    odd_part = jnp.where((~even & valid)[:, None, None, :], response, jnp.zeros_like(response))
    stacked = jnp.stack([even_part, odd_part], axis=2).reshape(per_owner, 8, degree_count)
    partial_sorted = jnp.einsum(
        "olk,ocl->ock", legendre, stacked, preferred_element_type=jnp.float32
    )
    partial_value = jnp.take(partial_sorted, cycle_order, axis=2)
    reduced = lax.psum_scatter(partial_value, "lon", scatter_dimension=0, tiled=True)
    returned = lax.all_to_all(reduced, "band", split_axis=2, concat_axis=0, tiled=True)
    gathered = lax.all_gather(returned[None], "lon", axis=0, tiled=True).reshape(
        orders, 8, cycle_pairs
    )
    slot_ids = jnp.transpose(order_list.reshape(owners, lon_count, quarter), (1, 0, 2)).reshape(
        orders
    )
    cosine_back, sine_back = cycle_basis(slot_ids, positions, total)
    pieces = gathered.reshape(orders, 2, 2, 2, cycle_pairs)
    cycle_values = jnp.stack(
        [pieces[:, :, 0] + pieces[:, :, 1], pieces[:, :, 0] - pieces[:, :, 1]], axis=2
    )
    factor = jnp.where(slot_ids == 0, 1.0, 2.0).astype(jnp.float32)
    inverse = jnp.stack([cosine_back.T, -sine_back.T], axis=0)
    scaled = cycle_values * factor[:, None, None, None, None]
    return jnp.einsum("sghrp,rsx->ghpx", scaled, inverse, precision=highest)


def solution(mesh):
    return jax.shard_map(
        per_device,
        mesh=mesh,
        in_specs=(
            P(None, None, "band", "lon"),
            P("band", "lon", None),
            P(None, None, "lon"),
            P(),
            P(),
            P(),
        ),
        out_specs=P(None, None, "band", "lon"),
        check_vma=False,
    )
```

```python
import functools
import math

import jax
import jax.numpy as jnp
from jax import lax
from jax.experimental import pallas as pl
from jax.experimental.pallas import tpu as pltpu
from jax.sharding import PartitionSpec as P

LANES = 128
ROWS = 8
VMEM_LIMIT = 12 << 20
NT = (((1,), (1,)), ((), ()))


def iota(shape, axis):
    return lax.broadcasted_iota(jnp.int32, shape, axis)


def turn(phase, total):
    shift = (total // 4).bit_length() - 1
    quadrant = (phase + total // 8) >> shift
    x = (phase - (quadrant << shift)).astype(jnp.float32) * (2.0 * math.pi / total)
    z = x * x
    s = ((-1.9515295891e-4 * z + 8.3321608736e-3) * z - 1.6666654611e-1) * z * x + x
    c = ((2.443315711809948e-5 * z - 1.388731625493765e-3) * z + 4.166664568298827e-2) * z * z
    c = c - 0.5 * z + 1.0
    odd = (quadrant & 1) == 1
    cosine = jnp.where(odd, s, c)
    sine = jnp.where(odd, c, s)
    cosine = jnp.where(((quadrant + 1) & 2) == 2, -cosine, cosine)
    sine = jnp.where((quadrant & 2) == 2, -sine, sine)
    return cosine, sine


def split(x):
    high = x.astype(jnp.bfloat16)
    return high, (x - high.astype(jnp.float32)).astype(jnp.bfloat16)


def dot(a, b):
    return jnp.dot(a, b, preferred_element_type=jnp.float32)


def dot_nt(a, b):
    return lax.dot_general(a, b, NT, preferred_element_type=jnp.float32)


def analyse_grid(total, after_ref, also_after_ref, right_ref, turn_ref, weight_ref, cycle_ref, *refs):
    del after_ref, also_after_ref
    parts, out_ref, points_ref, mid_ref = refs[:-3], refs[-3], refs[-2], refs[-1]
    cycles = parts[0].shape[2]
    blocks = parts[0].shape[3] // LANES
    count, width = turn_ref.shape[1:]
    owners = width // (LANES // 2)
    lon_count = out_ref.shape[0] // owners
    quarter = width // owners // 2
    pieces = LANES // quarter
    step = 2 * cycles

    for q, part in enumerate(parts):
        for a in range(blocks):
            for f in range(2):
                north = part[f, 0, :, a * LANES : (a + 1) * LANES]
                south = part[f, 1, :, a * LANES : (a + 1) * LANES]
                at = ((q * blocks + a) * 2 + f) * step
                points_ref[at : at + step] = jnp.concatenate([north + south, north - south], axis=0)
    high, low = split(points_ref[...])
    mid_ref[...] = dot(jnp.concatenate([high, low, high], axis=1), right_ref[...])

    sums = [[jnp.zeros((step, width), jnp.float32) for _ in range(2)] for _ in range(2)]
    for a in range(count):
        ca, sa = turn_ref[0, a : a + 1], turn_ref[1, a : a + 1]
        for f in range(2):
            at = (a * 2 + f) * step
            tc = mid_ref[at : at + step, :width]
            ts = mid_ref[at : at + step, width:]
            sums[f][0] = sums[f][0] + (ca * tc - sa * ts)
            sums[f][1] = sums[f][1] - (sa * tc + ca * ts)

    slot = iota((1, LANES), 1) // quarter
    northern = cycle_ref.shape[1]
    lane = iota((step, northern), 1)
    row = lax.axis_index("band") * cycles + iota((step, northern), 0) % cycles
    listed = jnp.sum(jnp.where(lane == row, cycle_ref[...].astype(jnp.float32), 0.0), axis=1, keepdims=True)
    weight = jnp.sum(jnp.where(lane == listed.astype(jnp.int32), weight_ref[...], 0.0), axis=1, keepdims=True)
    weight = weight * (1.0 / math.sqrt(total))
    for owner in range(owners):
        for side in range(2):
            t, i = (2 * owner + side) // pieces, (2 * owner + side) % pieces
            block = None
            for e in range(4):
                piece = sums[e // 2][e % 2][:, t * LANES : (t + 1) * LANES]
                move = (e - i) * quarter % LANES
                piece = pltpu.roll(piece, move, 1) if move else piece
                block = piece if block is None else jnp.where(slot == e, piece, block)
            block = block * weight
            for q in range(side, lon_count, 2):
                out_ref[owner * lon_count + q] = block


def add_points(parts_ref, out_ref):
    sides, owners = out_ref.shape[:2]
    lon_count = parts_ref.shape[0] // owners
    for c in range(sides):
        for b in range(owners):
            value = parts_ref[b * lon_count + c]
            for q in range(c + sides, lon_count, sides):
                value = value + parts_ref[b * lon_count + q]
            out_ref[c, b] = value.astype(out_ref.dtype)


def products(fine, coarse):
    for k in range(coarse[0].shape[0]):
        cc, cs = coarse[0][k : k + 1], coarse[1][k : k + 1]
        yield fine[0] * cc - fine[1] * cs, fine[1] * cc + fine[0] * cs


def opening(out_ref):
    out_ref[...] = jnp.zeros_like(out_ref)


def forward_tables(blocks, total, orders_ref, after_ref, right_ref, first_ref):
    del after_ref
    owners, per_owner = orders_ref.shape
    share = per_owner // 2
    lon = lax.axis_index("lon")
    side = lon % 2
    first_lanes = iota((1, LANES), 1) < share

    mine = pltpu.roll(orders_ref[...], (LANES - share * side) % LANES, 1)
    moved = pltpu.roll(mine, share, 1)
    orders = jnp.concatenate(
        [jnp.where(first_lanes, mine[b : b + 1], moved[b + 1 : b + 2]) for b in range(0, owners, 2)], axis=1
    )
    width = orders.shape[1]
    fine = turn(iota((ROWS, width), 0) * orders, total)
    coarse = turn((iota((LANES // ROWS, width), 0) * ROWS * orders) & (total - 1), total)
    kept = []
    for k, pair in enumerate(products(fine, coarse)):
        kept.append([split(table) for table in pair])
        if k % 2 == 0:
            continue
        for c in range(2):
            high, low = [jnp.concatenate([kept[k - 1][c][i], kept[k][c][i]], axis=0) for i in range(2)]
            for i, value in enumerate((high, high, low)):
                at = i * LANES + (k - 1) * ROWS
                right_ref[at : at + 2 * ROWS, c * width : (c + 1) * width] = value
    for k in range(2):
        origin = lon if k == 0 else lon + 1 - 2 * side
        step = iota((blocks, width), 0) + origin * blocks
        for c, table in enumerate(turn((step * LANES * orders) & (total - 1), total)):
            first_ref[c, k * blocks : (k + 1) * blocks] = table


def cycle_tables(owners, cycles, after_ref, cycle_ref, pick_ref, put_ref):
    del after_ref
    northern = owners * cycles
    lane = iota((1, LANES), 1)

    listed = jnp.broadcast_to(cycle_ref[...].astype(jnp.float32), (LANES, northern)).astype(jnp.bfloat16)
    index = iota((LANES, northern), 0)

    def places(repeat):
        place = index // (repeat * cycles) * cycles + index % cycles
        return jnp.where(place == iota((LANES, northern), 1), 1.0, 0.0).astype(jnp.bfloat16)

    arriving = dot_nt(listed[: 2 * ROWS], places(2))[:1].astype(jnp.int32)
    found = (iota((northern, LANES), 0) == arriving) & (lane < 2 * northern)
    for p in range(2):
        one = jnp.where(found & (lane // cycles % 2 == p), 1.0, 0.0)
        copies = jnp.concatenate([one] * (LANES // northern), axis=0)
        pick_ref[p * LANES : (p + 1) * LANES] = copies.astype(jnp.bfloat16)
    leaving = dot_nt(places(4), listed).astype(jnp.int32)
    found = leaving == iota((LANES, LANES), 1) % northern
    part = iota((LANES, LANES), 0) // cycles % 4
    for i in range(4):
        put = jnp.where(found & (part == i), 1.0, 0.0)
        put_ref[i // 2, :, i % 2 * LANES : (i % 2 + 1) * LANES] = put.astype(jnp.bfloat16)


def inverse_tables(total, orders_ref, after_ref, rows_ref, turn_ref, basis_ref):
    del after_ref
    owners, per_owner = orders_ref.shape
    blocks = turn_ref.shape[2]
    quarter = per_owner // 4
    lon = lax.axis_index("lon")
    own = orders_ref[pl.ds(lax.axis_index("band"), 1), :].astype(jnp.float32)
    rows_ref[...] = jnp.transpose(jnp.broadcast_to(own, (LANES, per_owner))).astype(jnp.int32)

    slot = iota((1, LANES), 1) // quarter
    orders = orders_ref[...]
    ahead, behind = pltpu.roll(orders, LANES - quarter, 1), pltpu.roll(orders, quarter, 1)
    arranged = jnp.where(slot == 1, ahead, jnp.where(slot == 2, behind, orders))
    scale = 1.0 / math.sqrt(total)
    for b in range(owners):
        order = arranged[b : b + 1]
        factor = jnp.where(order == 0, scale, 2.0 * scale)
        step = iota((blocks, per_owner), 0) + lon * blocks
        for c, table in enumerate(turn((step * LANES * order) & (total - 1), total)):
            turn_ref[c, b] = table * factor
        fine = turn(iota((ROWS, per_owner), 0) * order, total)
        coarse = turn((iota((LANES // ROWS, per_owner), 0) * ROWS * order) & (total - 1), total)
        kept = []
        for k, pair in enumerate(products(fine, coarse)):
            kept.append([split(table) for table in pair])
            if k % 2 == 1:
                rows = slice((k - 1) * ROWS, (k + 1) * ROWS)
                for c in range(2):
                    at = (c * owners + b) * per_owner
                    for i in range(2):
                        both = jnp.concatenate([kept[k - 1][c][i], kept[k][c][i]], axis=0)
                        basis_ref[i, rows, at : at + per_owner] = both


def spectral(
    pick_ref,
    put_ref,
    rows_ref,
    folded_ref,
    own_table_ref,
    other_table_hbm,
    own_love_ref,
    other_love_ref,
    out_ref,
    spread_ref,
    kept_ref,
    partial_ref,
    other_table_ref,
    landed,
):
    parts, owners, height = folded_ref.shape[:3]
    quarter = rows_ref.shape[0] // (2 * parts)
    degrees = own_table_ref.shape[1]
    northern = owners * height // 2
    group = degrees // northern
    wide = group * northern
    lon = lax.axis_index("lon")
    side = lon % 2

    span = quarter * northern
    copies = []
    for q in range(parts):
        start = pl.multiple_of((2 * q + side) * span, span)
        source = other_table_hbm.at[pl.ds(start, span)]
        copies.append(pltpu.make_async_copy(source, other_table_ref.at[q * span : (q + 1) * span], landed.at[q]))
        copies[q].start()

    pad = jnp.zeros((LANES - 2 * northern, LANES), jnp.float32)
    turned = []
    for q in range(parts):
        pieces = [folded_ref[q, b].astype(jnp.float32) for b in range(owners)]
        turned.append(jnp.transpose(jnp.concatenate(pieces + [pad], axis=0)))
    spread_ref[...] = dot_nt(jnp.concatenate(turned, axis=0).astype(jnp.bfloat16), pick_ref[...])

    lane = iota((ROWS, degrees), 1)
    degree = [lon * degrees + lane, (lon + 1 - 2 * side) * degrees + lane]
    love = [[[ref[g, f : f + 1, :] for f in range(2)] for g in range(2)] for ref in (own_love_ref, other_love_ref)]
    diagonal = iota((ROWS, wide), 0) == iota((ROWS, wide), 1) // northern
    across = LANES // northern
    upper = iota((ROWS, LANES), 0) < across
    folded_diagonal = iota((ROWS, LANES), 0) % across == iota((ROWS, LANES), 1) // northern
    groups = parts * quarter // group

    def first_order(n):
        q, first = n * group // quarter, n * group % quarter
        return (2 * q + side) * quarter + first

    def table(n, d):
        if d == 0:
            return own_table_ref[pl.ds(pl.multiple_of(first_order(n) * northern, wide), wide)]
        return other_table_ref[n * wide : (n + 1) * wide]

    def spread(n):
        q, first = n * group // quarter, n * group % quarter
        left = []
        for f in range(2):
            for p in range(2):
                for c in range(2):
                    at = q * LANES + (f * 2 + c) * quarter + first
                    piece = spread_ref[at : at + group, p * LANES : (p + 1) * LANES]
                    left.append(jnp.where(diagonal, jnp.concatenate([piece] * (wide // LANES), axis=1), 0.0))
        return jnp.concatenate(left, axis=0).astype(jnp.bfloat16)

    def respond(n, d, analysed):
        order = rows_ref[pl.ds(pl.multiple_of(first_order(n), group), group)]
        gap = degree[d] - jnp.concatenate([order] * (degrees // LANES), axis=1)
        valid = gap >= 0
        keep = [valid & ((gap & 1) == p) for p in range(2)]
        mixed = []
        for g in range(2):
            for p in range(2):
                for c in range(2):
                    lo = (p * 2 + c) * group
                    hi = ((2 + p) * 2 + c) * group
                    value = love[d][g][0] * analysed[lo : lo + group] + love[d][g][1] * analysed[hi : hi + group]
                    mixed.append(jnp.where(keep[p], value, 0.0))
        return dot_nt(jnp.concatenate(mixed, axis=0).astype(jnp.bfloat16), table(n, d))

    def keep_pair(n, halves):
        for g in range(2):
            for c in range(2):
                lo, hi = (g * 4 + c) * group, (g * 4 + 2 + c) * group
                at = c * parts * quarter + n * group
                rows = []
                for half in halves:
                    even, odd = half[lo : lo + group], half[hi : hi + group]
                    even = jnp.where(upper, even[:, :LANES], even[:, LANES:])
                    odd = jnp.where(upper, odd[:, :LANES], odd[:, LANES:])
                    rows.append([jnp.where(folded_diagonal, x, 0.0) for x in (even + odd, even - odd)])
                for h in range(2):
                    both = jnp.concatenate([row[h] for row in rows], axis=0).astype(jnp.bfloat16)
                    kept_ref[g, at : at + 2 * group, h * LANES : (h + 1) * LANES] = both

    steps = [(n, d) for d in range(2) for n in range(groups)]
    height = 8 * group
    analysed, partial = {}, {}
    for i in range(len(steps) + 2):
        if i < len(steps):
            n, d = steps[i]
            if d == 1 and n * group % quarter == 0:
                copies[n * group // quarter].wait()
            analysed[i] = dot(spread(n), table(n, d))
        if 1 <= i <= len(steps):
            n, d = steps[i - 1]
            value = respond(n, d, analysed.pop(i - 1))
            if d == 0:
                partial_ref[n * height : (n + 1) * height] = value
            else:
                partial[n] = partial_ref[n * height : (n + 1) * height] + value
        if i > groups + 2 and (i - groups) % 2 == 1:
            n = i - groups - 3
            keep_pair(n, [partial.pop(n), partial.pop(n + 1)])

    total = dot_nt(put_ref[0], kept_ref[0]) + dot_nt(put_ref[1], kept_ref[1])
    total = total.astype(out_ref.dtype)
    lon_count = out_ref.shape[0] // owners
    rows = out_ref.shape[1]
    for b in range(owners):
        for q in range(lon_count):
            out_ref[b * lon_count + q] = total[b * rows : (b + 1) * rows]


def synthesise_grid(turn_ref, basis_ref, values_ref, out_ref, left_ref):
    owners, blocks, per_owner = turn_ref.shape[1:]
    lon_count = values_ref.shape[0] // owners
    rows = values_ref.shape[1]
    cycles = out_ref.shape[2]
    count = owners * per_owner
    height = blocks * rows
    first_lanes = iota((1, LANES), 1) < per_owner // 2
    for b in range(owners):
        halves = []
        for c in range(2):
            value = values_ref[b * lon_count + c].astype(jnp.float32)
            for q in range(c + 2, lon_count, 2):
                value = value + values_ref[b * lon_count + q].astype(jnp.float32)
            halves.append(value)
        re = jnp.where(first_lanes, halves[0], pltpu.roll(halves[1], per_owner // 2, 1))
        im = jnp.where(first_lanes, pltpu.roll(halves[0], per_owner // 2, 1), halves[1])
        at = b * per_owner
        for a in range(blocks):
            ca, sa = turn_ref[0, b, a : a + 1], turn_ref[1, b, a : a + 1]
            for c, term in ((0, ca * re - sa * im), (1, -(sa * re + ca * im))):
                high, low = split(term)
                lanes = slice(c * count + at, c * count + at + per_owner)
                left_ref[a * rows : (a + 1) * rows, lanes] = high
                left_ref[height + a * rows : height + (a + 1) * rows, lanes] = low
    grid = dot_nt(left_ref[...], basis_ref[0])
    grid = grid[:height] + grid[height:] + dot_nt(left_ref[:height], basis_ref[1])
    for a in range(blocks):
        for g in range(2):
            for h in range(2):
                at = a * rows + (g * 2 + h) * cycles
                out_ref[g, h, :, a * LANES : (a + 1) * LANES] = grid[at : at + cycles]


def fits(owners, lon_count, cycles, points, per_owner, degrees):
    northern = owners * cycles
    total = points * lon_count
    return (
        per_owner == LANES
        and 4 * per_owner == lon_count * LANES
        and lon_count % 2 == 0
        and 2 * cycles == ROWS
        and 4 * northern == LANES
        and ROWS * northern == degrees
        and degrees % LANES == 0
        and owners == ROWS
        and points % LANES == 0
        and total & (total - 1) == 0
        and owners * per_owner * LANES < 1 << 24
    )


def per_device_kernels(loads, legendre, love, cycle_weight, order_list, cycle_order):
    owners = lax.axis_size("band")
    lon_count = lax.axis_size("lon")
    cycles, points = loads.shape[2], loads.shape[3]
    per_owner, degrees, northern = legendre.shape
    total = points * lon_count
    devices = owners * lon_count
    blocks = points // LANES
    everyone = ("band", "lon")
    vmem = pl.BlockSpec(memory_space=pltpu.VMEM)
    table = order_list.reshape(owners, per_owner)
    cycle_list = cycle_order.reshape(1, northern)

    def kernel(body, out_shape, in_specs, scratch_shapes, flops):
        return pl.pallas_call(
            body,
            out_shape=out_shape,
            in_specs=in_specs,
            out_specs=jax.tree.map(lambda _: vmem, out_shape),
            scratch_shapes=scratch_shapes,
            compiler_params=pltpu.CompilerParams(vmem_limit_bytes=VMEM_LIMIT),
            cost_estimate=pl.CostEstimate(flops=flops, bytes_accessed=1 << 20, transcendentals=0),
            name=getattr(body, "func", body).__name__,
        )

    partner = [(i, i ^ 1) for i in range(lon_count)]
    rows = jnp.transpose(legendre, (0, 2, 1)).reshape(per_owner * northern, degrees)
    parts = [loads, lax.ppermute(loads, "lon", partner)]
    other_rows = lax.ppermute(rows, "lon", partner)
    other_love = lax.ppermute(love, "lon", partner)
    count = 2 * blocks
    width = owners * per_owner // 2
    opened = kernel(opening, jax.ShapeDtypeStruct((ROWS, LANES), jnp.float32), [], [], 1 << 34)()
    right, first = kernel(
        functools.partial(forward_tables, blocks, total),
        (
            jax.ShapeDtypeStruct((3 * LANES, 2 * width), jnp.bfloat16),
            jax.ShapeDtypeStruct((2, count, width), jnp.float32),
        ),
        [vmem, vmem],
        [],
        1 << 31,
    )(table, opened)
    order_rows, turns, basis = kernel(
        functools.partial(inverse_tables, total),
        (
            jax.ShapeDtypeStruct((per_owner, LANES), jnp.int32),
            jax.ShapeDtypeStruct((2, owners, blocks, per_owner), jnp.float32),
            jax.ShapeDtypeStruct((2, LANES, 2 * owners * per_owner), jnp.bfloat16),
        ),
        [vmem, vmem],
        [],
        1 << 28,
    )(table, first)
    pick, put = kernel(
        functools.partial(cycle_tables, owners, cycles),
        (
            jax.ShapeDtypeStruct((2 * LANES, LANES), jnp.bfloat16),
            jax.ShapeDtypeStruct((2, LANES, 2 * LANES), jnp.bfloat16),
        ),
        [vmem, vmem],
        [],
        1 << 28,
    )(order_rows, cycle_list)
    sums = kernel(
        functools.partial(analyse_grid, total),
        jax.ShapeDtypeStruct((devices, 2 * cycles, LANES), jnp.float32),
        [vmem] * (6 + len(parts)),
        [
            pltpu.VMEM((count * 4 * cycles, LANES), jnp.float32),
            pltpu.VMEM((count * 4 * cycles, 2 * width), jnp.float32),
        ],
        1 << 34,
    )(pick, other_love, right, first, cycle_weight.reshape(1, northern), cycle_list, *parts)
    arrived = lax.all_to_all(sums, everyone, split_axis=0, concat_axis=0, tiled=True)
    folded = kernel(
        add_points,
        jax.ShapeDtypeStruct((2, owners, 2 * cycles, LANES), jnp.bfloat16),
        [vmem],
        [],
        1 << 28,
    )(arrived)
    values = kernel(
        spectral,
        jax.ShapeDtypeStruct((devices, 4 * cycles, per_owner), jnp.bfloat16),
        [vmem] * 5 + [pl.BlockSpec(memory_space=pl.ANY)] + [vmem] * 2,
        [
            pltpu.VMEM((2 * LANES, 2 * LANES), jnp.float32),
            pltpu.VMEM((2, per_owner, 2 * LANES), jnp.bfloat16),
            pltpu.VMEM((4 * per_owner, degrees), jnp.float32),
            pltpu.VMEM((per_owner * northern // 2, degrees), jnp.bfloat16),
            pltpu.SemaphoreType.DMA((2,)),
        ],
        1 << 31,
    )(pick, put, order_rows, folded, rows, other_rows, love, other_love)
    returned = lax.all_to_all(values, everyone, split_axis=0, concat_axis=0, tiled=True)

    return kernel(
        synthesise_grid,
        jax.ShapeDtypeStruct(loads.shape, jnp.float32),
        [vmem] * 3,
        [pltpu.VMEM((2 * 4 * cycles * blocks, 2 * owners * per_owner), jnp.bfloat16)],
        1 << 31,
    )(turns, basis, returned)


def per_device(loads, legendre, love, cycle_weight, order_list, cycle_order):
    sizes = (lax.axis_size("band"), lax.axis_size("lon"), loads.shape[2], loads.shape[3], legendre.shape[0], legendre.shape[1])
    form = per_device_kernels if fits(*sizes) else per_device_plain
    return form(loads, legendre, love, cycle_weight, order_list, cycle_order)


def cycle_basis(order_ids, positions, total):
    phase = positions[:, None] * order_ids[None, :] % total
    angle = phase.astype(jnp.float32) * (2.0 * math.pi / total)
    scale = 1.0 / math.sqrt(total)
    return (jnp.cos(angle) * scale, jnp.sin(angle) * scale)


def per_device_plain(loads, legendre, love, cycle_weight, order_list, cycle_order):
    highest = lax.Precision.HIGHEST
    owners = lax.axis_size("band")
    lon_count = lax.axis_size("lon")
    band_index = lax.axis_index("band")
    lon_index = lax.axis_index("lon")
    cycle_pairs = loads.shape[2]
    points = loads.shape[3]
    total = points * lon_count
    orders = order_list.shape[0]
    per_owner = legendre.shape[0]
    degree_count = legendre.shape[1]
    northern = legendre.shape[2]
    quarter = per_owner // lon_count
    positions = lon_index * points + jnp.arange(points, dtype=jnp.int32)
    cosine, sine = cycle_basis(order_list, positions, total)
    my_cycles = lax.dynamic_slice_in_dim(cycle_order, band_index * cycle_pairs, cycle_pairs)
    picker = my_cycles[:, None] == jnp.arange(northern, dtype=jnp.int32)[None, :]
    weights = jnp.sum(jnp.where(picker, cycle_weight[None, :], 0.0), axis=1)
    forward = jnp.stack([cosine, -sine], axis=1)
    spectrum = jnp.einsum("fhjx,xrm->fhjrm", loads, forward, precision=highest)
    spectrum = spectrum.reshape(2, 2, cycle_pairs, 2, owners, per_owner)
    summed = lax.psum_scatter(spectrum, "lon", scatter_dimension=5, tiled=True)
    cycle_scale = weights[None, :, None, None, None]
    symmetric = ((summed[:, 0] + summed[:, 1]) * cycle_scale).astype(jnp.bfloat16)
    antisym = ((summed[:, 0] - summed[:, 1]) * cycle_scale).astype(jnp.bfloat16)
    folded = jnp.stack([symmetric, antisym], axis=1)
    slot_width = folded.shape[5]
    outgoing = jnp.transpose(folded, (4, 5, 0, 1, 3, 2)).reshape(owners, slot_width, 8, cycle_pairs)
    arrived = lax.all_to_all(outgoing, "band", split_axis=0, concat_axis=3, tiled=True).reshape(
        slot_width, 8, northern
    )
    columns = lax.all_gather(arrived, "lon", axis=0, tiled=True)
    inverse_rows = jnp.argsort(cycle_order)
    columns_sorted = jnp.take(columns, inverse_rows, axis=2)
    my_orders = lax.dynamic_slice_in_dim(order_list, band_index * per_owner, per_owner)
    degrees = lon_index * degree_count + jnp.arange(degree_count, dtype=jnp.int32)
    analysed = jnp.einsum(
        "olk,ock->ocl", legendre, columns_sorted, preferred_element_type=jnp.float32
    )
    analysed = analysed.reshape(per_owner, 2, 2, 2, degree_count)
    even = (degrees[None, :] - my_orders[:, None]) % 2 == 0
    valid = degrees[None, :] >= my_orders[:, None]
    selected = jnp.where(even[:, None, None, :], analysed[:, :, 0], analysed[:, :, 1])
    selected = selected * valid[:, None, None, :].astype(jnp.float32)
    response = jnp.einsum("gfl,ofrl->ogrl", love, selected, precision=highest).astype(jnp.bfloat16)
    even_part = jnp.where((even & valid)[:, None, None, :], response, jnp.zeros_like(response))
    odd_part = jnp.where((~even & valid)[:, None, None, :], response, jnp.zeros_like(response))
    stacked = jnp.stack([even_part, odd_part], axis=2).reshape(per_owner, 8, degree_count)
    partial_sorted = jnp.einsum(
        "olk,ocl->ock", legendre, stacked, preferred_element_type=jnp.float32
    )
    partial_value = jnp.take(partial_sorted, cycle_order, axis=2)
    reduced = lax.psum_scatter(partial_value, "lon", scatter_dimension=0, tiled=True)
    returned = lax.all_to_all(reduced, "band", split_axis=2, concat_axis=0, tiled=True)
    gathered = lax.all_gather(returned[None], "lon", axis=0, tiled=True).reshape(
        orders, 8, cycle_pairs
    )
    slot_ids = jnp.transpose(order_list.reshape(owners, lon_count, quarter), (1, 0, 2)).reshape(
        orders
    )
    cosine_back, sine_back = cycle_basis(slot_ids, positions, total)
    pieces = gathered.reshape(orders, 2, 2, 2, cycle_pairs)
    cycle_values = jnp.stack(
        [pieces[:, :, 0] + pieces[:, :, 1], pieces[:, :, 0] - pieces[:, :, 1]], axis=2
    )
    factor = jnp.where(slot_ids == 0, 1.0, 2.0).astype(jnp.float32)
    inverse = jnp.stack([cosine_back.T, -sine_back.T], axis=0)
    scaled = cycle_values * factor[:, None, None, None, None]
    return jnp.einsum("sghrp,rsx->ghpx", scaled, inverse, precision=highest)


def solution(mesh):
    return jax.shard_map(
        per_device,
        mesh=mesh,
        in_specs=(
            P(None, None, "band", "lon"),
            P("band", "lon", None),
            P(None, None, "lon"),
            P(),
            P(),
            P(),
        ),
        out_specs=P(None, None, "band", "lon"),
        check_vma=False,
    )
```

```python
import functools
import math

import jax
import jax.numpy as jnp
from jax import lax
from jax.experimental import pallas as pl
from jax.experimental.pallas import tpu as pltpu
from jax.sharding import PartitionSpec as P


LANES = 128
ROWS = 8
VMEM_LIMIT = 12 << 20
NT = (((1,), (1,)), ((), ()))


def iota(shape, axis):
    return lax.broadcasted_iota(jnp.int32, shape, axis)


def turn(phase, total):
    shift = (total // 4).bit_length() - 1
    quadrant = (phase + total // 8) >> shift
    x = (phase - (quadrant << shift)).astype(jnp.float32) * (2.0 * math.pi / total)
    z = x * x
    s = ((-1.9515295891e-4 * z + 8.3321608736e-3) * z - 1.6666654611e-1) * z * x + x
    c = ((2.443315711809948e-5 * z - 1.388731625493765e-3) * z + 4.166664568298827e-2) * z * z
    c = c - 0.5 * z + 1.0
    odd = (quadrant & 1) == 1
    cosine = jnp.where(odd, s, c)
    sine = jnp.where(odd, c, s)
    cosine = jnp.where(((quadrant + 1) & 2) == 2, -cosine, cosine)
    sine = jnp.where((quadrant & 2) == 2, -sine, sine)
    return cosine, sine


def split(x):
    high = x.astype(jnp.bfloat16)
    return high, (x - high.astype(jnp.float32)).astype(jnp.bfloat16)


def dot(a, b):
    return jnp.dot(a, b, preferred_element_type=jnp.float32)


def dot_nt(a, b):
    return lax.dot_general(a, b, NT, preferred_element_type=jnp.float32)


def analyse_grid(total, after_ref, right_ref, turn_ref, weight_ref, cycle_ref, *refs):
    del after_ref
    parts, out_ref, points_ref, mid_ref = refs[:-3], refs[-3], refs[-2], refs[-1]
    cycles = parts[0].shape[2]
    blocks = parts[0].shape[3] // LANES
    count, width = turn_ref.shape[1:]
    owners = width // (LANES // 2)
    lon_count = out_ref.shape[0] // owners
    quarter = width // owners // 2
    pieces = LANES // quarter
    step = 2 * cycles

    for q, part in enumerate(parts):
        for a in range(blocks):
            for f in range(2):
                north = part[f, 0, :, a * LANES : (a + 1) * LANES]
                south = part[f, 1, :, a * LANES : (a + 1) * LANES]
                at = ((q * blocks + a) * 2 + f) * step
                points_ref[at : at + step] = jnp.concatenate([north + south, north - south], axis=0)
    high, low = split(points_ref[...])
    mid_ref[...] = dot(jnp.concatenate([high, low, high], axis=1), right_ref[...])

    sums = [[jnp.zeros((step, width), jnp.float32) for _ in range(2)] for _ in range(2)]
    for a in range(count):
        ca, sa = turn_ref[0, a : a + 1], turn_ref[1, a : a + 1]
        for f in range(2):
            at = (a * 2 + f) * step
            tc = mid_ref[at : at + step, :width]
            ts = mid_ref[at : at + step, width:]
            sums[f][0] = sums[f][0] + (ca * tc - sa * ts)
            sums[f][1] = sums[f][1] - (sa * tc + ca * ts)

    slot = iota((1, LANES), 1) // quarter
    northern = cycle_ref.shape[1]
    lane = iota((step, northern), 1)
    row = lax.axis_index("band") * cycles + iota((step, northern), 0) % cycles
    listed = jnp.sum(jnp.where(lane == row, cycle_ref[...].astype(jnp.float32), 0.0), axis=1, keepdims=True)
    weight = jnp.sum(jnp.where(lane == listed.astype(jnp.int32), weight_ref[...], 0.0), axis=1, keepdims=True)
    weight = weight * (1.0 / math.sqrt(total))
    for owner in range(owners):
        for side in range(2):
            t, i = (2 * owner + side) // pieces, (2 * owner + side) % pieces
            block = None
            for e in range(4):
                piece = sums[e // 2][e % 2][:, t * LANES : (t + 1) * LANES]
                move = (e - i) * quarter % LANES
                piece = pltpu.roll(piece, move, 1) if move else piece
                block = piece if block is None else jnp.where(slot == e, piece, block)
            block = block * weight
            for q in range(side, lon_count, 2):
                out_ref[owner * lon_count + q] = block


def add_points(parts_ref, out_ref):
    sides, owners = out_ref.shape[:2]
    lon_count = parts_ref.shape[0] // owners
    for c in range(sides):
        for b in range(owners):
            value = parts_ref[b * lon_count + c]
            for q in range(c + sides, lon_count, sides):
                value = value + parts_ref[b * lon_count + q]
            out_ref[c, b] = value.astype(out_ref.dtype)


def products(fine, coarse):
    for k in range(coarse[0].shape[0]):
        cc, cs = coarse[0][k : k + 1], coarse[1][k : k + 1]
        yield fine[0] * cc - fine[1] * cs, fine[1] * cc + fine[0] * cs


def opening(out_ref):
    out_ref[...] = jnp.zeros_like(out_ref)


def forward_tables(blocks, total, orders_ref, after_ref, right_ref, first_ref):
    del after_ref
    owners, per_owner = orders_ref.shape
    share = per_owner // 2
    lon = lax.axis_index("lon")
    side = lon % 2
    first_lanes = iota((1, LANES), 1) < share

    mine = pltpu.roll(orders_ref[...], (LANES - share * side) % LANES, 1)
    moved = pltpu.roll(mine, share, 1)
    orders = jnp.concatenate(
        [jnp.where(first_lanes, mine[b : b + 1], moved[b + 1 : b + 2]) for b in range(0, owners, 2)], axis=1
    )
    width = orders.shape[1]
    fine = turn(iota((ROWS, width), 0) * orders, total)
    coarse = turn((iota((LANES // ROWS, width), 0) * ROWS * orders) & (total - 1), total)
    kept = []
    for k, pair in enumerate(products(fine, coarse)):
        kept.append([split(table) for table in pair])
        if k % 2 == 0:
            continue
        for c in range(2):
            high, low = [jnp.concatenate([kept[k - 1][c][i], kept[k][c][i]], axis=0) for i in range(2)]
            for i, value in enumerate((high, high, low)):
                at = i * LANES + (k - 1) * ROWS
                right_ref[at : at + 2 * ROWS, c * width : (c + 1) * width] = value
    for k in range(2):
        origin = lon if k == 0 else lon + 1 - 2 * side
        step = iota((blocks, width), 0) + origin * blocks
        for c, table in enumerate(turn((step * LANES * orders) & (total - 1), total)):
            first_ref[c, k * blocks : (k + 1) * blocks] = table


def cycle_tables(owners, cycles, after_ref, cycle_ref, pick_ref, put_ref):
    del after_ref
    northern = owners * cycles
    lane = iota((1, LANES), 1)

    listed = jnp.broadcast_to(cycle_ref[...].astype(jnp.float32), (LANES, northern)).astype(jnp.bfloat16)
    index = iota((LANES, northern), 0)

    def places(repeat):
        place = index // (repeat * cycles) * cycles + index % cycles
        return jnp.where(place == iota((LANES, northern), 1), 1.0, 0.0).astype(jnp.bfloat16)

    arriving = dot_nt(listed[: 2 * ROWS], places(2))[:1].astype(jnp.int32)
    found = (iota((northern, LANES), 0) == arriving) & (lane < 2 * northern)
    for p in range(2):
        one = jnp.where(found & (lane // cycles % 2 == p), 1.0, 0.0)
        copies = jnp.concatenate([one] * (LANES // northern), axis=0)
        pick_ref[p * LANES : (p + 1) * LANES] = copies.astype(jnp.bfloat16)
    leaving = dot_nt(places(4), listed).astype(jnp.int32)
    found = leaving == iota((LANES, LANES), 1) % northern
    part = iota((LANES, LANES), 0) // cycles % 4
    for i in range(4):
        put = jnp.where(found & (part == i), 1.0, 0.0)
        put_ref[i // 2, :, i % 2 * LANES : (i % 2 + 1) * LANES] = put.astype(jnp.bfloat16)


def inverse_tables(total, orders_ref, after_ref, rows_ref, turn_ref, basis_ref):
    del after_ref
    owners, per_owner = orders_ref.shape
    blocks = turn_ref.shape[2]
    quarter = per_owner // 4
    lon = lax.axis_index("lon")
    own = orders_ref[pl.ds(lax.axis_index("band"), 1), :].astype(jnp.float32)
    rows_ref[...] = jnp.transpose(jnp.broadcast_to(own, (LANES, per_owner))).astype(jnp.int32)

    slot = iota((1, LANES), 1) // quarter
    orders = orders_ref[...]
    ahead, behind = pltpu.roll(orders, LANES - quarter, 1), pltpu.roll(orders, quarter, 1)
    arranged = jnp.where(slot == 1, ahead, jnp.where(slot == 2, behind, orders))
    scale = 1.0 / math.sqrt(total)
    for b in range(owners):
        order = arranged[b : b + 1]
        factor = jnp.where(order == 0, scale, 2.0 * scale)
        step = iota((blocks, per_owner), 0) + lon * blocks
        for c, table in enumerate(turn((step * LANES * order) & (total - 1), total)):
            turn_ref[c, b] = table * factor
        fine = turn(iota((ROWS, per_owner), 0) * order, total)
        coarse = turn((iota((LANES // ROWS, per_owner), 0) * ROWS * order) & (total - 1), total)
        kept = []
        for k, pair in enumerate(products(fine, coarse)):
            kept.append(pair)
            if k % 2 == 1:
                rows = slice((k - 1) * ROWS, (k + 1) * ROWS)
                for c in range(2):
                    at = (c * owners + b) * per_owner
                    both = jnp.concatenate([kept[k - 1][c], kept[k][c]], axis=0)
                    basis_ref[rows, at : at + per_owner] = both.astype(basis_ref.dtype)


def spectral(
    pick_ref,
    put_ref,
    rows_ref,
    folded_ref,
    own_table_ref,
    other_table_ref,
    own_love_ref,
    other_love_ref,
    out_ref,
    spread_ref,
    kept_ref,
):
    parts, owners, height = folded_ref.shape[:3]
    quarter = rows_ref.shape[0] // (2 * parts)
    degrees = own_table_ref.shape[1]
    northern = owners * height // 2
    group = degrees // northern
    wide = group * northern
    lon = lax.axis_index("lon")
    side = lon % 2

    pad = jnp.zeros((LANES - 2 * northern, LANES), jnp.float32)
    turned = []
    for q in range(parts):
        pieces = [folded_ref[q, b].astype(jnp.float32) for b in range(owners)]
        turned.append(jnp.transpose(jnp.concatenate(pieces + [pad], axis=0)))
    spread_ref[...] = dot_nt(jnp.concatenate(turned, axis=0).astype(jnp.bfloat16), pick_ref[...])

    lane = iota((ROWS, degrees), 1)
    degree = [lon * degrees + lane, (lon + 1 - 2 * side) * degrees + lane]
    tables = [own_table_ref, other_table_ref]
    love = [[[ref[g, f : f + 1, :] for f in range(2)] for g in range(2)] for ref in (own_love_ref, other_love_ref)]
    diagonal = iota((ROWS, wide), 0) == iota((ROWS, wide), 1) // northern
    across = LANES // northern
    upper = iota((ROWS, LANES), 0) < across
    folded_diagonal = iota((ROWS, LANES), 0) % across == iota((ROWS, LANES), 1) // northern
    groups = parts * quarter // group

    def first_order(n):
        q, first = n * group // quarter, n * group % quarter
        return (2 * q + side) * quarter + first

    def table(n, d):
        return tables[d][pl.ds(pl.multiple_of(first_order(n) * northern, wide), wide)]

    def spread(n):
        q, first = n * group // quarter, n * group % quarter
        left = []
        for f in range(2):
            for p in range(2):
                for c in range(2):
                    at = q * LANES + (f * 2 + c) * quarter + first
                    piece = spread_ref[at : at + group, p * LANES : (p + 1) * LANES]
                    left.append(jnp.where(diagonal, jnp.concatenate([piece] * (wide // LANES), axis=1), 0.0))
        return jnp.concatenate(left, axis=0).astype(jnp.bfloat16)

    def respond(n, d, analysed):
        order = rows_ref[pl.ds(pl.multiple_of(first_order(n), group), group)]
        gap = degree[d] - jnp.concatenate([order] * (degrees // LANES), axis=1)
        valid = gap >= 0
        keep = [valid & ((gap & 1) == p) for p in range(2)]
        mixed = []
        for g in range(2):
            for p in range(2):
                for c in range(2):
                    lo = (p * 2 + c) * group
                    hi = ((2 + p) * 2 + c) * group
                    value = love[d][g][0] * analysed[lo : lo + group] + love[d][g][1] * analysed[hi : hi + group]
                    mixed.append(jnp.where(keep[p], value, 0.0))
        return dot_nt(jnp.concatenate(mixed, axis=0).astype(jnp.bfloat16), table(n, d))

    def keep_pair(n, halves):
        for g in range(2):
            for c in range(2):
                lo, hi = (g * 4 + c) * group, (g * 4 + 2 + c) * group
                at = c * parts * quarter + n * group
                rows = []
                for half in halves:
                    even, odd = half[lo : lo + group], half[hi : hi + group]
                    even = jnp.where(upper, even[:, :LANES], even[:, LANES:])
                    odd = jnp.where(upper, odd[:, :LANES], odd[:, LANES:])
                    rows.append([jnp.where(folded_diagonal, x, 0.0) for x in (even + odd, even - odd)])
                for h in range(2):
                    both = jnp.concatenate([row[h] for row in rows], axis=0).astype(jnp.bfloat16)
                    kept_ref[g, at : at + 2 * group, h * LANES : (h + 1) * LANES] = both

    steps = [(n, d) for n in range(groups) for d in range(2)]
    left, analysed, partial = None, {}, {}
    for i in range(len(steps) + 2):
        if i < len(steps):
            n, d = steps[i]
            left = spread(n) if d == 0 else left
            analysed[i] = dot(left, table(n, d))
        if 1 <= i <= len(steps):
            n, d = steps[i - 1]
            value = respond(n, d, analysed.pop(i - 1))
            partial[n] = value if d == 0 else partial[n] + value
        if i >= 5 and i % 4 == 1:
            n = (i - 5) // 2
            keep_pair(n, [partial.pop(n), partial.pop(n + 1)])

    total = dot_nt(put_ref[0], kept_ref[0]) + dot_nt(put_ref[1], kept_ref[1])
    total = total.astype(out_ref.dtype)
    lon_count = out_ref.shape[0] // owners
    rows = out_ref.shape[1]
    for b in range(owners):
        for q in range(lon_count):
            out_ref[b * lon_count + q] = total[b * rows : (b + 1) * rows]


def synthesise_grid(turn_ref, basis_ref, values_ref, out_ref, left_ref):
    owners, blocks, per_owner = turn_ref.shape[1:]
    lon_count = values_ref.shape[0] // owners
    rows = values_ref.shape[1]
    cycles = out_ref.shape[2]
    count = owners * per_owner
    height = blocks * rows
    first_lanes = iota((1, LANES), 1) < per_owner // 2
    for b in range(owners):
        halves = []
        for c in range(2):
            value = values_ref[b * lon_count + c].astype(jnp.float32)
            for q in range(c + 2, lon_count, 2):
                value = value + values_ref[b * lon_count + q].astype(jnp.float32)
            halves.append(value)
        re = jnp.where(first_lanes, halves[0], pltpu.roll(halves[1], per_owner // 2, 1))
        im = jnp.where(first_lanes, pltpu.roll(halves[0], per_owner // 2, 1), halves[1])
        at = b * per_owner
        for a in range(blocks):
            ca, sa = turn_ref[0, b, a : a + 1], turn_ref[1, b, a : a + 1]
            for c, term in ((0, ca * re - sa * im), (1, -(sa * re + ca * im))):
                high, low = split(term)
                lanes = slice(c * count + at, c * count + at + per_owner)
                left_ref[a * rows : (a + 1) * rows, lanes] = high
                left_ref[height + a * rows : height + (a + 1) * rows, lanes] = low
    grid = dot_nt(left_ref[...], basis_ref[...])
    grid = grid[:height] + grid[height:]
    for a in range(blocks):
        for g in range(2):
            for h in range(2):
                at = a * rows + (g * 2 + h) * cycles
                out_ref[g, h, :, a * LANES : (a + 1) * LANES] = grid[at : at + cycles]


def fits(owners, lon_count, cycles, points, per_owner, degrees):
    northern = owners * cycles
    total = points * lon_count
    return (
        per_owner == LANES
        and 4 * per_owner == lon_count * LANES
        and lon_count % 2 == 0
        and 2 * cycles == ROWS
        and 4 * northern == LANES
        and ROWS * northern == degrees
        and degrees % LANES == 0
        and owners == ROWS
        and points % LANES == 0
        and total & (total - 1) == 0
        and owners * per_owner * LANES < 1 << 24
    )


def per_device_kernels(loads, legendre, love, cycle_weight, order_list, cycle_order):
    owners = lax.axis_size("band")
    lon_count = lax.axis_size("lon")
    cycles, points = loads.shape[2], loads.shape[3]
    per_owner, degrees, northern = legendre.shape
    total = points * lon_count
    devices = owners * lon_count
    blocks = points // LANES
    everyone = ("band", "lon")
    vmem = pl.BlockSpec(memory_space=pltpu.VMEM)
    table = order_list.reshape(owners, per_owner)
    cycle_list = cycle_order.reshape(1, northern)

    def kernel(body, out_shape, in_specs, scratch_shapes, flops):
        return pl.pallas_call(
            body,
            out_shape=out_shape,
            in_specs=in_specs,
            out_specs=jax.tree.map(lambda _: vmem, out_shape),
            scratch_shapes=scratch_shapes,
            compiler_params=pltpu.CompilerParams(vmem_limit_bytes=VMEM_LIMIT),
            cost_estimate=pl.CostEstimate(flops=flops, bytes_accessed=1 << 20, transcendentals=0),
        )

    partner = [(i, i ^ 1) for i in range(lon_count)]
    rows = jnp.transpose(legendre, (0, 2, 1)).reshape(per_owner * northern, degrees)
    parts = [loads, lax.ppermute(loads, "lon", partner)]
    other_rows = lax.ppermute(rows, "lon", partner)
    other_love = lax.ppermute(love, "lon", partner)
    count = 2 * blocks
    width = owners * per_owner // 2
    opened = kernel(opening, jax.ShapeDtypeStruct((ROWS, LANES), jnp.float32), [], [], 1 << 34)()
    right, first = kernel(
        functools.partial(forward_tables, blocks, total),
        (
            jax.ShapeDtypeStruct((3 * LANES, 2 * width), jnp.bfloat16),
            jax.ShapeDtypeStruct((2, count, width), jnp.float32),
        ),
        [vmem, vmem],
        [],
        1 << 34,
    )(table, opened)
    order_rows, turns, basis = kernel(
        functools.partial(inverse_tables, total),
        (
            jax.ShapeDtypeStruct((per_owner, LANES), jnp.int32),
            jax.ShapeDtypeStruct((2, owners, blocks, per_owner), jnp.float32),
            jax.ShapeDtypeStruct((LANES, 2 * owners * per_owner), jnp.bfloat16),
        ),
        [vmem, vmem],
        [],
        1 << 20,
    )(table, first)
    pick, put = kernel(
        functools.partial(cycle_tables, owners, cycles),
        (
            jax.ShapeDtypeStruct((2 * LANES, LANES), jnp.bfloat16),
            jax.ShapeDtypeStruct((2, LANES, 2 * LANES), jnp.bfloat16),
        ),
        [vmem, vmem],
        [],
        1 << 20,
    )(order_rows, cycle_list)
    sums = kernel(
        functools.partial(analyse_grid, total),
        jax.ShapeDtypeStruct((devices, 2 * cycles, LANES), jnp.float32),
        [vmem] * (5 + len(parts)),
        [
            pltpu.VMEM((count * 4 * cycles, LANES), jnp.float32),
            pltpu.VMEM((count * 4 * cycles, 2 * width), jnp.float32),
        ],
        1 << 24,
    )(pick, right, first, cycle_weight.reshape(1, northern), cycle_list, *parts)
    arrived = lax.all_to_all(sums, everyone, split_axis=0, concat_axis=0, tiled=True)
    folded = kernel(
        add_points,
        jax.ShapeDtypeStruct((2, owners, 2 * cycles, LANES), jnp.bfloat16),
        [vmem],
        [],
        1 << 28,
    )(arrived)
    values = kernel(
        spectral,
        jax.ShapeDtypeStruct((devices, 4 * cycles, per_owner), jnp.bfloat16),
        [vmem] * 8,
        [
            pltpu.VMEM((2 * LANES, 2 * LANES), jnp.float32),
            pltpu.VMEM((2, per_owner, 2 * LANES), jnp.bfloat16),
        ],
        1 << 31,
    )(pick, put, order_rows, folded, rows, other_rows, love, other_love)
    returned = lax.all_to_all(values, everyone, split_axis=0, concat_axis=0, tiled=True)

    return kernel(
        synthesise_grid,
        jax.ShapeDtypeStruct(loads.shape, jnp.float32),
        [vmem] * 3,
        [pltpu.VMEM((2 * 4 * cycles * blocks, 2 * owners * per_owner), jnp.bfloat16)],
        1 << 31,
    )(turns, basis, returned)


def per_device(loads, legendre, love, cycle_weight, order_list, cycle_order):
    sizes = (lax.axis_size("band"), lax.axis_size("lon"), loads.shape[2], loads.shape[3], legendre.shape[0], legendre.shape[1])
    form = per_device_kernels if fits(*sizes) else per_device_plain
    return form(loads, legendre, love, cycle_weight, order_list, cycle_order)


def cycle_basis(order_ids, positions, total):
    phase = positions[:, None] * order_ids[None, :] % total
    angle = phase.astype(jnp.float32) * (2.0 * math.pi / total)
    scale = 1.0 / math.sqrt(total)
    return (jnp.cos(angle) * scale, jnp.sin(angle) * scale)


def per_device_plain(loads, legendre, love, cycle_weight, order_list, cycle_order):
    highest = lax.Precision.HIGHEST
    owners = lax.axis_size("band")
    lon_count = lax.axis_size("lon")
    band_index = lax.axis_index("band")
    lon_index = lax.axis_index("lon")
    cycle_pairs = loads.shape[2]
    points = loads.shape[3]
    total = points * lon_count
    orders = order_list.shape[0]
    per_owner = legendre.shape[0]
    degree_count = legendre.shape[1]
    northern = legendre.shape[2]
    quarter = per_owner // lon_count
    positions = lon_index * points + jnp.arange(points, dtype=jnp.int32)
    cosine, sine = cycle_basis(order_list, positions, total)
    my_cycles = lax.dynamic_slice_in_dim(cycle_order, band_index * cycle_pairs, cycle_pairs)
    picker = my_cycles[:, None] == jnp.arange(northern, dtype=jnp.int32)[None, :]
    weights = jnp.sum(jnp.where(picker, cycle_weight[None, :], 0.0), axis=1)
    forward = jnp.stack([cosine, -sine], axis=1)
    spectrum = jnp.einsum("fhjx,xrm->fhjrm", loads, forward, precision=highest)
    spectrum = spectrum.reshape(2, 2, cycle_pairs, 2, owners, per_owner)
    summed = lax.psum_scatter(spectrum, "lon", scatter_dimension=5, tiled=True)
    cycle_scale = weights[None, :, None, None, None]
    symmetric = ((summed[:, 0] + summed[:, 1]) * cycle_scale).astype(jnp.bfloat16)
    antisym = ((summed[:, 0] - summed[:, 1]) * cycle_scale).astype(jnp.bfloat16)
    folded = jnp.stack([symmetric, antisym], axis=1)
    slot_width = folded.shape[5]
    outgoing = jnp.transpose(folded, (4, 5, 0, 1, 3, 2)).reshape(owners, slot_width, 8, cycle_pairs)
    arrived = lax.all_to_all(outgoing, "band", split_axis=0, concat_axis=3, tiled=True).reshape(
        slot_width, 8, northern
    )
    columns = lax.all_gather(arrived, "lon", axis=0, tiled=True)
    inverse_rows = jnp.argsort(cycle_order)
    columns_sorted = jnp.take(columns, inverse_rows, axis=2)
    my_orders = lax.dynamic_slice_in_dim(order_list, band_index * per_owner, per_owner)
    degrees = lon_index * degree_count + jnp.arange(degree_count, dtype=jnp.int32)
    analysed = jnp.einsum(
        "olk,ock->ocl", legendre, columns_sorted, preferred_element_type=jnp.float32
    )
    analysed = analysed.reshape(per_owner, 2, 2, 2, degree_count)
    even = (degrees[None, :] - my_orders[:, None]) % 2 == 0
    valid = degrees[None, :] >= my_orders[:, None]
    selected = jnp.where(even[:, None, None, :], analysed[:, :, 0], analysed[:, :, 1])
    selected = selected * valid[:, None, None, :].astype(jnp.float32)
    response = jnp.einsum("gfl,ofrl->ogrl", love, selected, precision=highest).astype(jnp.bfloat16)
    even_part = jnp.where((even & valid)[:, None, None, :], response, jnp.zeros_like(response))
    odd_part = jnp.where((~even & valid)[:, None, None, :], response, jnp.zeros_like(response))
    stacked = jnp.stack([even_part, odd_part], axis=2).reshape(per_owner, 8, degree_count)
    partial_sorted = jnp.einsum(
        "olk,ocl->ock", legendre, stacked, preferred_element_type=jnp.float32
    )
    partial_value = jnp.take(partial_sorted, cycle_order, axis=2)
    reduced = lax.psum_scatter(partial_value, "lon", scatter_dimension=0, tiled=True)
    returned = lax.all_to_all(reduced, "band", split_axis=2, concat_axis=0, tiled=True)
    gathered = lax.all_gather(returned[None], "lon", axis=0, tiled=True).reshape(
        orders, 8, cycle_pairs
    )
    slot_ids = jnp.transpose(order_list.reshape(owners, lon_count, quarter), (1, 0, 2)).reshape(
        orders
    )
    cosine_back, sine_back = cycle_basis(slot_ids, positions, total)
    pieces = gathered.reshape(orders, 2, 2, 2, cycle_pairs)
    cycle_values = jnp.stack(
        [pieces[:, :, 0] + pieces[:, :, 1], pieces[:, :, 0] - pieces[:, :, 1]], axis=2
    )
    factor = jnp.where(slot_ids == 0, 1.0, 2.0).astype(jnp.float32)
    inverse = jnp.stack([cosine_back.T, -sine_back.T], axis=0)
    scaled = cycle_values * factor[:, None, None, None, None]
    return jnp.einsum("sghrp,rsx->ghpx", scaled, inverse, precision=highest)


def solution(mesh):
    return jax.shard_map(
        per_device,
        mesh=mesh,
        in_specs=(
            P(None, None, "band", "lon"),
            P("band", "lon", None),
            P(None, None, "lon"),
            P(),
            P(),
            P(),
        ),
        out_specs=P(None, None, "band", "lon"),
        check_vma=False,
    )
```

```python
import functools
import math

import jax
import jax.numpy as jnp
from jax import lax
from jax.experimental import pallas as pl
from jax.experimental.pallas import tpu as pltpu
from jax.sharding import PartitionSpec as P


LANES = 128
ROWS = 8
VMEM_LIMIT = 12 << 20
NT = (((1,), (1,)), ((), ()))


def iota(shape, axis):
    return lax.broadcasted_iota(jnp.int32, shape, axis)


def turn(phase, total):
    shift = (total // 4).bit_length() - 1
    quadrant = (phase + total // 8) >> shift
    x = (phase - (quadrant << shift)).astype(jnp.float32) * (2.0 * math.pi / total)
    z = x * x
    s = ((-1.9515295891e-4 * z + 8.3321608736e-3) * z - 1.6666654611e-1) * z * x + x
    c = ((2.443315711809948e-5 * z - 1.388731625493765e-3) * z + 4.166664568298827e-2) * z * z
    c = c - 0.5 * z + 1.0
    odd = (quadrant & 1) == 1
    cosine = jnp.where(odd, s, c)
    sine = jnp.where(odd, c, s)
    cosine = jnp.where(((quadrant + 1) & 2) == 2, -cosine, cosine)
    sine = jnp.where((quadrant & 2) == 2, -sine, sine)
    return cosine, sine


def split(x):
    high = x.astype(jnp.bfloat16)
    return high, (x - high.astype(jnp.float32)).astype(jnp.bfloat16)


def dot(a, b):
    return jnp.dot(a, b, preferred_element_type=jnp.float32)


def dot_nt(a, b):
    return lax.dot_general(a, b, NT, preferred_element_type=jnp.float32)


def analyse_grid(total, after_ref, right_ref, turn_ref, weight_ref, cycle_ref, *refs):
    del after_ref
    parts, out_ref, points_ref, mid_ref = refs[:-3], refs[-3], refs[-2], refs[-1]
    cycles = parts[0].shape[2]
    blocks = parts[0].shape[3] // LANES
    count, width = turn_ref.shape[1:]
    owners = width // (LANES // 2)
    lon_count = out_ref.shape[0] // owners
    quarter = width // owners // 2
    pieces = LANES // quarter
    step = 2 * cycles

    for q, part in enumerate(parts):
        for a in range(blocks):
            for f in range(2):
                north = part[f, 0, :, a * LANES : (a + 1) * LANES]
                south = part[f, 1, :, a * LANES : (a + 1) * LANES]
                at = ((q * blocks + a) * 2 + f) * step
                points_ref[at : at + step] = jnp.concatenate([north + south, north - south], axis=0)
    high, low = split(points_ref[...])
    left = jnp.concatenate([high, low, high], axis=1)
    tiles = [slice(t * LANES, (t + 1) * LANES) for t in range(width // LANES)]
    for t, lanes in enumerate(tiles):
        sine = slice(width + t * LANES, width + (t + 1) * LANES)
        right = jnp.concatenate([right_ref[:, lanes], right_ref[:, sine]], axis=1)
        mid_ref[:, 2 * t * LANES : 2 * (t + 1) * LANES] = dot(left, right)

    sums = []
    for t, lanes in enumerate(tiles):
        parts_of = [[jnp.zeros((step, LANES), jnp.float32) for _ in range(2)] for _ in range(2)]
        for a in range(count):
            ca, sa = turn_ref[0, a : a + 1, lanes], turn_ref[1, a : a + 1, lanes]
            for f in range(2):
                at = (a * 2 + f) * step
                tc = mid_ref[at : at + step, 2 * t * LANES : (2 * t + 1) * LANES]
                ts = mid_ref[at : at + step, (2 * t + 1) * LANES : 2 * (t + 1) * LANES]
                parts_of[f][0] = parts_of[f][0] + (ca * tc - sa * ts)
                parts_of[f][1] = parts_of[f][1] - (sa * tc + ca * ts)
        sums.append(parts_of)

    slot = iota((1, LANES), 1) // quarter
    northern = cycle_ref.shape[1]
    lane = iota((step, northern), 1)
    row = lax.axis_index("band") * cycles + iota((step, northern), 0) % cycles
    listed = jnp.sum(jnp.where(lane == row, cycle_ref[...].astype(jnp.float32), 0.0), axis=1, keepdims=True)
    weight = jnp.sum(jnp.where(lane == listed.astype(jnp.int32), weight_ref[...], 0.0), axis=1, keepdims=True)
    weight = weight * (1.0 / math.sqrt(total))
    for owner in range(owners):
        for side in range(2):
            t, i = (2 * owner + side) // pieces, (2 * owner + side) % pieces
            block = None
            for e in range(4):
                piece = sums[t][e // 2][e % 2]
                move = (e - i) * quarter % LANES
                piece = pltpu.roll(piece, move, 1) if move else piece
                block = piece if block is None else jnp.where(slot == e, piece, block)
            block = block * weight
            for q in range(side, lon_count, 2):
                out_ref[owner * lon_count + q] = block


def add_points(parts_ref, out_ref):
    sides, owners = out_ref.shape[:2]
    lon_count = parts_ref.shape[0] // owners
    for c in range(sides):
        for b in range(owners):
            value = parts_ref[b * lon_count + c]
            for q in range(c + sides, lon_count, sides):
                value = value + parts_ref[b * lon_count + q]
            out_ref[c, b] = value.astype(out_ref.dtype)


def products(fine, coarse):
    for k in range(coarse[0].shape[0]):
        cc, cs = coarse[0][k : k + 1], coarse[1][k : k + 1]
        yield fine[0] * cc - fine[1] * cs, fine[1] * cc + fine[0] * cs


def opening(out_ref):
    out_ref[...] = jnp.zeros_like(out_ref)


def forward_tables(blocks, total, orders_ref, after_ref, right_ref, first_ref):
    del after_ref
    owners, per_owner = orders_ref.shape
    share = per_owner // 2
    lon = lax.axis_index("lon")
    side = lon % 2
    first_lanes = iota((1, LANES), 1) < share

    mine = pltpu.roll(orders_ref[...], (LANES - share * side) % LANES, 1)
    moved = pltpu.roll(mine, share, 1)
    orders = jnp.concatenate(
        [jnp.where(first_lanes, mine[b : b + 1], moved[b + 1 : b + 2]) for b in range(0, owners, 2)], axis=1
    )
    width = orders.shape[1]
    fine = turn(iota((ROWS, width), 0) * orders, total)
    coarse = turn((iota((LANES // ROWS, width), 0) * ROWS * orders) & (total - 1), total)
    kept = []
    for k, pair in enumerate(products(fine, coarse)):
        kept.append([split(table) for table in pair])
        if k % 2 == 0:
            continue
        for c in range(2):
            high, low = [jnp.concatenate([kept[k - 1][c][i], kept[k][c][i]], axis=0) for i in range(2)]
            for i, value in enumerate((high, high, low)):
                at = i * LANES + (k - 1) * ROWS
                right_ref[at : at + 2 * ROWS, c * width : (c + 1) * width] = value
    for k in range(2):
        origin = lon if k == 0 else lon + 1 - 2 * side
        step = iota((blocks, width), 0) + origin * blocks
        for c, table in enumerate(turn((step * LANES * orders) & (total - 1), total)):
            first_ref[c, k * blocks : (k + 1) * blocks] = table


def cycle_tables(owners, cycles, after_ref, cycle_ref, pick_ref, put_ref):
    del after_ref
    northern = owners * cycles
    lane = iota((1, LANES), 1)

    listed = jnp.broadcast_to(cycle_ref[...].astype(jnp.float32), (LANES, northern)).astype(jnp.bfloat16)
    index = iota((LANES, northern), 0)

    def places(repeat):
        place = index // (repeat * cycles) * cycles + index % cycles
        return jnp.where(place == iota((LANES, northern), 1), 1.0, 0.0).astype(jnp.bfloat16)

    arriving = dot_nt(listed[: 2 * ROWS], places(2))[:1].astype(jnp.int32)
    found = (iota((northern, LANES), 0) == arriving) & (lane < 2 * northern)
    for p in range(2):
        one = jnp.where(found & (lane // cycles % 2 == p), 1.0, 0.0)
        copies = jnp.concatenate([one] * (LANES // northern), axis=0)
        pick_ref[p * LANES : (p + 1) * LANES] = copies.astype(jnp.bfloat16)
    leaving = dot_nt(places(4), listed).astype(jnp.int32)
    found = leaving == iota((LANES, LANES), 1) % northern
    part = iota((LANES, LANES), 0) // cycles % 4
    for i in range(4):
        put = jnp.where(found & (part == i), 1.0, 0.0)
        put_ref[i // 2, :, i % 2 * LANES : (i % 2 + 1) * LANES] = put.astype(jnp.bfloat16)


def inverse_tables(total, orders_ref, after_ref, rows_ref, turn_ref, basis_ref):
    del after_ref
    owners, per_owner = orders_ref.shape
    blocks = turn_ref.shape[2]
    quarter = per_owner // 4
    lon = lax.axis_index("lon")
    own = orders_ref[pl.ds(lax.axis_index("band"), 1), :].astype(jnp.float32)
    rows_ref[...] = jnp.transpose(jnp.broadcast_to(own, (LANES, per_owner))).astype(jnp.int32)

    slot = iota((1, LANES), 1) // quarter
    orders = orders_ref[...]
    ahead, behind = pltpu.roll(orders, LANES - quarter, 1), pltpu.roll(orders, quarter, 1)
    arranged = jnp.where(slot == 1, ahead, jnp.where(slot == 2, behind, orders))
    scale = 1.0 / math.sqrt(total)
    for b in range(owners):
        order = arranged[b : b + 1]
        factor = jnp.where(order == 0, scale, 2.0 * scale)
        step = iota((blocks, per_owner), 0) + lon * blocks
        for c, table in enumerate(turn((step * LANES * order) & (total - 1), total)):
            turn_ref[c, b] = table * factor
        fine = turn(iota((ROWS, per_owner), 0) * order, total)
        coarse = turn((iota((LANES // ROWS, per_owner), 0) * ROWS * order) & (total - 1), total)
        kept = []
        for k, pair in enumerate(products(fine, coarse)):
            kept.append(pair)
            if k % 2 == 1:
                rows = slice((k - 1) * ROWS, (k + 1) * ROWS)
                for c in range(2):
                    at = (b * 2 + c) * per_owner
                    both = jnp.concatenate([kept[k - 1][c], kept[k][c]], axis=0)
                    basis_ref[rows, at : at + per_owner] = both.astype(basis_ref.dtype)


def spectral(
    pick_ref,
    put_ref,
    rows_ref,
    folded_ref,
    own_table_ref,
    other_table_ref,
    own_love_ref,
    other_love_ref,
    out_ref,
    spread_ref,
    kept_ref,
):
    parts, owners, height = folded_ref.shape[:3]
    quarter = rows_ref.shape[0] // (2 * parts)
    degrees = own_table_ref.shape[1]
    northern = owners * height // 2
    group = degrees // northern
    wide = group * northern
    lon = lax.axis_index("lon")
    side = lon % 2

    pad = jnp.zeros((LANES - 2 * northern, LANES), jnp.float32)
    turned = []
    for q in range(parts):
        pieces = [folded_ref[q, b].astype(jnp.float32) for b in range(owners)]
        turned.append(jnp.transpose(jnp.concatenate(pieces + [pad], axis=0)))
    spread_ref[...] = dot_nt(jnp.concatenate(turned, axis=0).astype(jnp.bfloat16), pick_ref[...])

    lane = iota((ROWS, degrees), 1)
    degree = [lon * degrees + lane, (lon + 1 - 2 * side) * degrees + lane]
    tables = [own_table_ref, other_table_ref]
    love = [[[ref[g, f : f + 1, :] for f in range(2)] for g in range(2)] for ref in (own_love_ref, other_love_ref)]
    diagonal = iota((ROWS, wide), 0) == iota((ROWS, wide), 1) // northern
    across = LANES // northern
    upper = iota((ROWS, LANES), 0) < across
    folded_diagonal = iota((ROWS, LANES), 0) % across == iota((ROWS, LANES), 1) // northern
    groups = parts * quarter // group

    def first_order(n):
        q, first = n * group // quarter, n * group % quarter
        return (2 * q + side) * quarter + first

    def table(n, d):
        return tables[d][pl.ds(pl.multiple_of(first_order(n) * northern, wide), wide)]

    def spread(n):
        q, first = n * group // quarter, n * group % quarter
        left = []
        for f in range(2):
            for p in range(2):
                for c in range(2):
                    at = q * LANES + (f * 2 + c) * quarter + first
                    piece = spread_ref[at : at + group, p * LANES : (p + 1) * LANES]
                    left.append(jnp.where(diagonal, jnp.concatenate([piece] * (wide // LANES), axis=1), 0.0))
        return jnp.concatenate(left, axis=0).astype(jnp.bfloat16)

    def respond(n, d, analysed):
        order = rows_ref[pl.ds(pl.multiple_of(first_order(n), group), group)]
        gap = degree[d] - jnp.concatenate([order] * (degrees // LANES), axis=1)
        valid = gap >= 0
        keep = [valid & ((gap & 1) == p) for p in range(2)]
        mixed = []
        for g in range(2):
            for p in range(2):
                for c in range(2):
                    lo = (p * 2 + c) * group
                    hi = ((2 + p) * 2 + c) * group
                    value = love[d][g][0] * analysed[lo : lo + group] + love[d][g][1] * analysed[hi : hi + group]
                    mixed.append(jnp.where(keep[p], value, 0.0))
        return dot_nt(jnp.concatenate(mixed, axis=0).astype(jnp.bfloat16), table(n, d))

    def keep_pair(n, halves):
        for g in range(2):
            for c in range(2):
                lo, hi = (g * 4 + c) * group, (g * 4 + 2 + c) * group
                at = c * parts * quarter + n * group
                rows = []
                for half in halves:
                    even, odd = half[lo : lo + group], half[hi : hi + group]
                    even = jnp.where(upper, even[:, :LANES], even[:, LANES:])
                    odd = jnp.where(upper, odd[:, :LANES], odd[:, LANES:])
                    rows.append([jnp.where(folded_diagonal, x, 0.0) for x in (even + odd, even - odd)])
                for h in range(2):
                    both = jnp.concatenate([row[h] for row in rows], axis=0).astype(jnp.bfloat16)
                    kept_ref[g, at : at + 2 * group, h * LANES : (h + 1) * LANES] = both

    steps = [(n, d) for n in range(groups) for d in range(2)]
    left, analysed, partial = None, {}, {}
    for i in range(len(steps) + 3):
        if i < len(steps):
            n, d = steps[i]
            left = spread(n) if d == 0 else left
            analysed[i] = dot(left, table(n, d))
        if 2 <= i < len(steps) + 2:
            n, d = steps[i - 2]
            value = respond(n, d, analysed.pop(i - 2))
            partial[n] = value if d == 0 else partial[n] + value
        if i >= 6 and i % 4 == 2:
            n = (i - 6) // 2
            keep_pair(n, [partial.pop(n), partial.pop(n + 1)])

    total = dot_nt(put_ref[0], kept_ref[0]) + dot_nt(put_ref[1], kept_ref[1])
    total = total.astype(out_ref.dtype)
    lon_count = out_ref.shape[0] // owners
    rows = out_ref.shape[1]
    for b in range(owners):
        for q in range(lon_count):
            out_ref[b * lon_count + q] = total[b * rows : (b + 1) * rows]


def synthesise_grid(turn_ref, basis_ref, values_ref, out_ref, left_ref):
    owners, blocks, per_owner = turn_ref.shape[1:]
    lon_count = values_ref.shape[0] // owners
    rows = values_ref.shape[1]
    cycles = out_ref.shape[2]
    height = blocks * rows
    first_lanes = iota((1, LANES), 1) < per_owner // 2
    for b in range(owners):
        halves = []
        for c in range(2):
            value = values_ref[b * lon_count + c].astype(jnp.float32)
            for q in range(c + 2, lon_count, 2):
                value = value + values_ref[b * lon_count + q].astype(jnp.float32)
            halves.append(value)
        re = jnp.where(first_lanes, halves[0], pltpu.roll(halves[1], per_owner // 2, 1))
        im = jnp.where(first_lanes, pltpu.roll(halves[0], per_owner // 2, 1), halves[1])
        at = 2 * b * per_owner
        for a in range(blocks):
            ca, sa = turn_ref[0, b, a : a + 1], turn_ref[1, b, a : a + 1]
            for c, term in ((0, ca * re - sa * im), (1, -(sa * re + ca * im))):
                high, low = split(term)
                lanes = slice(at + c * per_owner, at + (c + 1) * per_owner)
                left_ref[a * rows : (a + 1) * rows, lanes] = high
                left_ref[height + a * rows : height + (a + 1) * rows, lanes] = low
    grid = None
    for b in range(owners):
        lanes = slice(2 * b * per_owner, 2 * (b + 1) * per_owner)
        term = dot_nt(left_ref[:, lanes], basis_ref[:, lanes])
        grid = term if grid is None else grid + term
    grid = grid[:height] + grid[height:]
    for a in range(blocks):
        for g in range(2):
            for h in range(2):
                at = a * rows + (g * 2 + h) * cycles
                out_ref[g, h, :, a * LANES : (a + 1) * LANES] = grid[at : at + cycles]


def fits(owners, lon_count, cycles, points, per_owner, degrees):
    northern = owners * cycles
    total = points * lon_count
    return (
        per_owner == LANES
        and 4 * per_owner == lon_count * LANES
        and lon_count % 2 == 0
        and 2 * cycles == ROWS
        and 4 * northern == LANES
        and ROWS * northern == degrees
        and degrees % LANES == 0
        and owners == ROWS
        and points % LANES == 0
        and total & (total - 1) == 0
        and owners * per_owner * LANES < 1 << 24
    )


def per_device_kernels(loads, legendre, love, cycle_weight, order_list, cycle_order):
    owners = lax.axis_size("band")
    lon_count = lax.axis_size("lon")
    cycles, points = loads.shape[2], loads.shape[3]
    per_owner, degrees, northern = legendre.shape
    total = points * lon_count
    devices = owners * lon_count
    blocks = points // LANES
    everyone = ("band", "lon")
    vmem = pl.BlockSpec(memory_space=pltpu.VMEM)
    table = order_list.reshape(owners, per_owner)
    cycle_list = cycle_order.reshape(1, northern)

    def kernel(body, out_shape, in_specs, scratch_shapes, flops):
        return pl.pallas_call(
            body,
            out_shape=out_shape,
            in_specs=in_specs,
            out_specs=jax.tree.map(lambda _: vmem, out_shape),
            scratch_shapes=scratch_shapes,
            compiler_params=pltpu.CompilerParams(vmem_limit_bytes=VMEM_LIMIT),
            cost_estimate=pl.CostEstimate(flops=flops, bytes_accessed=1 << 20, transcendentals=0),
        )

    partner = [(i, i ^ 1) for i in range(lon_count)]
    rows = jnp.transpose(legendre, (0, 2, 1)).reshape(per_owner * northern, degrees)
    parts = [loads, lax.ppermute(loads, "lon", partner)]
    other_rows = lax.ppermute(rows, "lon", partner)
    other_love = lax.ppermute(love, "lon", partner)
    count = 2 * blocks
    width = owners * per_owner // 2
    opened = kernel(opening, jax.ShapeDtypeStruct((ROWS, LANES), jnp.float32), [], [], 1 << 34)()
    right, first = kernel(
        functools.partial(forward_tables, blocks, total),
        (
            jax.ShapeDtypeStruct((3 * LANES, 2 * width), jnp.bfloat16),
            jax.ShapeDtypeStruct((2, count, width), jnp.float32),
        ),
        [vmem, vmem],
        [],
        1 << 34,
    )(table, opened)
    order_rows, turns, basis = kernel(
        functools.partial(inverse_tables, total),
        (
            jax.ShapeDtypeStruct((per_owner, LANES), jnp.int32),
            jax.ShapeDtypeStruct((2, owners, blocks, per_owner), jnp.float32),
            jax.ShapeDtypeStruct((LANES, 2 * owners * per_owner), jnp.bfloat16),
        ),
        [vmem, vmem],
        [],
        1 << 20,
    )(table, first)
    pick, put = kernel(
        functools.partial(cycle_tables, owners, cycles),
        (
            jax.ShapeDtypeStruct((2 * LANES, LANES), jnp.bfloat16),
            jax.ShapeDtypeStruct((2, LANES, 2 * LANES), jnp.bfloat16),
        ),
        [vmem, vmem],
        [],
        1 << 20,
    )(order_rows, cycle_list)
    sums = kernel(
        functools.partial(analyse_grid, total),
        jax.ShapeDtypeStruct((devices, 2 * cycles, LANES), jnp.float32),
        [vmem] * (5 + len(parts)),
        [
            pltpu.VMEM((count * 4 * cycles, LANES), jnp.float32),
            pltpu.VMEM((count * 4 * cycles, 2 * width), jnp.float32),
        ],
        1 << 24,
    )(pick, right, first, cycle_weight.reshape(1, northern), cycle_list, *parts)
    arrived = lax.all_to_all(sums, everyone, split_axis=0, concat_axis=0, tiled=True)
    folded = kernel(
        add_points,
        jax.ShapeDtypeStruct((2, owners, 2 * cycles, LANES), jnp.bfloat16),
        [vmem],
        [],
        1 << 28,
    )(arrived)
    values = kernel(
        spectral,
        jax.ShapeDtypeStruct((devices, 4 * cycles, per_owner), jnp.bfloat16),
        [vmem] * 8,
        [
            pltpu.VMEM((2 * LANES, 2 * LANES), jnp.float32),
            pltpu.VMEM((2, per_owner, 2 * LANES), jnp.bfloat16),
        ],
        1 << 31,
    )(pick, put, order_rows, folded, rows, other_rows, love, other_love)
    returned = lax.all_to_all(values, everyone, split_axis=0, concat_axis=0, tiled=True)

    return kernel(
        synthesise_grid,
        jax.ShapeDtypeStruct(loads.shape, jnp.float32),
        [vmem] * 3,
        [pltpu.VMEM((2 * 4 * cycles * blocks, 2 * owners * per_owner), jnp.bfloat16)],
        1 << 31,
    )(turns, basis, returned)


def per_device(loads, legendre, love, cycle_weight, order_list, cycle_order):
    sizes = (lax.axis_size("band"), lax.axis_size("lon"), loads.shape[2], loads.shape[3], legendre.shape[0], legendre.shape[1])
    form = per_device_kernels if fits(*sizes) else per_device_plain
    return form(loads, legendre, love, cycle_weight, order_list, cycle_order)


def cycle_basis(order_ids, positions, total):
    phase = positions[:, None] * order_ids[None, :] % total
    angle = phase.astype(jnp.float32) * (2.0 * math.pi / total)
    scale = 1.0 / math.sqrt(total)
    return (jnp.cos(angle) * scale, jnp.sin(angle) * scale)


def per_device_plain(loads, legendre, love, cycle_weight, order_list, cycle_order):
    highest = lax.Precision.HIGHEST
    owners = lax.axis_size("band")
    lon_count = lax.axis_size("lon")
    band_index = lax.axis_index("band")
    lon_index = lax.axis_index("lon")
    cycle_pairs = loads.shape[2]
    points = loads.shape[3]
    total = points * lon_count
    orders = order_list.shape[0]
    per_owner = legendre.shape[0]
    degree_count = legendre.shape[1]
    northern = legendre.shape[2]
    quarter = per_owner // lon_count
    positions = lon_index * points + jnp.arange(points, dtype=jnp.int32)
    cosine, sine = cycle_basis(order_list, positions, total)
    my_cycles = lax.dynamic_slice_in_dim(cycle_order, band_index * cycle_pairs, cycle_pairs)
    picker = my_cycles[:, None] == jnp.arange(northern, dtype=jnp.int32)[None, :]
    weights = jnp.sum(jnp.where(picker, cycle_weight[None, :], 0.0), axis=1)
    forward = jnp.stack([cosine, -sine], axis=1)
    spectrum = jnp.einsum("fhjx,xrm->fhjrm", loads, forward, precision=highest)
    spectrum = spectrum.reshape(2, 2, cycle_pairs, 2, owners, per_owner)
    summed = lax.psum_scatter(spectrum, "lon", scatter_dimension=5, tiled=True)
    cycle_scale = weights[None, :, None, None, None]
    symmetric = ((summed[:, 0] + summed[:, 1]) * cycle_scale).astype(jnp.bfloat16)
    antisym = ((summed[:, 0] - summed[:, 1]) * cycle_scale).astype(jnp.bfloat16)
    folded = jnp.stack([symmetric, antisym], axis=1)
    slot_width = folded.shape[5]
    outgoing = jnp.transpose(folded, (4, 5, 0, 1, 3, 2)).reshape(owners, slot_width, 8, cycle_pairs)
    arrived = lax.all_to_all(outgoing, "band", split_axis=0, concat_axis=3, tiled=True).reshape(
        slot_width, 8, northern
    )
    columns = lax.all_gather(arrived, "lon", axis=0, tiled=True)
    inverse_rows = jnp.argsort(cycle_order)
    columns_sorted = jnp.take(columns, inverse_rows, axis=2)
    my_orders = lax.dynamic_slice_in_dim(order_list, band_index * per_owner, per_owner)
    degrees = lon_index * degree_count + jnp.arange(degree_count, dtype=jnp.int32)
    analysed = jnp.einsum(
        "olk,ock->ocl", legendre, columns_sorted, preferred_element_type=jnp.float32
    )
    analysed = analysed.reshape(per_owner, 2, 2, 2, degree_count)
    even = (degrees[None, :] - my_orders[:, None]) % 2 == 0
    valid = degrees[None, :] >= my_orders[:, None]
    selected = jnp.where(even[:, None, None, :], analysed[:, :, 0], analysed[:, :, 1])
    selected = selected * valid[:, None, None, :].astype(jnp.float32)
    response = jnp.einsum("gfl,ofrl->ogrl", love, selected, precision=highest).astype(jnp.bfloat16)
    even_part = jnp.where((even & valid)[:, None, None, :], response, jnp.zeros_like(response))
    odd_part = jnp.where((~even & valid)[:, None, None, :], response, jnp.zeros_like(response))
    stacked = jnp.stack([even_part, odd_part], axis=2).reshape(per_owner, 8, degree_count)
    partial_sorted = jnp.einsum(
        "olk,ocl->ock", legendre, stacked, preferred_element_type=jnp.float32
    )
    partial_value = jnp.take(partial_sorted, cycle_order, axis=2)
    reduced = lax.psum_scatter(partial_value, "lon", scatter_dimension=0, tiled=True)
    returned = lax.all_to_all(reduced, "band", split_axis=2, concat_axis=0, tiled=True)
    gathered = lax.all_gather(returned[None], "lon", axis=0, tiled=True).reshape(
        orders, 8, cycle_pairs
    )
    slot_ids = jnp.transpose(order_list.reshape(owners, lon_count, quarter), (1, 0, 2)).reshape(
        orders
    )
    cosine_back, sine_back = cycle_basis(slot_ids, positions, total)
    pieces = gathered.reshape(orders, 2, 2, 2, cycle_pairs)
    cycle_values = jnp.stack(
        [pieces[:, :, 0] + pieces[:, :, 1], pieces[:, :, 0] - pieces[:, :, 1]], axis=2
    )
    factor = jnp.where(slot_ids == 0, 1.0, 2.0).astype(jnp.float32)
    inverse = jnp.stack([cosine_back.T, -sine_back.T], axis=0)
    scaled = cycle_values * factor[:, None, None, None, None]
    return jnp.einsum("sghrp,rsx->ghpx", scaled, inverse, precision=highest)


def solution(mesh):
    return jax.shard_map(
        per_device,
        mesh=mesh,
        in_specs=(
            P(None, None, "band", "lon"),
            P("band", "lon", None),
            P(None, None, "lon"),
            P(),
            P(),
            P(),
        ),
        out_specs=P(None, None, "band", "lon"),
        check_vma=False,
    )
```

```python
import functools
import math

import jax
import jax.numpy as jnp
from jax import lax
from jax.experimental import pallas as pl
from jax.experimental.pallas import tpu as pltpu
from jax.sharding import PartitionSpec as P


LANES = 128
ROWS = 8
VMEM_LIMIT = 12 << 20
NT = (((1,), (1,)), ((), ()))


def iota(shape, axis):
    return lax.broadcasted_iota(jnp.int32, shape, axis)


def turn(phase, total):
    shift = (total // 4).bit_length() - 1
    quadrant = (phase + total // 8) >> shift
    x = (phase - (quadrant << shift)).astype(jnp.float32) * (2.0 * math.pi / total)
    z = x * x
    s = ((-1.9515295891e-4 * z + 8.3321608736e-3) * z - 1.6666654611e-1) * z * x + x
    c = ((2.443315711809948e-5 * z - 1.388731625493765e-3) * z + 4.166664568298827e-2) * z * z
    c = c - 0.5 * z + 1.0
    odd = (quadrant & 1) == 1
    cosine = jnp.where(odd, s, c)
    sine = jnp.where(odd, c, s)
    cosine = jnp.where(((quadrant + 1) & 2) == 2, -cosine, cosine)
    sine = jnp.where((quadrant & 2) == 2, -sine, sine)
    return cosine, sine


def split(x):
    high = x.astype(jnp.bfloat16)
    return high, (x - high.astype(jnp.float32)).astype(jnp.bfloat16)


def dot(a, b):
    return jnp.dot(a, b, preferred_element_type=jnp.float32)


def dot_nt(a, b):
    return lax.dot_general(a, b, NT, preferred_element_type=jnp.float32)


def analyse_grid(total, after_ref, right_ref, turn_ref, weight_ref, cycle_ref, *refs):
    del after_ref
    parts, out_ref, points_ref, mid_ref = refs[:-3], refs[-3], refs[-2], refs[-1]
    cycles = parts[0].shape[2]
    blocks = parts[0].shape[3] // LANES
    count, width = turn_ref.shape[1:]
    owners = width // (LANES // 2)
    lon_count = out_ref.shape[0] // owners
    quarter = width // owners // 2
    pieces = LANES // quarter
    step = 2 * cycles

    for q, part in enumerate(parts):
        for a in range(blocks):
            for f in range(2):
                north = part[f, 0, :, a * LANES : (a + 1) * LANES]
                south = part[f, 1, :, a * LANES : (a + 1) * LANES]
                at = ((q * blocks + a) * 2 + f) * step
                points_ref[at : at + step] = jnp.concatenate([north + south, north - south], axis=0)
    high, low = split(points_ref[...])
    left = jnp.concatenate([high, low, high], axis=1)
    tiles = [slice(t * LANES, (t + 1) * LANES) for t in range(width // LANES)]
    for t, lanes in enumerate(tiles):
        sine = slice(width + t * LANES, width + (t + 1) * LANES)
        right = jnp.concatenate([right_ref[:, lanes], right_ref[:, sine]], axis=1)
        mid_ref[:, 2 * t * LANES : 2 * (t + 1) * LANES] = dot(left, right)

    sums = []
    for t, lanes in enumerate(tiles):
        parts_of = [[jnp.zeros((step, LANES), jnp.float32) for _ in range(2)] for _ in range(2)]
        for a in range(count):
            ca, sa = turn_ref[0, a : a + 1, lanes], turn_ref[1, a : a + 1, lanes]
            for f in range(2):
                at = (a * 2 + f) * step
                tc = mid_ref[at : at + step, 2 * t * LANES : (2 * t + 1) * LANES]
                ts = mid_ref[at : at + step, (2 * t + 1) * LANES : 2 * (t + 1) * LANES]
                parts_of[f][0] = parts_of[f][0] + (ca * tc - sa * ts)
                parts_of[f][1] = parts_of[f][1] - (sa * tc + ca * ts)
        sums.append(parts_of)

    slot = iota((1, LANES), 1) // quarter
    northern = cycle_ref.shape[1]
    lane = iota((step, northern), 1)
    row = lax.axis_index("band") * cycles + iota((step, northern), 0) % cycles
    listed = jnp.sum(jnp.where(lane == row, cycle_ref[...].astype(jnp.float32), 0.0), axis=1, keepdims=True)
    weight = jnp.sum(jnp.where(lane == listed.astype(jnp.int32), weight_ref[...], 0.0), axis=1, keepdims=True)
    weight = weight * (1.0 / math.sqrt(total))
    for owner in range(owners):
        for side in range(2):
            t, i = (2 * owner + side) // pieces, (2 * owner + side) % pieces
            block = None
            for e in range(4):
                piece = sums[t][e // 2][e % 2]
                move = (e - i) * quarter % LANES
                piece = pltpu.roll(piece, move, 1) if move else piece
                block = piece if block is None else jnp.where(slot == e, piece, block)
            block = block * weight
            for q in range(side, lon_count, 2):
                out_ref[owner * lon_count + q] = block


def add_points(parts_ref, out_ref):
    sides, owners = out_ref.shape[:2]
    lon_count = parts_ref.shape[0] // owners
    for c in range(sides):
        for b in range(owners):
            value = parts_ref[b * lon_count + c]
            for q in range(c + sides, lon_count, sides):
                value = value + parts_ref[b * lon_count + q]
            out_ref[c, b] = value.astype(out_ref.dtype)


def products(fine, coarse):
    for k in range(coarse[0].shape[0]):
        cc, cs = coarse[0][k : k + 1], coarse[1][k : k + 1]
        yield fine[0] * cc - fine[1] * cs, fine[1] * cc + fine[0] * cs


def opening(out_ref):
    out_ref[...] = jnp.zeros_like(out_ref)


def coarse_turns(orders, total):
    half = LANES // ROWS // 2
    c, s = turn((iota((half, orders.shape[1]), 0) * ROWS * orders) & (total - 1), total)
    last, one = slice(half - 1, half), slice(1, 2)
    rc, rs = c[last] * c[one] - s[last] * s[one], s[last] * c[one] + c[last] * s[one]
    return jnp.concatenate([c, c * rc - s * rs], axis=0), jnp.concatenate([s, s * rc + c * rs], axis=0)


def forward_tables(blocks, total, orders_ref, after_ref, right_ref, first_ref):
    del after_ref
    owners, per_owner = orders_ref.shape
    share = per_owner // 2
    lon = lax.axis_index("lon")
    side = lon % 2
    first_lanes = iota((1, LANES), 1) < share

    mine = pltpu.roll(orders_ref[...], (LANES - share * side) % LANES, 1)
    moved = pltpu.roll(mine, share, 1)
    orders = jnp.concatenate(
        [jnp.where(first_lanes, mine[b : b + 1], moved[b + 1 : b + 2]) for b in range(0, owners, 2)], axis=1
    )
    width = orders.shape[1]
    fine = turn(iota((ROWS, width), 0) * orders, total)
    coarse = coarse_turns(orders, total)
    kept = []
    for k, pair in enumerate(products(fine, coarse)):
        kept.append([split(table) for table in pair])
        if k % 2 == 0:
            continue
        for c in range(2):
            high, low = [jnp.concatenate([kept[k - 1][c][i], kept[k][c][i]], axis=0) for i in range(2)]
            for i, value in enumerate((high, high, low)):
                at = i * LANES + (k - 1) * ROWS
                right_ref[at : at + 2 * ROWS, c * width : (c + 1) * width] = value
    for k in range(2):
        origin = lon if k == 0 else lon + 1 - 2 * side
        step = iota((blocks, width), 0) + origin * blocks
        for c, table in enumerate(turn((step * LANES * orders) & (total - 1), total)):
            first_ref[c, k * blocks : (k + 1) * blocks] = table


def cycle_tables(owners, cycles, after_ref, cycle_ref, pick_ref, put_ref):
    del after_ref
    northern = owners * cycles
    lane = iota((1, LANES), 1)

    listed = jnp.broadcast_to(cycle_ref[...].astype(jnp.float32), (LANES, northern)).astype(jnp.bfloat16)
    index = iota((LANES, northern), 0)

    def places(repeat):
        place = index // (repeat * cycles) * cycles + index % cycles
        return jnp.where(place == iota((LANES, northern), 1), 1.0, 0.0).astype(jnp.bfloat16)

    arriving = dot_nt(listed[: 2 * ROWS], places(2))[:1].astype(jnp.int32)
    found = (iota((northern, LANES), 0) == arriving) & (lane < 2 * northern)
    for p in range(2):
        one = jnp.where(found & (lane // cycles % 2 == p), 1.0, 0.0)
        copies = jnp.concatenate([one] * (LANES // northern), axis=0)
        pick_ref[p * LANES : (p + 1) * LANES] = copies.astype(jnp.bfloat16)
    leaving = dot_nt(places(4), listed).astype(jnp.int32)
    found = leaving == iota((LANES, LANES), 1) % northern
    part = iota((LANES, LANES), 0) // cycles % 4
    for i in range(4):
        put = jnp.where(found & (part == i), 1.0, 0.0)
        put_ref[i // 2, :, i % 2 * LANES : (i % 2 + 1) * LANES] = put.astype(jnp.bfloat16)


def inverse_tables(total, orders_ref, after_ref, rows_ref, turn_ref, basis_ref):
    del after_ref
    owners, per_owner = orders_ref.shape
    blocks = turn_ref.shape[2]
    quarter = per_owner // 4
    lon = lax.axis_index("lon")
    own = orders_ref[pl.ds(lax.axis_index("band"), 1), :].astype(jnp.float32)
    rows_ref[...] = jnp.transpose(jnp.broadcast_to(own, (LANES, per_owner))).astype(jnp.int32)

    slot = iota((1, LANES), 1) // quarter
    orders = orders_ref[...]
    ahead, behind = pltpu.roll(orders, LANES - quarter, 1), pltpu.roll(orders, quarter, 1)
    arranged = jnp.where(slot == 1, ahead, jnp.where(slot == 2, behind, orders))
    scale = 1.0 / math.sqrt(total)
    for b in range(owners):
        order = arranged[b : b + 1]
        factor = jnp.where(order == 0, scale, 2.0 * scale)
        step = iota((blocks, per_owner), 0) + lon * blocks
        for c, table in enumerate(turn((step * LANES * order) & (total - 1), total)):
            turn_ref[c, b] = table * factor
        fine = turn(iota((ROWS, per_owner), 0) * order, total)
        coarse = coarse_turns(order, total)
        kept = []
        for k, pair in enumerate(products(fine, coarse)):
            kept.append(pair)
            if k % 2 == 1:
                rows = slice((k - 1) * ROWS, (k + 1) * ROWS)
                for c in range(2):
                    at = (b * 2 + c) * per_owner
                    both = jnp.concatenate([kept[k - 1][c], kept[k][c]], axis=0)
                    basis_ref[rows, at : at + per_owner] = both.astype(basis_ref.dtype)


def spectral(
    pick_ref,
    put_ref,
    rows_ref,
    folded_ref,
    own_table_ref,
    other_table_ref,
    own_love_ref,
    other_love_ref,
    out_ref,
    spread_ref,
    kept_ref,
):
    parts, owners, height = folded_ref.shape[:3]
    quarter = rows_ref.shape[0] // (2 * parts)
    degrees = own_table_ref.shape[1]
    northern = owners * height // 2
    group = degrees // northern
    wide = group * northern
    lon = lax.axis_index("lon")
    side = lon % 2

    pad = jnp.zeros((LANES - 2 * northern, LANES), jnp.float32)
    turned = []
    for q in range(parts):
        pieces = [folded_ref[q, b].astype(jnp.float32) for b in range(owners)]
        turned.append(jnp.transpose(jnp.concatenate(pieces + [pad], axis=0)))
    spread_ref[...] = dot_nt(jnp.concatenate(turned, axis=0).astype(jnp.bfloat16), pick_ref[...])

    lane = iota((ROWS, degrees), 1)
    degree = [lon * degrees + lane, (lon + 1 - 2 * side) * degrees + lane]
    tables = [own_table_ref, other_table_ref]
    love = [[[ref[g, f : f + 1, :] for f in range(2)] for g in range(2)] for ref in (own_love_ref, other_love_ref)]
    diagonal = iota((ROWS, wide), 0) == iota((ROWS, wide), 1) // northern
    across = LANES // northern
    upper = iota((ROWS, LANES), 0) < across
    folded_diagonal = iota((ROWS, LANES), 0) % across == iota((ROWS, LANES), 1) // northern
    groups = parts * quarter // group

    def first_order(n):
        q, first = n * group // quarter, n * group % quarter
        return (2 * q + side) * quarter + first

    def table(n, d):
        return tables[d][pl.ds(pl.multiple_of(first_order(n) * northern, wide), wide)]

    def spread(n):
        q, first = n * group // quarter, n * group % quarter
        left = []
        for f in range(2):
            for p in range(2):
                for c in range(2):
                    at = q * LANES + (f * 2 + c) * quarter + first
                    piece = spread_ref[at : at + group, p * LANES : (p + 1) * LANES]
                    left.append(jnp.where(diagonal, jnp.concatenate([piece] * (wide // LANES), axis=1), 0.0))
        return jnp.concatenate(left, axis=0).astype(jnp.bfloat16)

    def respond(n, d, analysed):
        order = rows_ref[pl.ds(pl.multiple_of(first_order(n), group), group)]
        gap = degree[d] - jnp.concatenate([order] * (degrees // LANES), axis=1)
        valid = gap >= 0
        keep = [valid & ((gap & 1) == p) for p in range(2)]
        mixed = []
        for g in range(2):
            for p in range(2):
                for c in range(2):
                    lo = (p * 2 + c) * group
                    hi = ((2 + p) * 2 + c) * group
                    value = love[d][g][0] * analysed[lo : lo + group] + love[d][g][1] * analysed[hi : hi + group]
                    mixed.append(jnp.where(keep[p], value, 0.0))
        return dot_nt(jnp.concatenate(mixed, axis=0).astype(jnp.bfloat16), table(n, d))

    def keep_pair(n, halves):
        for g in range(2):
            for c in range(2):
                lo, hi = (g * 4 + c) * group, (g * 4 + 2 + c) * group
                at = c * parts * quarter + n * group
                rows = []
                for half in halves:
                    even, odd = half[lo : lo + group], half[hi : hi + group]
                    even = jnp.where(upper, even[:, :LANES], even[:, LANES:])
                    odd = jnp.where(upper, odd[:, :LANES], odd[:, LANES:])
                    rows.append([jnp.where(folded_diagonal, x, 0.0) for x in (even + odd, even - odd)])
                for h in range(2):
                    both = jnp.concatenate([row[h] for row in rows], axis=0).astype(jnp.bfloat16)
                    kept_ref[g, at : at + 2 * group, h * LANES : (h + 1) * LANES] = both

    steps = [(n, d) for n in range(groups) for d in range(2)]
    left, analysed, partial = None, {}, {}
    for i in range(len(steps) + 3):
        if i < len(steps):
            n, d = steps[i]
            left = spread(n) if d == 0 else left
            analysed[i] = dot(left, table(n, d))
        if 2 <= i < len(steps) + 2:
            n, d = steps[i - 2]
            value = respond(n, d, analysed.pop(i - 2))
            partial[n] = value if d == 0 else partial[n] + value
        if i >= 6 and i % 4 == 2:
            n = (i - 6) // 2
            keep_pair(n, [partial.pop(n), partial.pop(n + 1)])

    total = dot_nt(put_ref[0], kept_ref[0]) + dot_nt(put_ref[1], kept_ref[1])
    total = total.astype(out_ref.dtype)
    lon_count = out_ref.shape[0] // owners
    rows = out_ref.shape[1]
    for b in range(owners):
        for q in range(lon_count):
            out_ref[b * lon_count + q] = total[b * rows : (b + 1) * rows]


def synthesise_grid(turn_ref, basis_ref, values_ref, out_ref, left_ref):
    owners, blocks, per_owner = turn_ref.shape[1:]
    lon_count = values_ref.shape[0] // owners
    rows = values_ref.shape[1]
    cycles = out_ref.shape[2]
    height = blocks * rows
    first_lanes = iota((1, LANES), 1) < per_owner // 2
    for b in range(owners):
        halves = []
        for c in range(2):
            value = values_ref[b * lon_count + c].astype(jnp.float32)
            for q in range(c + 2, lon_count, 2):
                value = value + values_ref[b * lon_count + q].astype(jnp.float32)
            halves.append(value)
        re = jnp.where(first_lanes, halves[0], pltpu.roll(halves[1], per_owner // 2, 1))
        im = jnp.where(first_lanes, pltpu.roll(halves[0], per_owner // 2, 1), halves[1])
        at = 2 * b * per_owner
        for a in range(blocks):
            ca, sa = turn_ref[0, b, a : a + 1], turn_ref[1, b, a : a + 1]
            for c, term in ((0, ca * re - sa * im), (1, -(sa * re + ca * im))):
                high, low = split(term)
                lanes = slice(at + c * per_owner, at + (c + 1) * per_owner)
                left_ref[a * rows : (a + 1) * rows, lanes] = high
                left_ref[height + a * rows : height + (a + 1) * rows, lanes] = low
    grid = None
    for b in range(owners):
        lanes = slice(2 * b * per_owner, 2 * (b + 1) * per_owner)
        term = dot_nt(left_ref[:, lanes], basis_ref[:, lanes])
        grid = term if grid is None else grid + term
    grid = grid[:height] + grid[height:]
    for a in range(blocks):
        for g in range(2):
            for h in range(2):
                at = a * rows + (g * 2 + h) * cycles
                out_ref[g, h, :, a * LANES : (a + 1) * LANES] = grid[at : at + cycles]


def fits(owners, lon_count, cycles, points, per_owner, degrees):
    northern = owners * cycles
    total = points * lon_count
    return (
        per_owner == LANES
        and 4 * per_owner == lon_count * LANES
        and lon_count % 2 == 0
        and 2 * cycles == ROWS
        and 4 * northern == LANES
        and ROWS * northern == degrees
        and degrees % LANES == 0
        and owners == ROWS
        and points % LANES == 0
        and total & (total - 1) == 0
        and owners * per_owner * LANES < 1 << 24
    )


def per_device_kernels(loads, legendre, love, cycle_weight, order_list, cycle_order):
    owners = lax.axis_size("band")
    lon_count = lax.axis_size("lon")
    cycles, points = loads.shape[2], loads.shape[3]
    per_owner, degrees, northern = legendre.shape
    total = points * lon_count
    devices = owners * lon_count
    blocks = points // LANES
    everyone = ("band", "lon")
    vmem = pl.BlockSpec(memory_space=pltpu.VMEM)
    table = order_list.reshape(owners, per_owner)
    cycle_list = cycle_order.reshape(1, northern)

    def kernel(body, out_shape, in_specs, scratch_shapes, flops):
        return pl.pallas_call(
            body,
            out_shape=out_shape,
            in_specs=in_specs,
            out_specs=jax.tree.map(lambda _: vmem, out_shape),
            scratch_shapes=scratch_shapes,
            compiler_params=pltpu.CompilerParams(vmem_limit_bytes=VMEM_LIMIT),
            cost_estimate=pl.CostEstimate(flops=flops, bytes_accessed=1 << 20, transcendentals=0),
        )

    partner = [(i, i ^ 1) for i in range(lon_count)]
    rows = jnp.transpose(legendre, (0, 2, 1)).reshape(per_owner * northern, degrees)
    parts = [loads, lax.ppermute(loads, "lon", partner)]
    other_rows = lax.ppermute(rows, "lon", partner)
    other_love = lax.ppermute(love, "lon", partner)
    count = 2 * blocks
    width = owners * per_owner // 2
    opened = kernel(opening, jax.ShapeDtypeStruct((ROWS, LANES), jnp.float32), [], [], 1 << 34)()
    right, first = kernel(
        functools.partial(forward_tables, blocks, total),
        (
            jax.ShapeDtypeStruct((3 * LANES, 2 * width), jnp.bfloat16),
            jax.ShapeDtypeStruct((2, count, width), jnp.float32),
        ),
        [vmem, vmem],
        [],
        1 << 34,
    )(table, opened)
    order_rows, turns, basis = kernel(
        functools.partial(inverse_tables, total),
        (
            jax.ShapeDtypeStruct((per_owner, LANES), jnp.int32),
            jax.ShapeDtypeStruct((2, owners, blocks, per_owner), jnp.float32),
            jax.ShapeDtypeStruct((LANES, 2 * owners * per_owner), jnp.bfloat16),
        ),
        [vmem, vmem],
        [],
        1 << 20,
    )(table, first)
    pick, put = kernel(
        functools.partial(cycle_tables, owners, cycles),
        (
            jax.ShapeDtypeStruct((2 * LANES, LANES), jnp.bfloat16),
            jax.ShapeDtypeStruct((2, LANES, 2 * LANES), jnp.bfloat16),
        ),
        [vmem, vmem],
        [],
        1 << 20,
    )(order_rows, cycle_list)
    sums = kernel(
        functools.partial(analyse_grid, total),
        jax.ShapeDtypeStruct((devices, 2 * cycles, LANES), jnp.float32),
        [vmem] * (5 + len(parts)),
        [
            pltpu.VMEM((count * 4 * cycles, LANES), jnp.float32),
            pltpu.VMEM((count * 4 * cycles, 2 * width), jnp.float32),
        ],
        1 << 24,
    )(pick, right, first, cycle_weight.reshape(1, northern), cycle_list, *parts)
    arrived = lax.all_to_all(sums, everyone, split_axis=0, concat_axis=0, tiled=True)
    folded = kernel(
        add_points,
        jax.ShapeDtypeStruct((2, owners, 2 * cycles, LANES), jnp.bfloat16),
        [vmem],
        [],
        1 << 28,
    )(arrived)
    values = kernel(
        spectral,
        jax.ShapeDtypeStruct((devices, 4 * cycles, per_owner), jnp.bfloat16),
        [vmem] * 8,
        [
            pltpu.VMEM((2 * LANES, 2 * LANES), jnp.float32),
            pltpu.VMEM((2, per_owner, 2 * LANES), jnp.bfloat16),
        ],
        1 << 31,
    )(pick, put, order_rows, folded, rows, other_rows, love, other_love)
    returned = lax.all_to_all(values, everyone, split_axis=0, concat_axis=0, tiled=True)

    return kernel(
        synthesise_grid,
        jax.ShapeDtypeStruct(loads.shape, jnp.float32),
        [vmem] * 3,
        [pltpu.VMEM((2 * 4 * cycles * blocks, 2 * owners * per_owner), jnp.bfloat16)],
        1 << 31,
    )(turns, basis, returned)


def per_device(loads, legendre, love, cycle_weight, order_list, cycle_order):
    sizes = (lax.axis_size("band"), lax.axis_size("lon"), loads.shape[2], loads.shape[3], legendre.shape[0], legendre.shape[1])
    form = per_device_kernels if fits(*sizes) else per_device_plain
    return form(loads, legendre, love, cycle_weight, order_list, cycle_order)


def cycle_basis(order_ids, positions, total):
    phase = positions[:, None] * order_ids[None, :] % total
    angle = phase.astype(jnp.float32) * (2.0 * math.pi / total)
    scale = 1.0 / math.sqrt(total)
    return (jnp.cos(angle) * scale, jnp.sin(angle) * scale)


def per_device_plain(loads, legendre, love, cycle_weight, order_list, cycle_order):
    highest = lax.Precision.HIGHEST
    owners = lax.axis_size("band")
    lon_count = lax.axis_size("lon")
    band_index = lax.axis_index("band")
    lon_index = lax.axis_index("lon")
    cycle_pairs = loads.shape[2]
    points = loads.shape[3]
    total = points * lon_count
    orders = order_list.shape[0]
    per_owner = legendre.shape[0]
    degree_count = legendre.shape[1]
    northern = legendre.shape[2]
    quarter = per_owner // lon_count
    positions = lon_index * points + jnp.arange(points, dtype=jnp.int32)
    cosine, sine = cycle_basis(order_list, positions, total)
    my_cycles = lax.dynamic_slice_in_dim(cycle_order, band_index * cycle_pairs, cycle_pairs)
    picker = my_cycles[:, None] == jnp.arange(northern, dtype=jnp.int32)[None, :]
    weights = jnp.sum(jnp.where(picker, cycle_weight[None, :], 0.0), axis=1)
    forward = jnp.stack([cosine, -sine], axis=1)
    spectrum = jnp.einsum("fhjx,xrm->fhjrm", loads, forward, precision=highest)
    spectrum = spectrum.reshape(2, 2, cycle_pairs, 2, owners, per_owner)
    summed = lax.psum_scatter(spectrum, "lon", scatter_dimension=5, tiled=True)
    cycle_scale = weights[None, :, None, None, None]
    symmetric = ((summed[:, 0] + summed[:, 1]) * cycle_scale).astype(jnp.bfloat16)
    antisym = ((summed[:, 0] - summed[:, 1]) * cycle_scale).astype(jnp.bfloat16)
    folded = jnp.stack([symmetric, antisym], axis=1)
    slot_width = folded.shape[5]
    outgoing = jnp.transpose(folded, (4, 5, 0, 1, 3, 2)).reshape(owners, slot_width, 8, cycle_pairs)
    arrived = lax.all_to_all(outgoing, "band", split_axis=0, concat_axis=3, tiled=True).reshape(
        slot_width, 8, northern
    )
    columns = lax.all_gather(arrived, "lon", axis=0, tiled=True)
    inverse_rows = jnp.argsort(cycle_order)
    columns_sorted = jnp.take(columns, inverse_rows, axis=2)
    my_orders = lax.dynamic_slice_in_dim(order_list, band_index * per_owner, per_owner)
    degrees = lon_index * degree_count + jnp.arange(degree_count, dtype=jnp.int32)
    analysed = jnp.einsum(
        "olk,ock->ocl", legendre, columns_sorted, preferred_element_type=jnp.float32
    )
    analysed = analysed.reshape(per_owner, 2, 2, 2, degree_count)
    even = (degrees[None, :] - my_orders[:, None]) % 2 == 0
    valid = degrees[None, :] >= my_orders[:, None]
    selected = jnp.where(even[:, None, None, :], analysed[:, :, 0], analysed[:, :, 1])
    selected = selected * valid[:, None, None, :].astype(jnp.float32)
    response = jnp.einsum("gfl,ofrl->ogrl", love, selected, precision=highest).astype(jnp.bfloat16)
    even_part = jnp.where((even & valid)[:, None, None, :], response, jnp.zeros_like(response))
    odd_part = jnp.where((~even & valid)[:, None, None, :], response, jnp.zeros_like(response))
    stacked = jnp.stack([even_part, odd_part], axis=2).reshape(per_owner, 8, degree_count)
    partial_sorted = jnp.einsum(
        "olk,ocl->ock", legendre, stacked, preferred_element_type=jnp.float32
    )
    partial_value = jnp.take(partial_sorted, cycle_order, axis=2)
    reduced = lax.psum_scatter(partial_value, "lon", scatter_dimension=0, tiled=True)
    returned = lax.all_to_all(reduced, "band", split_axis=2, concat_axis=0, tiled=True)
    gathered = lax.all_gather(returned[None], "lon", axis=0, tiled=True).reshape(
        orders, 8, cycle_pairs
    )
    slot_ids = jnp.transpose(order_list.reshape(owners, lon_count, quarter), (1, 0, 2)).reshape(
        orders
    )
    cosine_back, sine_back = cycle_basis(slot_ids, positions, total)
    pieces = gathered.reshape(orders, 2, 2, 2, cycle_pairs)
    cycle_values = jnp.stack(
        [pieces[:, :, 0] + pieces[:, :, 1], pieces[:, :, 0] - pieces[:, :, 1]], axis=2
    )
    factor = jnp.where(slot_ids == 0, 1.0, 2.0).astype(jnp.float32)
    inverse = jnp.stack([cosine_back.T, -sine_back.T], axis=0)
    scaled = cycle_values * factor[:, None, None, None, None]
    return jnp.einsum("sghrp,rsx->ghpx", scaled, inverse, precision=highest)


def solution(mesh):
    return jax.shard_map(
        per_device,
        mesh=mesh,
        in_specs=(
            P(None, None, "band", "lon"),
            P("band", "lon", None),
            P(None, None, "lon"),
            P(),
            P(),
            P(),
        ),
        out_specs=P(None, None, "band", "lon"),
        check_vma=False,
    )
```
